32 devices in a mesh: tile: 4 (over z), sub: 8 (over y, x, core).
Axes of the slice: x: 2, y: 2, z: 4, core: 2. Of those that a mesh axis runs over, the one named last changes fastest.
Arguments:
- initial: float32 [64, 64, 2048], P(None, 'tile', 'sub'), may hold values from -6 to 6
- targets: float32 [64, 64, 2048], P(None, 'tile', 'sub'), may hold values from -6 to 6
- diffusivity: float32 [64, 2048], P('tile', 'sub'), may hold values from 0.02 to 0.24
- column_order: int32 [32, 4096], P(('tile', 'sub')), may hold values from 0 to 4095, each once within a row
- send_counts: int32 [32, 32], P(('tile', 'sub')), may hold values from 0 to 256, as said below
- w_first: bfloat16 [8, 64, 192], P('sub'), may hold values from -0.75 to 0.75
- w_inner: bfloat16 [8, 3, 192, 192], P('sub'), may hold values from -0.4375 to 0.4375
- w_last: bfloat16 [8, 192, 64], P('sub'), may hold values from -0.4375 to 0.4375
- b_inner: float32 [8, 4, 192], P('sub'), may hold values from -2 to 2
- b_last: float32 [8, 64], P('sub'), may hold values from -2 to 2
Outputs:
- grad_initial: float32 [64, 64, 2048], P(None, 'tile', 'sub')
- step_first: float32 [8, 64, 192], P('sub')
- step_inner: float32 [8, 3, 192, 192], P('sub')
- step_last: float32 [8, 192, 64], P('sub')
- step_bias_inner: float32 [8, 4, 192], P('sub')
- step_bias_last: float32 [8, 64], P('sub')
The draws below stay inside these ranges and needn't reach their ends.
Inputs may be any that keep to these rules, and one draw needn't show every extreme that they name: `send_counts`: each row sums to 4096. For every pair of destinations d and d plus half of 32 (same sub index, tile indices half the tile axis apart) the two entries of a row sum to 256; some destination receives 256 from every device.
All inputs are finite; a program needn't handle non-finite values.
Results may differ from the reference program's by a relative error of at most 0.0095.
Values may be sent and summed in bfloat16 or wider, within the bound.
No kernel may reach another device: no remote copies, remote signals or barrier semaphores. Data moves between devices by JAX's collectives and lax.ppermute only.
A program may use at most 64 MiB of HBM per device.

```python
import math
import jax
import jax.numpy as jnp
from jax import lax

LEV = 64
WIDTH = 192
CX = 16
CY = 256
STEPS = 2
NCOL = 4096
NX = 64
NY = 2048
CAP = 256
EXPERTS = 8
N_TILE = 4
N_SUB = 8
DEVICES = 32


def draw_send_counts(key, part):
    half_count = DEVICES // 2
    first_key, second_key = jax.random.split(jax.random.fold_in(key, 11))
    first_share = jax.random.randint(first_key, (DEVICES, half_count), 0, CAP + 1)
    pair_order = jax.random.permutation(second_key, half_count)
    hot_pairs = pair_order < max(1, DEVICES // 16)
    first_share = jnp.where(hot_pairs[None, :], CAP, first_share)
    return jnp.concatenate([first_share, CAP - first_share], axis=1).astype(jnp.int32)


def steps_of(key, dims, cuts, smallest, high):
    factor_of, own = 1.0, jax.random.fold_in(key, 6)
    for dim, shards_of in cuts:
        draws = jnp.exp(jax.random.uniform(jax.random.fold_in(own, dim), (shards_of,), jnp.float32, smallest / len(cuts), high / len(cuts)))
        factor_of = factor_of * jnp.repeat(draws, dims[dim] // shards_of).reshape([-1 if axis == dim else 1 for axis in range(len(dims))])
    return factor_of


def scatter_about(rng, extent, deviation, reach, cuts=(), kind=jnp.bfloat16):
    array = deviation * jax.random.normal(rng, extent, jnp.float32)
    if cuts:
        array = array * steps_of(rng, extent, cuts, -0.22, 0.18)
    return jnp.clip(array, -reach, reach).astype(kind)


def setup_inputs(seed: int = 0) -> dict:
    key_of = jax.random.split(jax.random.key(seed), 11)
    initial = scatter_about(key_of[0], (LEV, NX, NY), 1.0, 6.0, ((1, 4), (2, 8)), jnp.float32)
    targets = scatter_about(key_of[1], (LEV, NX, NY), 1.0, 6.0, ((1, 4), (2, 8)), jnp.float32)
    diffusivity = jnp.clip(jnp.exp(math.log(0.24) - 2.4849066 * jax.random.uniform(key_of[2], (NX, NY), jnp.float32) ** steps_of(key_of[2], (NX, NY), ((0, 4), (1, 8)), -0.2, 0.2)), 0.02, 0.24)
    column_order = jax.vmap(lambda own: jax.random.permutation(own, NCOL))(jax.random.split(key_of[3], DEVICES)).reshape((DEVICES, NCOL)).astype(jnp.int32)
    send_counts = draw_send_counts(jax.random.fold_in(key_of[10], 71), 0)
    w_first = scatter_about(key_of[5], (EXPERTS, LEV, WIDTH), LEV ** -0.5, 0.75, ((0, 8),))
    w_inner = scatter_about(key_of[6], (EXPERTS, 3, WIDTH, WIDTH), WIDTH ** -0.5, 0.4375, ((0, 8),))
    w_last = scatter_about(key_of[7], (EXPERTS, WIDTH, LEV), WIDTH ** -0.5, 0.4375, ((0, 8),))
    b_inner = scatter_about(key_of[8], (EXPERTS, 4, WIDTH), 0.3, 2.0, ((0, 8),), jnp.float32)
    b_last = scatter_about(key_of[9], (EXPERTS, LEV), 0.3, 2.0, ((0, 8),), jnp.float32)
    return {"initial": initial, "targets": targets, "diffusivity": diffusivity, "column_order": column_order, "send_counts": send_counts, "w_first": w_first, "w_inner": w_inner, "w_last": w_last, "b_inner": b_inner, "b_last": b_last}


def laplace(quantity):
    near = jnp.roll(quantity, 1, 1) + jnp.roll(quantity, -1, 1)
    near = near + jnp.roll(quantity, 1, 2) + jnp.roll(quantity, -1, 2)
    return near - 4.0 * quantity

def silu_slope(preact):
    sigmoid_value = jax.nn.sigmoid(preact)
    return sigmoid_value * (1.0 + preact * (1.0 - sigmoid_value))

def run_network(inputs, misfit, usable, w_first, w_inner, w_last, b_inner, b_last):
    layers = [w_first, w_inner[0], w_inner[1], w_inner[2]]
    feeds = [inputs]
    preacts = []
    current = inputs
    for layer_index in range(4):
        preact = jnp.dot(current, layers[layer_index], preferred_element_type=jnp.float32) + b_inner[layer_index]
        preacts.append(preact)
        current = jax.nn.silu(preact).astype(jnp.bfloat16)
        feeds.append(current)
    output = jnp.dot(current, w_last, preferred_element_type=jnp.float32) + b_last
    residue = (misfit.astype(jnp.float32) + output) * usable[:, None]
    error_bf = residue.astype(jnp.bfloat16)
    grad_last = jnp.dot(current.T, error_bf, preferred_element_type=jnp.float32)
    bias_last = lax.optimization_barrier(jnp.sum(error_bf.astype(jnp.float32), axis=0))
    carried = jnp.dot(error_bf, w_last.T, preferred_element_type=jnp.float32)
    weight_grads = [None, None, None, None]
    bias_grads = [None, None, None, None]
    for layer_index in (3, 2, 1, 0):
        error_bf = (carried * silu_slope(preacts[layer_index])).astype(jnp.bfloat16)
        weight_grads[layer_index] = jnp.dot(feeds[layer_index].T, error_bf, preferred_element_type=jnp.float32)
        bias_grads[layer_index] = lax.optimization_barrier(jnp.sum(error_bf.astype(jnp.float32), axis=0))
        carried = jnp.dot(error_bf, layers[layer_index].T, preferred_element_type=jnp.float32)
    returned_grad = (residue + carried).astype(jnp.bfloat16)
    gradients = (weight_grads[0], jnp.stack(weight_grads[1:]), grad_last, jnp.stack(bias_grads), bias_last)
    return (returned_grad, gradients)

def normalize(gradients):
    total = 0.0
    count = 0
    for member in gradients:
        total = total + lax.optimization_barrier(jnp.sum(member * member, axis=tuple(range(1, member.ndim))))
        count = count + member[0].size
    factor = 1.0 / jnp.sqrt(total / count + 1e-06)
    return tuple((member * factor.reshape((-1,) + (1,) * (member.ndim - 1)) for member in gradients))

def to_columns(grid_field):
    shaped = grid_field.reshape(LEV, N_TILE, CX, N_SUB, CY).transpose(1, 3, 2, 4, 0)
    return shaped.reshape(DEVICES, NCOL, LEV)

def from_columns(column_data):
    shaped = column_data.reshape(N_TILE, N_SUB, CX, CY, LEV).transpose(4, 0, 2, 1, 3)
    return shaped.reshape(LEV, NX, NY)

def reference(initial, targets, diffusivity, column_order, send_counts, w_first, w_inner, w_last, b_inner, b_last):
    grid_field = initial
    for iteration in range(STEPS):
        grid_field = grid_field + diffusivity[None] * laplace(grid_field)
    inputs = to_columns(grid_field).astype(jnp.bfloat16)
    misfit = to_columns(grid_field - targets).astype(jnp.bfloat16)
    packed = jnp.concatenate([inputs, misfit], axis=2)
    ordered = jnp.take_along_axis(packed, column_order.astype(jnp.int32)[:, :, None], axis=1)
    counts = send_counts.astype(jnp.int32)
    starts = (jnp.cumsum(counts, axis=1) - counts).astype(jnp.int32)
    slot_ids = jnp.arange(CAP, dtype=jnp.int32)

    def per_target(target_dev):
        position = starts[:, target_dev][:, None] + slot_ids[None, :]
        usable = slot_ids[None, :] < counts[:, target_dev][:, None]
        clipped = jnp.minimum(position, NCOL - 1).astype(jnp.int32)
        row_data = jnp.take_along_axis(ordered, clipped[:, :, None], axis=1)
        row_data = jnp.where(usable[:, :, None], row_data, jnp.zeros_like(row_data))
        network_id = target_dev % N_SUB
        flat = row_data.reshape(DEVICES * CAP, 2 * LEV)
        returned_grad, gradients = run_network(flat[:, :LEV], flat[:, LEV:], usable.reshape(-1).astype(jnp.float32), w_first[network_id], w_inner[network_id], w_last[network_id], b_inner[network_id], b_last[network_id])
        return (returned_grad.reshape(DEVICES, CAP, LEV), gradients)
    answers, gradients = lax.map(per_target, jnp.arange(DEVICES, dtype=jnp.int32))
    gradients = tuple((member.reshape((N_TILE, N_SUB) + member.shape[1:]).sum(axis=0) for member in gradients))
    steps_out = normalize(gradients)
    position = starts[:, :, None] + slot_ids[None, None, :]
    usable = slot_ids[None, None, :] < counts[:, :, None]
    slot_index = jnp.where(usable, position, NCOL).astype(jnp.int32)
    source_ids = jnp.arange(DEVICES, dtype=jnp.int32)[:, None, None]
    values = answers.transpose(1, 0, 2, 3).astype(jnp.float32)
    ordered_back = jnp.zeros((DEVICES, NCOL + 1, LEV), jnp.float32).at[source_ids, slot_index].set(values)[:, :NCOL]
    column_back = jnp.zeros((DEVICES, NCOL, LEV), jnp.float32).at[jnp.arange(DEVICES, dtype=jnp.int32)[:, None], column_order.astype(jnp.int32)].set(ordered_back)
    cotangent = from_columns(column_back)
    for iteration in range(STEPS):
        cotangent = cotangent + laplace(diffusivity[None] * cotangent)
    return (cotangent, steps_out[0], steps_out[1], steps_out[2], steps_out[3], steps_out[4])
```

```python
import jax
import jax.numpy as jnp
from jax import lax
from jax.sharding import PartitionSpec as P

STEPS = 2


def extended(cells, sides, width):
    for axis, dim in sides:
        count = lax.axis_size(axis)
        head = lax.slice_in_dim(cells, 0, width, axis=dim)
        tail = lax.slice_in_dim(cells, cells.shape[dim] - width, cells.shape[dim], axis=dim)
        cells = jnp.concatenate(
            [
                lax.ppermute(tail, axis, [(i, (i + 1) % count) for i in range(count)]),
                cells,
                lax.ppermute(head, axis, [((i + 1) % count, i) for i in range(count)]),
            ],
            axis=dim,
        )
    return cells


def laplace(quantity):
    padded = extended(quantity, (("tile", 1), ("sub", 2)), 1)
    center = padded[:, 1:-1, 1:-1]
    near = padded[:, 2:, 1:-1] + padded[:, :-2, 1:-1] + padded[:, 1:-1, 2:] + padded[:, 1:-1, :-2]
    return near - 4.0 * center


def silu_slope(preact):
    sigmoid_value = jax.nn.sigmoid(preact)
    return sigmoid_value * (1.0 + preact * (1.0 - sigmoid_value))


def run_network(inputs, misfit, usable, w_first, w_inner, w_last, b_inner, b_last):
    layers = [w_first, w_inner[0], w_inner[1], w_inner[2]]
    feeds = [inputs]
    preacts = []
    current = inputs
    for layer_index in range(4):
        preact = (
            jnp.dot(current, layers[layer_index], preferred_element_type=jnp.float32)
            + b_inner[layer_index]
        )
        preacts.append(preact)
        current = jax.nn.silu(preact).astype(jnp.bfloat16)
        feeds.append(current)
    output = jnp.dot(current, w_last, preferred_element_type=jnp.float32) + b_last
    residue = (misfit.astype(jnp.float32) + output) * usable[:, None]
    error_bf = residue.astype(jnp.bfloat16)
    grad_last = jnp.dot(current.T, error_bf, preferred_element_type=jnp.float32)
    bias_last = jnp.sum(error_bf.astype(jnp.float32), axis=0)
    carried = jnp.dot(error_bf, w_last.T, preferred_element_type=jnp.float32)
    weight_grads = [None, None, None, None]
    bias_grads = [None, None, None, None]
    for layer_index in (3, 2, 1, 0):
        error_bf = (carried * silu_slope(preacts[layer_index])).astype(jnp.bfloat16)
        weight_grads[layer_index] = jnp.dot(
            feeds[layer_index].T, error_bf, preferred_element_type=jnp.float32
        )
        bias_grads[layer_index] = jnp.sum(error_bf.astype(jnp.float32), axis=0)
        carried = jnp.dot(error_bf, layers[layer_index].T, preferred_element_type=jnp.float32)
    returned_grad = (residue + carried).astype(jnp.bfloat16)
    gradients = (
        weight_grads[0],
        jnp.stack(weight_grads[1:]),
        grad_last,
        jnp.stack(bias_grads),
        bias_last,
    )
    return (returned_grad, gradients)


def normalize(gradients):
    total = 0.0
    count = 0
    for member in gradients:
        total = total + jnp.sum(member * member, axis=tuple(range(1, member.ndim)))
        count = count + member[0].size
    factor = 1.0 / jnp.sqrt(total / count + 1e-06)
    return tuple(
        (member * factor.reshape((-1,) + (1,) * (member.ndim - 1)) for member in gradients)
    )


def per_device(
    initial,
    targets,
    diffusivity,
    column_order,
    send_counts,
    w_first,
    w_inner,
    w_last,
    b_inner,
    b_last,
):
    levels, width_x, width_y = initial.shape
    column_count = width_x * width_y
    devices = send_counts.shape[1]
    capacity = 2 * column_count // devices
    tile_count = lax.axis_size("tile")
    sub_count = lax.axis_size("sub")
    grid_field = initial
    for iteration in range(STEPS):
        grid_field = grid_field + diffusivity[None] * laplace(grid_field)
    inputs = grid_field.reshape(levels, column_count).T.astype(jnp.bfloat16)
    misfit = (grid_field - targets).reshape(levels, column_count).T.astype(jnp.bfloat16)
    packed = jnp.concatenate([inputs, misfit], axis=1)
    counts_row = send_counts[0]
    starts = jnp.cumsum(counts_row) - counts_row
    slot_ids = jnp.arange(capacity, dtype=jnp.int32)
    half_dev = devices // 2
    low_counts = counts_row[:half_dev]
    pair_pos = jnp.where(
        slot_ids[None, :] < low_counts[:, None],
        starts[:half_dev][:, None] + slot_ids[None, :],
        starts[half_dev:][:, None] + slot_ids[None, :] - low_counts[:, None],
    )
    pairs = tile_count // 2
    flat_cells = column_order[0][pair_pos.reshape(pairs, sub_count, capacity).transpose(1, 0, 2).reshape(-1)]
    blocks = packed[flat_cells].reshape(sub_count, pairs * capacity, 2 * levels)
    incoming = lax.all_to_all(blocks, "sub", split_axis=0, concat_axis=0, tiled=True)
    received = incoming.reshape(-1, 2 * levels)
    arrived = jnp.ones((received.shape[0],), jnp.float32)
    returned_grad, gradients = run_network(
        received[:, :levels],
        received[:, levels:],
        arrived,
        w_first[0],
        w_inner[0],
        w_last[0],
        b_inner[0],
        b_last[0],
    )
    returning = returned_grad.reshape(sub_count, pairs * capacity // 2, 2 * levels)
    answers = lax.all_to_all(returning, "sub", split_axis=0, concat_axis=0, tiled=True)
    answer_rows = answers.reshape(column_count, levels).astype(jnp.float32)
    flat = jnp.concatenate([member.astype(jnp.bfloat16).reshape(-1) for member in gradients])
    size = flat.shape[0]
    unit = tile_count * 2048
    share = (size + unit - 1) // unit * 2048
    flat = jnp.pad(flat, (0, share * tile_count - size)).reshape(tile_count, share // 128, 128)
    parts = lax.all_to_all(flat, "tile", split_axis=0, concat_axis=0, tiled=True)
    part = jnp.sum(parts.astype(jnp.float32), axis=0).astype(jnp.bfloat16)
    whole = lax.all_to_all(
        jnp.broadcast_to(part[None], parts.shape), "tile", split_axis=0, concat_axis=0, tiled=True
    ).reshape(-1)
    summed = []
    offset = 0
    for member in gradients:
        summed.append(whole[offset : offset + member.size].reshape(member.shape).astype(jnp.float32))
        offset += member.size
    steps_out = normalize(tuple((member[None] for member in summed)))
    column_back = (
        jnp.zeros((column_count, levels), jnp.float32).at[flat_cells].set(answer_rows, unique_indices=True)
    )
    cotangent = column_back.T.reshape(levels, width_x, width_y)
    for iteration in range(STEPS):
        cotangent = cotangent + laplace(diffusivity[None] * cotangent)
    return (cotangent, steps_out[0], steps_out[1], steps_out[2], steps_out[3], steps_out[4])


def solution(mesh):
    placed = (
        P(None, "tile", "sub"),
        P(None, "tile", "sub"),
        P("tile", "sub"),
        P(("tile", "sub"), None),
        P(("tile", "sub"), None),
        P("sub", None, None),
        P("sub", None, None, None),
        P("sub", None, None),
        P("sub", None, None),
        P("sub", None),
    )
    return jax.shard_map(
        per_device,
        mesh=mesh,
        in_specs=placed,
        out_specs=(
            P(None, "tile", "sub"),
            P("sub", None, None),
            P("sub", None, None, None),
            P("sub", None, None),
            P("sub", None, None),
            P("sub", None),
        ),
        check_vma=False,
    )
```

```python
import functools
import jax
import jax.numpy as jnp
from jax import lax
from jax.experimental import pallas as pl
from jax.experimental.pallas import tpu as pltpu
from jax.sharding import PartitionSpec as P

LANES = 128
SUBLANES = 8
SECOND = 32
UNROLL = 16
VMEM = pl.BlockSpec(memory_space=pltpu.VMEM)
SMEM = pl.BlockSpec(memory_space=pltpu.SMEM)
PARAMS = pltpu.CompilerParams(vmem_limit_bytes=50 * 1024 * 1024)
F32 = jnp.float32
BF16 = jnp.bfloat16


def tile_rows(cells):
    levels, width_x, width_y = cells.shape
    split = cells.reshape(levels, width_x // SUBLANES, SUBLANES, width_y // LANES, LANES)
    return split.transpose(0, 1, 3, 2, 4).reshape(-1, LANES)


def untile_rows(rows, levels, width_x, width_y):
    split = rows.reshape(levels, width_x // SUBLANES, width_y // LANES, SUBLANES, LANES)
    return split.transpose(0, 1, 3, 2, 4).reshape(levels, width_x, width_y)


def row_offset(x, y_tile, y_tiles):
    return (x // SUBLANES * y_tiles + y_tile) * SUBLANES + x % SUBLANES


def load_row(ref, group, x, width_x, width_y):
    y_tiles = width_y // LANES
    stride = width_x * y_tiles
    base = group * (SUBLANES * stride)
    return jnp.concatenate(
        [
            ref[pl.ds(base + row_offset(x, y_tile, y_tiles), SUBLANES, stride=stride), :]
            for y_tile in range(y_tiles)
        ],
        axis=1,
    )


def load_wide(ref, x, width_y):
    y_tiles = width_y // LANES
    return jnp.concatenate(
        [
            jnp.broadcast_to(ref[pl.ds(row_offset(x, y_tile, y_tiles), 1), :], (SUBLANES, LANES))
            for y_tile in range(y_tiles)
        ],
        axis=1,
    )


def lane_ids(width):
    return lax.broadcasted_iota(jnp.int32, (SUBLANES, width), 1)


def compact_edges(row_of, width_x, width_y):
    lane = lane_ids(LANES)
    low = jnp.zeros((SUBLANES, LANES), F32)
    high = jnp.zeros((SUBLANES, LANES), F32)
    for x in range(width_x):
        row = row_of(x)
        low = jnp.where(lane == 1 + x, row[:, 0:1], low)
        low = jnp.where(lane == SECOND + 1 + x, row[:, 1:2], low)
        high = jnp.where(lane == 1 + x, row[:, width_y - 1 : width_y], high)
        high = jnp.where(lane == SECOND + 1 + x, row[:, width_y - 2 : width_y - 1], high)
    return low, high


def groups_at(group):
    return pl.ds(pl.multiple_of(group * SUBLANES, SUBLANES), SUBLANES)


def pack_body(levels, width_x, width_y, field, diff, top, bottom, low, high):
    def emit(where, row_of):
        for k in range(2):
            top[where, k * width_y : (k + 1) * width_y] = row_of(k)
            bottom[where, k * width_y : (k + 1) * width_y] = row_of(width_x - 2 + k)
        low_value, high_value = compact_edges(row_of, width_x, width_y)
        low[where, :] = low_value
        high[where, :] = high_value

    def step(group, carry):
        emit(groups_at(group), lambda x: load_row(field, group, x, width_x, width_y))
        return carry

    lax.fori_loop(0, levels // SUBLANES, step, 0)
    emit(pl.ds(levels, SUBLANES), lambda x: load_wide(diff, x, width_y))


def pack_edges(field_rows, diff_rows, levels, width_x, width_y):
    tall = levels + SUBLANES
    return pl.pallas_call(
        functools.partial(pack_body, levels, width_x, width_y),
        out_shape=[
            jax.ShapeDtypeStruct((tall, 2 * width_y), F32),
            jax.ShapeDtypeStruct((tall, 2 * width_y), F32),
            jax.ShapeDtypeStruct((tall, LANES), F32),
            jax.ShapeDtypeStruct((tall, LANES), F32),
        ],
        in_specs=[VMEM] * 2,
        out_specs=[VMEM] * 4,
        compiler_params=PARAMS,
        name="pack_edges",
    )(field_rows, diff_rows)


def shifted(array, shift_tile, shift_sub):
    tiles, subs = lax.axis_size("tile"), lax.axis_size("sub")
    if shift_tile == 0:
        return lax.ppermute(array, "sub", [(i, (i + shift_sub) % subs) for i in range(subs)])
    if shift_sub == 0:
        return lax.ppermute(array, "tile", [(i, (i + shift_tile) % tiles) for i in range(tiles)])
    pairs = []
    for t in range(tiles):
        for s in range(subs):
            target = (t + shift_tile) % tiles * subs + (s + shift_sub) % subs
            pairs.append((t * subs + s, target))
    return lax.ppermute(array, ("tile", "sub"), pairs)


def exchange(top, bottom, low, high):
    return (
        shifted(bottom, 1, 0),
        shifted(top, -1, 0),
        shifted(high, 0, 1),
        shifted(low, 0, -1),
        shifted(high, 1, 1),
        shifted(low, 1, -1),
        shifted(high, -1, 1),
        shifted(low, -1, -1),
    )


def with_corners(side, before, after, width_x):
    lane = lane_ids(LANES)
    value = jnp.where(lane == 0, pltpu.roll(before, LANES - width_x, 1), side)
    return jnp.where(lane == width_x + 1, pltpu.roll(after, width_x, 1), value)


def around(side):
    return pltpu.roll(side, 1, 1) + pltpu.roll(side, LANES - 1, 1)


def second(side):
    return pltpu.roll(side, LANES - SECOND, 1)


def beside(row, left, right, x):
    width = row.shape[1]
    lane = lane_ids(width)
    return jnp.where(lane == 0, left[:, x + 1 : x + 2], pltpu.roll(row, 1, 1)) + jnp.where(
        lane == width - 1, right[:, x + 1 : x + 2], pltpu.roll(row, width - 1, 1)
    )


def fill_starts(counts, starts, devices):
    def step(index, total):
        starts[index] = total
        return total + counts[index]

    lax.fori_loop(0, devices, step, jnp.int32(0))


def forward_body(
    levels, width_x, width_y, tiles, subs,
    counts, order, field, target, diff, own_low, own_high, up, down, left, right,
    up_left, up_right, down_left, down_right, out, e0, e1, wide, both, rows, picked, starts,
):
    cells = width_x * width_y
    devices = tiles * subs

    def at(x):
        return slice((x + 2) * width_y, (x + 3) * width_y)

    def sides(where):
        return (
            with_corners(left[where, :], up_left[where, :], down_left[where, :], width_x),
            with_corners(right[where, :], up_right[where, :], down_right[where, :], width_x),
        )

    last = pl.ds(levels, SUBLANES)
    for x in range(width_x):
        wide[:, at(x)] = load_wide(diff, x, width_y)
    wide[:, at(-1)] = up[last, width_y:]
    wide[:, at(width_x)] = down[last, :width_y]
    diff_left, diff_right = sides(last)

    def step(group, carry):
        where = groups_at(group)
        for x in range(width_x):
            e0[:, at(x)] = load_row(field, group, x, width_x, width_y)
        for k in range(2):
            e0[:, at(k - 2)] = up[where, k * width_y : (k + 1) * width_y]
            e0[:, at(width_x + k)] = down[where, k * width_y : (k + 1) * width_y]
        side_left, side_right = sides(where)

        def next_side(side, outer, own, coefficient):
            return side + coefficient * (around(side) + second(outer) + own - 4.0 * side)

        next_left = next_side(side_left, left[where, :], own_low[where, :], diff_left)
        next_right = next_side(side_right, right[where, :], own_high[where, :], diff_right)
        for x in range(-1, width_x + 1):
            row = e0[:, at(x)]
            near = e0[:, at(x - 1)] + e0[:, at(x + 1)] + beside(row, side_left, side_right, x)
            e1[:, at(x)] = row + wide[:, at(x)] * (near - 4.0 * row)
        for x in range(width_x):
            row = e1[:, at(x)]
            near = e1[:, at(x - 1)] + e1[:, at(x + 1)] + beside(row, next_left, next_right, x)
            value = row + wide[:, at(x)] * (near - 4.0 * row)
            both[where, x * width_y : (x + 1) * width_y] = value
            both[
                pl.ds(pl.multiple_of(levels + group * SUBLANES, SUBLANES), SUBLANES),
                x * width_y : (x + 1) * width_y,
            ] = value - load_row(target, group, x, width_x, width_y)
        return carry

    lax.fori_loop(0, levels // SUBLANES, step, 0)
    fill_starts(counts, starts, devices)

    def turn(tile, carry):
        span = pl.ds(pl.multiple_of(tile * LANES, LANES), LANES)
        rows[span, :] = both[:, span].T
        return carry

    lax.fori_loop(0, cells // LANES, turn, 0, unroll=2)

    def run(index, base):
        device = index % tiles * subs + index // tiles
        count = counts[device]
        start = starts[device]

        def copy(chunk, carry):
            offset = chunk * UNROLL
            taken = [rows[pl.ds(order[start + offset + u], 1), :] for u in range(UNROLL)]
            for u in range(UNROLL):
                picked[pl.ds(base + offset + u, 1), :] = taken[u]
            return carry

        lax.fori_loop(0, (count + UNROLL - 1) // UNROLL, copy, 0)
        return base + count

    lax.fori_loop(0, devices, run, jnp.int32(0))
    out[...] = picked[:cells, :].astype(BF16)


def forward(counts, order, field_rows, target_rows, diff_rows, own_low, own_high, halos, sizes):
    levels, width_x, width_y, tiles, subs = sizes
    cells = width_x * width_y
    return pl.pallas_call(
        functools.partial(forward_body, levels, width_x, width_y, tiles, subs),
        out_shape=jax.ShapeDtypeStruct((cells, 2 * levels), BF16),
        in_specs=[SMEM] * 2 + [VMEM] * 13,
        out_specs=VMEM,
        scratch_shapes=[
            pltpu.VMEM((SUBLANES, (width_x + 4) * width_y), F32),
            pltpu.VMEM((SUBLANES, (width_x + 4) * width_y), F32),
            pltpu.VMEM((SUBLANES, (width_x + 4) * width_y), F32),
            pltpu.VMEM((2 * levels, cells), F32),
            pltpu.VMEM((cells + SUBLANES, 2 * levels), F32),
            pltpu.VMEM((cells + UNROLL, 2 * levels), F32),
            pltpu.SMEM((tiles * subs,), jnp.int32),
        ],
        compiler_params=PARAMS,
        name="forward",
    )(counts, order, field_rows, target_rows, diff_rows, own_low, own_high, *halos)


def squeeze_lanes(wide_part, half):
    count = wide_part.shape[0] // 2
    lane = lax.broadcasted_iota(jnp.int32, (count, LANES), 1)
    low = wide_part[:count]
    high = wide_part[count:]
    if half == 0:
        high = pltpu.roll(high, LANES // 2, 1)
    else:
        low = pltpu.roll(low, LANES // 2, 1)
    return jnp.where(lane < LANES // 2, low, high)


def network_body(
    levels, width, packet, inputs, first_in, first_out, inner, last, bias, bias_last,
    out, grads, acc_first, acc_inner, acc_last, acc_bias, acc_bias_last,
):
    block = pl.program_id(0)
    cells = inputs.shape[0]
    lane = lax.broadcasted_iota(jnp.int32, (cells, LANES), 1)

    @pl.when(block == 0)
    def _():
        for ref in (acc_first, acc_inner, acc_last, acc_bias, acc_bias_last):
            ref[...] = jnp.zeros(ref.shape, ref.dtype)

    given = inputs[...]
    feeds = [given]
    slopes = []
    for k in range(4):
        weight = first_in[...] if k == 0 else inner[k - 1]
        preact = jnp.dot(feeds[-1], weight, preferred_element_type=F32) + bias[k : k + 1, :]
        gate = 0.5 * jnp.tanh(0.5 * preact) + 0.5
        active = preact * gate
        slopes.append(gate + active * (1.0 - gate))
        feeds.append(active.astype(BF16))
    output = jnp.dot(feeds[-1], last[...], preferred_element_type=F32) + bias_last[...]
    residue = jnp.where(lane >= levels, given.astype(F32) + output, 0.0)
    error = residue.astype(BF16)
    over_rows = (((0,), (0,)), ((), ()))
    over_lanes = (((1,), (1,)), ((), ()))

    def row_sum(value):
        return jnp.sum(value.reshape(cells // SUBLANES, SUBLANES, value.shape[1]), axis=0)

    acc_bias_last[...] += row_sum(error.astype(F32))
    acc_last[...] += lax.dot_general(feeds[4], error, over_rows, preferred_element_type=F32)
    carried = lax.dot_general(error, last[...], over_lanes, preferred_element_type=F32)
    for k in (3, 2, 1, 0):
        exact = carried * slopes[k]
        error = exact.astype(BF16)
        acc_bias[k] += row_sum(error.astype(F32))
        product = lax.dot_general(feeds[k], error, over_rows, preferred_element_type=F32)
        if k > 0:
            acc_inner[k - 1] += product
            carried = lax.dot_general(error, inner[k - 1], over_lanes, preferred_element_type=F32)
        else:
            acc_first[...] += product[:levels]
            carried = lax.dot_general(error, first_out[...], over_lanes, preferred_element_type=F32)
    back = residue + carried
    out[...] = squeeze_lanes(back, 1).astype(BF16)

    @pl.when(block == pl.num_programs(0) - 1)
    def _():
        row = 0

        def put(value):
            nonlocal row
            grads[row : row + value.shape[0], :] = value.astype(BF16)
            row += value.shape[0]

        for k in range(3):
            put(acc_inner[k][:, :LANES])
            put(squeeze_lanes(widen(acc_inner[k][:, LANES:]), 0))
        put(acc_first[...][:, :LANES])
        put(squeeze_lanes(widen(acc_first[...][:, LANES:]), 0))
        put(squeeze_lanes(acc_last[...], 1))
        pieces = [jnp.sum(acc_bias[k], axis=0, keepdims=True) for k in range(4)]
        tail = [piece[:, :LANES] for piece in pieces]
        tail += [widen(piece[:, LANES:]) for piece in pieces]
        tail.append(pltpu.roll(jnp.sum(acc_bias_last[...], axis=0, keepdims=True), LANES // 2, 1))
        tail.append(jnp.zeros((grads.shape[0] - row - len(tail), LANES), F32))
        put(jnp.concatenate(tail, axis=0))


def widen(value):
    missing = LANES - value.shape[1]
    return jnp.concatenate([value, jnp.zeros((value.shape[0], missing), value.dtype)], axis=1)


def grad_rows(levels, width, tiles):
    rows = 3 * (width + width // 2) + levels + levels // 2 + width // 2 + 16
    unit = 16 * tiles
    return (rows + unit - 1) // unit * unit


def network(received, w_first, w_inner, w_last, b_inner, b_last, tiles, subs):
    cells, doubled = received.shape
    levels = doubled // 2
    width = w_first.shape[1]
    block = cells // subs
    zeros = jnp.zeros_like(w_first)
    first_in = jnp.concatenate([w_first, zeros], axis=0)
    first_out = jnp.concatenate([zeros, w_first], axis=0)
    last = jnp.concatenate([jnp.zeros_like(w_last), w_last], axis=1)
    bias_last = jnp.concatenate([jnp.zeros_like(b_last), b_last])[None]
    rows = grad_rows(levels, width, tiles)

    def whole(*shape):
        return pl.BlockSpec(shape, lambda i: (0,) * len(shape))

    return pl.pallas_call(
        functools.partial(network_body, levels, width, block),
        grid=(subs,),
        out_shape=[
            jax.ShapeDtypeStruct((cells // 2, doubled), BF16),
            jax.ShapeDtypeStruct((rows, LANES), BF16),
        ],
        in_specs=[
            pl.BlockSpec((block, doubled), lambda i: (i, 0)),
            whole(doubled, width),
            whole(doubled, width),
            whole(3, width, width),
            whole(width, doubled),
            whole(4, width),
            whole(1, doubled),
        ],
        out_specs=[
            pl.BlockSpec((block // 2, doubled), lambda i: (i, 0)),
            whole(rows, LANES),
        ],
        scratch_shapes=[
            pltpu.VMEM((levels, width), F32),
            pltpu.VMEM((3, width, width), F32),
            pltpu.VMEM((width, doubled), F32),
            pltpu.VMEM((4, SUBLANES, width), F32),
            pltpu.VMEM((SUBLANES, doubled), F32),
        ],
        compiler_params=PARAMS,
        name="network",
    )(received, first_in, first_out, w_inner, last, b_inner, bias_last)


def sum_body(parts, out):
    total = parts[0].astype(F32)
    for index in range(1, parts.shape[0]):
        total = total + parts[index].astype(F32)
    total = total.astype(BF16)
    for index in range(parts.shape[0]):
        out[index] = total


def sum_parts(parts):
    return pl.pallas_call(
        sum_body,
        out_shape=jax.ShapeDtypeStruct(parts.shape, BF16),
        in_specs=[VMEM],
        out_specs=VMEM,
        compiler_params=PARAMS,
        name="sum_parts",
    )(parts)


def steps_body(levels, width, count, whole, first, inner, last, bias, bias_last):
    def squares(index, total):
        part = whole[pl.ds(pl.multiple_of(index * 16, 16), 16), :].astype(F32)
        return total + part * part

    total = lax.fori_loop(0, whole.shape[0] // 16, squares, jnp.zeros((16, LANES), F32), unroll=4)
    factor = 1.0 / jnp.sqrt(jnp.broadcast_to(jnp.sum(total), (1, LANES)) / count + 1e-06)
    row = 0

    def take(size):
        nonlocal row
        value = whole[row : row + size, :].astype(F32) * factor
        row += size
        return value

    half = LANES // 2

    def unpack(ref, size):
        low = take(size)
        narrow = take(size // 2)
        ref[:, :LANES] = low
        ref[: size // 2, LANES:] = narrow[:, :half]
        ref[size // 2 :, LANES:] = pltpu.roll(narrow, half, 1)[:, :half]

    for k in range(3):
        unpack(inner.at[k], width)
    unpack(first, levels)
    narrow = take(width // 2)
    last[: width // 2, :] = narrow[:, :half]
    last[width // 2 :, :] = pltpu.roll(narrow, half, 1)[:, :half]
    tail = take(16)
    bias[:, :LANES] = tail[0:4]
    bias[:, LANES:] = tail[4:8, :half]
    bias_last[...] = tail[8:9, :half]


def make_steps(whole, levels, width):
    count = 2 * levels * width + 3 * width * width + 4 * width + levels
    return pl.pallas_call(
        functools.partial(steps_body, levels, width, float(count)),
        out_shape=[
            jax.ShapeDtypeStruct((levels, width), F32),
            jax.ShapeDtypeStruct((3, width, width), F32),
            jax.ShapeDtypeStruct((width, levels), F32),
            jax.ShapeDtypeStruct((4, width), F32),
            jax.ShapeDtypeStruct((1, levels), F32),
        ],
        in_specs=[VMEM],
        out_specs=[VMEM] * 5,
        compiler_params=PARAMS,
        name="make_steps",
    )(whole)


def scatter_body(
    levels, width_x, width_y, tiles, subs,
    counts, order, answers, grid, top, bottom, low, high, slots, rows, bases, starts,
):
    cells = width_x * width_y
    devices = tiles * subs
    packet = cells // subs
    half = packet // 2
    fill_starts(counts, starts, devices)

    def place(index, base):
        device = index % tiles * subs + index // tiles
        bases[device] = base
        return base + counts[device]

    lax.fori_loop(0, devices, place, jnp.int32(0))
    for expert in range(subs):
        pair = answers[expert * half : (expert + 1) * half, :].astype(F32)
        slots[expert * packet : expert * packet + half, :] = pair
        slots[expert * packet + half : (expert + 1) * packet, :] = pltpu.roll(pair, levels, 1)

    def run(device, carry):
        count = counts[device]
        start = starts[device]
        base = bases[device]

        def copy(chunk, carry):
            offset = chunk * UNROLL
            taken = [slots[pl.ds(base + offset + u, 1), :] for u in range(UNROLL)]
            for u in range(UNROLL):
                rows[pl.ds(order[start + offset + u], 1), :] = taken[u]
            return carry

        lax.fori_loop(0, (count + UNROLL - 1) // UNROLL, copy, 0)
        return carry

    lax.fori_loop(0, devices, run, 0)

    def turn(tile, carry):
        span = pl.ds(pl.multiple_of(tile * LANES, LANES), LANES)
        grid[:, span] = rows[span, :].T[:levels]
        return carry

    lax.fori_loop(0, cells // LANES, turn, 0, unroll=2)

    lows, highs = [], []
    for group in range(levels // SUBLANES):
        where = slice(group * SUBLANES, (group + 1) * SUBLANES)
        low_value, high_value = compact_edges(
            lambda x: grid[where, x * width_y : (x + 1) * width_y], width_x, width_y
        )
        lows.append(low_value)
        highs.append(high_value)
    low[...] = jnp.concatenate(lows, axis=0).astype(BF16)
    high[...] = jnp.concatenate(highs, axis=0).astype(BF16)
    top[...] = grid[:, : 2 * width_y].astype(BF16)
    bottom[...] = grid[:, cells - 2 * width_y :].astype(BF16)


def scatter(counts, order, answers, sizes):
    levels, width_x, width_y, tiles, subs = sizes
    cells = width_x * width_y
    return pl.pallas_call(
        functools.partial(scatter_body, levels, width_x, width_y, tiles, subs),
        out_shape=[
            jax.ShapeDtypeStruct((levels, cells), F32),
            jax.ShapeDtypeStruct((levels, 2 * width_y), BF16),
            jax.ShapeDtypeStruct((levels, 2 * width_y), BF16),
            jax.ShapeDtypeStruct((levels, LANES), BF16),
            jax.ShapeDtypeStruct((levels, LANES), BF16),
        ],
        in_specs=[SMEM] * 2 + [VMEM],
        out_specs=[VMEM] * 5,
        scratch_shapes=[
            pltpu.VMEM((cells + UNROLL, 2 * levels), F32),
            pltpu.VMEM((cells + SUBLANES, 2 * levels), F32),
            pltpu.SMEM((tiles * subs,), jnp.int32),
            pltpu.SMEM((tiles * subs,), jnp.int32),
        ],
        compiler_params=PARAMS,
        name="scatter",
    )(counts, order, answers)


def adjoint_body(
    levels, width_x, width_y,
    grid, diff, own_low, own_high, diff_own_low, diff_own_high,
    up, down, left, right, up_left, up_right, down_left, down_right,
    diff_up, diff_down, diff_left, diff_right,
    diff_up_left, diff_up_right, diff_down_left, diff_down_right,
    out, wide, flow, e1,
):
    y_tiles = width_y // LANES
    stride = width_x * y_tiles

    def at(x):
        return slice((x + 2) * width_y, (x + 3) * width_y)

    last = pl.ds(levels, SUBLANES)
    for x in range(width_x):
        wide[:, at(x)] = load_wide(diff, x, width_y)
    for k in range(2):
        wide[:, at(k - 2)] = diff_up[last, k * width_y : (k + 1) * width_y]
        wide[:, at(width_x + k)] = diff_down[last, k * width_y : (k + 1) * width_y]
    rate_left = with_corners(
        diff_left[last, :], diff_up_left[last, :], diff_down_left[last, :], width_x
    )
    rate_right = with_corners(
        diff_right[last, :], diff_up_right[last, :], diff_down_right[last, :], width_x
    )

    def pair(value, which):
        return value.astype(F32)[which * SUBLANES : (which + 1) * SUBLANES]

    def step(double, carry):
        where = pl.ds(pl.multiple_of(double * 2 * SUBLANES, 2 * SUBLANES), 2 * SUBLANES)
        packed = [
            ref[where, :]
            for ref in (
                own_low, own_high, up, down, left, right,
                up_left, up_right, down_left, down_right,
            )
        ]
        for which in range(2):
            group = double * 2 + which
            own = groups_at(group)
            (
                own_l, own_h, above, below, at_left, at_right, at_ul, at_ur, at_dl, at_dr
            ) = [pair(value, which) for value in packed]
            side_left = with_corners(at_left, at_ul, at_dl, width_x)
            side_right = with_corners(at_right, at_ur, at_dr, width_x)

            def next_side(side, rate, outer, outer_rate, mine, mine_rate):
                product = side * rate
                return product, side + (
                    around(product)
                    + second(outer) * second(outer_rate)
                    + mine * mine_rate
                    - 4.0 * product
                )

            flow_left, next_left = next_side(
                side_left, rate_left, at_left, diff_left[last, :], own_l, diff_own_low[last, :]
            )
            flow_right, next_right = next_side(
                side_right, rate_right, at_right, diff_right[last, :], own_h, diff_own_high[last, :]
            )

            def value(x):
                if x < 0:
                    return above[:, (x + 2) * width_y : (x + 3) * width_y]
                if x >= width_x:
                    return below[:, (x - width_x) * width_y : (x - width_x + 1) * width_y]
                return grid[own, x * width_y : (x + 1) * width_y]

            for x in range(-2, width_x + 2):
                flow[:, at(x)] = value(x) * wide[:, at(x)]
            for x in range(-1, width_x + 1):
                row = flow[:, at(x)]
                near = flow[:, at(x - 1)] + flow[:, at(x + 1)]
                near = near + beside(row, flow_left, flow_right, x)
                e1[:, at(x)] = value(x) + near - 4.0 * row
            for x in range(-1, width_x + 1):
                flow[:, at(x)] = e1[:, at(x)] * wide[:, at(x)]
            flow_left = next_left * rate_left
            flow_right = next_right * rate_right
            for x in range(width_x):
                row = flow[:, at(x)]
                near = flow[:, at(x - 1)] + flow[:, at(x + 1)]
                near = near + beside(row, flow_left, flow_right, x)
                result = e1[:, at(x)] + near - 4.0 * row
                for y_tile in range(y_tiles):
                    offset = group * (SUBLANES * stride) + row_offset(x, y_tile, y_tiles)
                    out[pl.ds(offset, SUBLANES, stride=stride), :] = result[
                        :, y_tile * LANES : (y_tile + 1) * LANES
                    ]
        return carry

    lax.fori_loop(0, levels // (2 * SUBLANES), step, 0)


def adjoint(grid, diff_rows, own, diff_own, halos, diff_halos, sizes):
    levels, width_x, width_y, _, _ = sizes
    extended = (SUBLANES, (width_x + 4) * width_y)
    return pl.pallas_call(
        functools.partial(adjoint_body, levels, width_x, width_y),
        out_shape=jax.ShapeDtypeStruct((levels * width_x * width_y // LANES, LANES), F32),
        in_specs=[VMEM] * 22,
        out_specs=VMEM,
        scratch_shapes=[pltpu.VMEM(extended, F32)] * 3,
        compiler_params=PARAMS,
        name="adjoint",
    )(grid, diff_rows, *own, *diff_own, *halos, *diff_halos)


def per_device(
    initial, targets, diffusivity, column_order, send_counts,
    w_first, w_inner, w_last, b_inner, b_last,
):
    levels, width_x, width_y = initial.shape
    tiles, subs = lax.axis_size("tile"), lax.axis_size("sub")
    cells = width_x * width_y
    sizes = (levels, width_x, width_y, tiles, subs)
    field_rows = tile_rows(initial)
    target_rows = tile_rows(targets)
    diff_rows = tile_rows(diffusivity[None])
    counts = send_counts[0]
    order = jnp.pad(column_order[0], (0, LANES), constant_values=cells)
    top, bottom, low, high = pack_edges(field_rows, diff_rows, levels, width_x, width_y)
    halos = exchange(top, bottom, low, high)
    blocks = forward(counts, order, field_rows, target_rows, diff_rows, low, high, halos, sizes)
    received = lax.all_to_all(
        blocks.reshape(subs, cells // subs, 2 * levels), "sub", split_axis=0, concat_axis=0, tiled=True
    ).reshape(cells, 2 * levels)
    returning, gradients = network(
        received, w_first[0], w_inner[0], w_last[0], b_inner[0], b_last[0], tiles, subs
    )
    answers = lax.all_to_all(
        returning.reshape(subs, cells // subs // 2, 2 * levels),
        "sub", split_axis=0, concat_axis=0, tiled=True,
    ).reshape(cells // 2, 2 * levels)
    parts = lax.all_to_all(
        gradients.reshape(tiles, -1, LANES), "tile", split_axis=0, concat_axis=0, tiled=True
    )
    whole = lax.all_to_all(
        sum_parts(parts), "tile", split_axis=0, concat_axis=0, tiled=True
    ).reshape(-1, LANES)
    steps = make_steps(whole, levels, w_first.shape[2])
    grid, g_top, g_bottom, g_low, g_high = scatter(counts, order, answers, sizes)
    g_halos = exchange(g_top, g_bottom, g_low, g_high)
    result = adjoint(grid, diff_rows, (g_low, g_high), (low, high), g_halos, halos, sizes)
    return (
        untile_rows(result, levels, width_x, width_y),
        steps[0][None], steps[1][None], steps[2][None], steps[3][None], steps[4],
    )


def solution(mesh):
    placed = (
        P(None, "tile", "sub"),
        P(None, "tile", "sub"),
        P("tile", "sub"),
        P(("tile", "sub"), None),
        P(("tile", "sub"), None),
        P("sub", None, None),
        P("sub", None, None, None),
        P("sub", None, None),
        P("sub", None, None),
        P("sub", None),
    )
    return jax.shard_map(
        per_device,
        mesh=mesh,
        in_specs=placed,
        out_specs=(
            P(None, "tile", "sub"),
            P("sub", None, None),
            P("sub", None, None, None),
            P("sub", None, None),
            P("sub", None, None),
            P("sub", None),
        ),
        check_vma=False,
    )
```

```python
import functools
import jax
import jax.numpy as jnp
from jax import lax
from jax.experimental import pallas as pl
from jax.experimental.pallas import tpu as pltpu
from jax.sharding import PartitionSpec as P

LANES = 128
SUBLANES = 8
SECOND = 32
UNROLL = 16
VMEM = pl.BlockSpec(memory_space=pltpu.VMEM)
SMEM = pl.BlockSpec(memory_space=pltpu.SMEM)
PARAMS = pltpu.CompilerParams(vmem_limit_bytes=32 * 1024 * 1024)
F32 = jnp.float32
BF16 = jnp.bfloat16


def tile_rows(cells):
    levels, width_x, width_y = cells.shape
    split = cells.reshape(levels, width_x // SUBLANES, SUBLANES, width_y // LANES, LANES)
    return split.transpose(0, 1, 3, 2, 4).reshape(-1, LANES)


def untile_rows(rows, levels, width_x, width_y):
    split = rows.reshape(levels, width_x // SUBLANES, width_y // LANES, SUBLANES, LANES)
    return split.transpose(0, 1, 3, 2, 4).reshape(levels, width_x, width_y)


def row_offset(x, y_tile, y_tiles):
    return (x // SUBLANES * y_tiles + y_tile) * SUBLANES + x % SUBLANES


def load_row(ref, group, x, width_x, width_y):
    y_tiles = width_y // LANES
    stride = width_x * y_tiles
    base = group * (SUBLANES * stride)
    return jnp.concatenate(
        [
            ref[pl.ds(base + row_offset(x, y_tile, y_tiles), SUBLANES, stride=stride), :]
            for y_tile in range(y_tiles)
        ],
        axis=1,
    )


def load_wide(ref, x, width_y):
    y_tiles = width_y // LANES
    return jnp.concatenate(
        [
            jnp.broadcast_to(ref[pl.ds(row_offset(x, y_tile, y_tiles), 1), :], (SUBLANES, LANES))
            for y_tile in range(y_tiles)
        ],
        axis=1,
    )


def lane_ids(width):
    return lax.broadcasted_iota(jnp.int32, (SUBLANES, width), 1)


def compact_edges(row_of, width_x, width_y):
    lane = lane_ids(LANES)
    low = jnp.zeros((SUBLANES, LANES), F32)
    high = jnp.zeros((SUBLANES, LANES), F32)
    for x in range(width_x):
        row = row_of(x)
        low = jnp.where(lane == 1 + x, row[:, 0:1], low)
        low = jnp.where(lane == SECOND + 1 + x, row[:, 1:2], low)
        high = jnp.where(lane == 1 + x, row[:, width_y - 1 : width_y], high)
        high = jnp.where(lane == SECOND + 1 + x, row[:, width_y - 2 : width_y - 1], high)
    return low, high


def groups_at(group):
    return pl.ds(pl.multiple_of(group * SUBLANES, SUBLANES), SUBLANES)


def pack_body(levels, width_x, width_y, field, diff, top, bottom, low, high):
    def emit(where, row_of):
        for k in range(2):
            top[where, k * width_y : (k + 1) * width_y] = row_of(k)
            bottom[where, k * width_y : (k + 1) * width_y] = row_of(width_x - 2 + k)
        low_value, high_value = compact_edges(row_of, width_x, width_y)
        low[where, :] = low_value
        high[where, :] = high_value

    def step(group, carry):
        emit(groups_at(group), lambda x: load_row(field, group, x, width_x, width_y))
        return carry

    lax.fori_loop(0, levels // SUBLANES, step, 0)
    emit(pl.ds(levels, SUBLANES), lambda x: load_wide(diff, x, width_y))


def pack_edges(field_rows, diff_rows, levels, width_x, width_y):
    tall = levels + SUBLANES
    return pl.pallas_call(
        functools.partial(pack_body, levels, width_x, width_y),
        out_shape=[
            jax.ShapeDtypeStruct((tall, 2 * width_y), F32),
            jax.ShapeDtypeStruct((tall, 2 * width_y), F32),
            jax.ShapeDtypeStruct((tall, LANES), F32),
            jax.ShapeDtypeStruct((tall, LANES), F32),
        ],
        in_specs=[VMEM] * 2,
        out_specs=[VMEM] * 4,
        compiler_params=PARAMS,
        name="pack_edges",
    )(field_rows, diff_rows)


def shifted(array, shift_tile, shift_sub):
    tiles, subs = lax.axis_size("tile"), lax.axis_size("sub")
    if shift_tile == 0:
        return lax.ppermute(array, "sub", [(i, (i + shift_sub) % subs) for i in range(subs)])
    if shift_sub == 0:
        return lax.ppermute(array, "tile", [(i, (i + shift_tile) % tiles) for i in range(tiles)])
    pairs = []
    for t in range(tiles):
        for s in range(subs):
            target = (t + shift_tile) % tiles * subs + (s + shift_sub) % subs
            pairs.append((t * subs + s, target))
    return lax.ppermute(array, ("tile", "sub"), pairs)


def exchange(top, bottom, low, high):
    return (
        shifted(bottom, 1, 0),
        shifted(top, -1, 0),
        shifted(high, 0, 1),
        shifted(low, 0, -1),
        shifted(high, 1, 1),
        shifted(low, 1, -1),
        shifted(high, -1, 1),
        shifted(low, -1, -1),
    )


def with_corners(side, before, after, width_x):
    lane = lane_ids(LANES)
    value = jnp.where(lane == 0, pltpu.roll(before, LANES - width_x, 1), side)
    return jnp.where(lane == width_x + 1, pltpu.roll(after, width_x, 1), value)


def around(side):
    return pltpu.roll(side, 1, 1) + pltpu.roll(side, LANES - 1, 1)


def second(side):
    return pltpu.roll(side, LANES - SECOND, 1)


def beside(row, left, right, x):
    width = row.shape[1]
    lane = lane_ids(width)
    return jnp.where(lane == 0, left[:, x + 1 : x + 2], pltpu.roll(row, 1, 1)) + jnp.where(
        lane == width - 1, right[:, x + 1 : x + 2], pltpu.roll(row, width - 1, 1)
    )


def forward_body(
    levels, width_x, width_y,
    field, target, diff, own_low, own_high, up, down, left, right,
    up_left, up_right, down_left, down_right, rows, e0, e1, wide, both,
):
    cells = width_x * width_y

    def at(x):
        return slice((x + 2) * width_y, (x + 3) * width_y)

    def sides(where):
        return (
            with_corners(left[where, :], up_left[where, :], down_left[where, :], width_x),
            with_corners(right[where, :], up_right[where, :], down_right[where, :], width_x),
        )

    last = pl.ds(levels, SUBLANES)
    for x in range(width_x):
        wide[:, at(x)] = load_wide(diff, x, width_y)
    wide[:, at(-1)] = up[last, width_y:]
    wide[:, at(width_x)] = down[last, :width_y]
    diff_left, diff_right = sides(last)

    def step(group, carry):
        where = groups_at(group)
        for x in range(width_x):
            e0[:, at(x)] = load_row(field, group, x, width_x, width_y)
        for k in range(2):
            e0[:, at(k - 2)] = up[where, k * width_y : (k + 1) * width_y]
            e0[:, at(width_x + k)] = down[where, k * width_y : (k + 1) * width_y]
        side_left, side_right = sides(where)

        def next_side(side, outer, own, coefficient):
            return side + coefficient * (around(side) + second(outer) + own - 4.0 * side)

        next_left = next_side(side_left, left[where, :], own_low[where, :], diff_left)
        next_right = next_side(side_right, right[where, :], own_high[where, :], diff_right)
        for x in range(-1, width_x + 1):
            row = e0[:, at(x)]
            near = e0[:, at(x - 1)] + e0[:, at(x + 1)] + beside(row, side_left, side_right, x)
            e1[:, at(x)] = row + wide[:, at(x)] * (near - 4.0 * row)
        for x in range(width_x):
            row = e1[:, at(x)]
            near = e1[:, at(x - 1)] + e1[:, at(x + 1)] + beside(row, next_left, next_right, x)
            value = row + wide[:, at(x)] * (near - 4.0 * row)
            both[where, x * width_y : (x + 1) * width_y] = value
            both[
                pl.ds(pl.multiple_of(levels + group * SUBLANES, SUBLANES), SUBLANES),
                x * width_y : (x + 1) * width_y,
            ] = value - load_row(target, group, x, width_x, width_y)
        return carry

    lax.fori_loop(0, levels // SUBLANES, step, 0)

    def turn(tile, carry):
        span = pl.ds(pl.multiple_of(tile * LANES, LANES), LANES)
        rows[span, :] = both[:, span].T
        return carry

    lax.fori_loop(0, cells // LANES, turn, 0, unroll=2)


def forward(field_rows, target_rows, diff_rows, own_low, own_high, halos, sizes):
    levels, width_x, width_y, _, _ = sizes
    cells = width_x * width_y
    return pl.pallas_call(
        functools.partial(forward_body, levels, width_x, width_y),
        out_shape=jax.ShapeDtypeStruct((cells, 2 * levels), F32),
        in_specs=[VMEM] * 13,
        out_specs=VMEM,
        scratch_shapes=[
            pltpu.VMEM((SUBLANES, (width_x + 4) * width_y), F32),
            pltpu.VMEM((SUBLANES, (width_x + 4) * width_y), F32),
            pltpu.VMEM((SUBLANES, (width_x + 4) * width_y), F32),
            pltpu.VMEM((2 * levels, cells), F32),
        ],
        compiler_params=PARAMS,
        name="forward",
    )(field_rows, target_rows, diff_rows, own_low, own_high, *halos)


def index_body(tiles, subs, lead, rows_each, parity, counts, order, out, starts):
    devices = tiles * subs

    def begin(index, total):
        starts[index] = total
        return total + counts[index]

    lax.fori_loop(0, devices, begin, jnp.int32(0))
    half = subs // 2
    flip = parity[0]
    lane = lax.broadcasted_iota(jnp.int32, (SUBLANES, LANES), 1)
    slot = lax.broadcasted_iota(jnp.int32, (SUBLANES, LANES), 0) * LANES + lane

    def expert(block, carry):
        second_half = block // half
        network_id = (block - second_half * half) * 2 + (1 - flip) * (1 - second_half) + flip * second_half
        value = jnp.zeros((SUBLANES, LANES), jnp.int32)
        base = jnp.int32(0)
        for t in range(tiles):
            device = t * subs + network_id
            count = counts[device]
            offset = starts[device] - base + lead
            shift = lax.rem(offset, LANES)
            window = order[pl.ds(lax.div(offset, LANES), SUBLANES), :]
            turned = pltpu.roll(window, lax.rem(LANES - shift, LANES), 1)
            following = jnp.concatenate([turned[1:], turned[:1]], axis=0)
            moved = jnp.where(lane < LANES - shift, turned, following)
            value = jnp.where((slot >= base) & (slot < base + count), moved, value)
            base = base + count
        out[pl.ds(block * rows_each, SUBLANES), :] = value
        return carry

    lax.fori_loop(0, subs, expert, 0)


def slot_cells(parity, counts, column_order, sizes):
    _, width_x, width_y, tiles, subs = sizes
    cells = width_x * width_y
    packet = cells // subs
    rows_each = packet // LANES
    lead = packet
    order = jnp.pad(column_order, (lead, SUBLANES * LANES)).reshape(-1, LANES)
    return pl.pallas_call(
        functools.partial(index_body, tiles, subs, lead, rows_each),
        out_shape=jax.ShapeDtypeStruct((cells // LANES + SUBLANES, LANES), jnp.int32),
        in_specs=[SMEM] * 2 + [VMEM],
        out_specs=VMEM,
        scratch_shapes=[pltpu.SMEM((tiles * subs,), jnp.int32)],
        compiler_params=PARAMS,
        name="slot_cells",
    )(parity, counts, order).reshape(-1)


def widen(value):
    missing = LANES - value.shape[1]
    return jnp.concatenate([value, jnp.zeros((value.shape[0], missing), value.dtype)], axis=1)


def lower_half(rows):
    return lax.broadcasted_iota(jnp.int32, (rows, LANES), 1) < LANES // 2


def swap_halves(value):
    return pltpu.roll(value, LANES // 2, 1)


def squeeze_rows(value):
    count = value.shape[0] // 2
    return jnp.where(lower_half(count), value[:count], swap_halves(value[count:]))


def pack_rows(put, inner, first, last, biases):
    width = first.shape[1]
    for k in range(3):
        put(inner[k][:, :LANES])
    low = lower_half(width)
    put(jnp.where(low, widen(inner[0][:, LANES:]), swap_halves(widen(inner[1][:, LANES:]))))
    put(jnp.where(low, widen(inner[2][:, LANES:]), last))
    put(first[:, :LANES])
    put(squeeze_rows(widen(first[:, LANES:])))
    tail = []
    for bias, bias_last in biases:
        tail += [piece[:, :LANES] for piece in bias]
        tail += [
            jnp.where(
                lower_half(1), widen(bias[k][:, LANES:]), swap_halves(widen(bias[k + 1][:, LANES:]))
            )
            for k in (0, 2)
        ]
        tail.append(bias_last)
    return tail


def pack_size(levels, width, tiles):
    rows = 5 * width + levels + levels // 2 + 16
    unit = 16 * tiles
    return (rows + unit - 1) // unit * unit


def weights_body(w_first, w_inner, w_last, b_inner, b_last, out):
    row = 0

    def put(value):
        nonlocal row
        value = value.astype(BF16)
        for copy in range(out.shape[0]):
            out[copy, row : row + value.shape[0], :] = value
        row += value.shape[0]

    bias = b_inner[...]
    bias_last = swap_halves(widen(b_last[...]))
    bias_high = bias.astype(BF16).astype(F32)
    last_high = bias_last.astype(BF16).astype(F32)
    bias_low = bias - bias_high
    last_low = bias_last - last_high
    tail = pack_rows(
        put,
        [w_inner[k].astype(F32) for k in range(3)],
        w_first[...].astype(F32),
        swap_halves(widen(w_last[...].astype(F32))),
        [
            ([bias_high[k : k + 1] for k in range(4)], last_high),
            ([bias_low[k : k + 1] for k in range(4)], last_low),
        ],
    )
    tail.append(jnp.zeros((out.shape[1] - row - len(tail), LANES), F32))
    put(jnp.concatenate(tail, axis=0))


def pack_weights(w_first, w_inner, w_last, b_inner, b_last, tiles, copies):
    levels, width = w_first.shape
    return pl.pallas_call(
        weights_body,
        out_shape=jax.ShapeDtypeStruct((copies, pack_size(levels, width, tiles), LANES), BF16),
        in_specs=[VMEM] * 5,
        out_specs=VMEM,
        compiler_params=PARAMS,
        name="pack_weights",
    )(w_first, w_inner, w_last, b_inner, b_last)


def network_body(
    levels, width, packet, shift_block,
    cells_of, packs, rows, back_in, back, grads,
    taken, given_back, first_in, first_out, inner, last, last_half, bias, bias_last,
):
    block = pl.program_id(0)
    blocks = pl.num_programs(0)
    narrow = width - LANES
    lane = lax.broadcasted_iota(jnp.int32, (packet, LANES), 1)

    def fetch(base, first_slot, count):
        for u in range(first_slot, first_slot + count):
            taken[u : u + 1, :] = rows[pl.ds(cells_of[base + u], 1), :]

    def deliver(base, first_slot, count):
        for u in range(first_slot, first_slot + count):
            back[pl.ds(cells_of[base + u], 1), :] = given_back[u : u + 1, :]

    here = (block + shift_block) * packet

    @pl.when(block == 0)
    def _():
        def step(index, carry):
            for u in range(UNROLL):
                slot = index * UNROLL + u
                taken[pl.ds(slot, 1), :] = rows[pl.ds(cells_of[here + slot], 1), :]
            return carry

        lax.fori_loop(0, packet // UNROLL, step, 0)

    row = 0

    def take(size):
        nonlocal row
        value = packs[0, row : row + size, :].astype(F32)
        row += size
        return value

    def halves(value):
        return value[:, :narrow], swap_halves(value)[:, :narrow]

    for k in range(3):
        inner[k, :, :LANES] = (0.5 * take(width)).astype(BF16)
    narrow_a, narrow_b = halves(0.5 * take(width))
    inner[0, :, LANES:] = narrow_a.astype(BF16)
    inner[1, :, LANES:] = narrow_b.astype(BF16)
    mixed = take(width)
    inner[2, :, LANES:] = (0.5 * mixed[:, :narrow]).astype(BF16)
    out_weight = jnp.where(lower_half(width), 0.0, mixed)
    last[...] = out_weight.astype(BF16)
    last_half[...] = (0.5 * out_weight).astype(BF16)
    wide_first = take(levels)
    narrow_a, narrow_b = halves(take(levels // 2))
    first_in[levels:, :] = jnp.zeros((levels, width), BF16)
    first_out[:levels, :] = jnp.zeros((levels, width), BF16)
    first_in[:levels, :LANES] = (0.5 * wide_first).astype(BF16)
    first_out[levels:, :LANES] = wide_first.astype(BF16)
    half_levels = levels // 2
    first_in[:half_levels, LANES:] = (0.5 * narrow_a).astype(BF16)
    first_in[half_levels:levels, LANES:] = (0.5 * narrow_b).astype(BF16)
    first_out[levels : levels + half_levels, LANES:] = narrow_a.astype(BF16)
    first_out[levels + half_levels :, LANES:] = narrow_b.astype(BF16)
    tail = take(16)
    tail = tail[0:7] + tail[7:14]
    bias[:, :LANES] = 0.5 * tail[0:4]
    for k in (0, 2):
        narrow_a, narrow_b = halves(0.5 * tail[4 + k // 2 : 5 + k // 2])
        bias[k : k + 1, LANES:] = narrow_a
        bias[k + 1 : k + 2, LANES:] = narrow_b
    bias_last[...] = tail[6:7]

    given = taken[...].astype(BF16)
    ahead = (lax.rem(block + 1, blocks) + shift_block) * packet
    behind = (jnp.maximum(block - 1, 0) + shift_block) * packet
    pieces = 8
    size = packet // pieces

    def move(piece):
        deliver(behind, piece * size, size)
        fetch(ahead, piece * size, size)

    over_rows = (((0,), (0,)), ((), ()))
    over_lanes = (((1,), (1,)), ((), ()))
    feeds = [given]
    slopes = []
    for k in range(4):
        weight = first_in[...] if k == 0 else inner[k - 1]
        half_preact = jnp.dot(feeds[-1], weight, preferred_element_type=F32) + bias[k : k + 1, :]
        turn = jnp.tanh(half_preact)
        plus = 1.0 + turn
        active = half_preact * plus
        slopes.append(plus + active * (1.0 - turn))
        feeds.append(active.astype(BF16))
        move(k)
    output = jnp.dot(feeds[-1], last[...], preferred_element_type=F32) + bias_last[...]
    residue = jnp.where(lane >= levels, given.astype(F32) + output, 0.0)
    error = residue.astype(BF16)

    def row_sum(value):
        return jnp.sum(value, axis=0, keepdims=True)

    last_bias = row_sum(residue)
    last_grad = lax.dot_general(feeds[4], error, over_rows, preferred_element_type=F32)
    carried = lax.dot_general(error, last_half[...], over_lanes, preferred_element_type=F32)
    weight_grads = [None] * 4
    bias_grads = [None] * 4
    for k in (3, 2, 1, 0):
        exact = carried * slopes[k]
        error = exact.astype(BF16)
        bias_grads[k] = row_sum(exact)
        weight_grads[k] = lax.dot_general(feeds[k], error, over_rows, preferred_element_type=F32)
        weight = inner[k - 1] if k > 0 else first_out[...]
        carried = lax.dot_general(error, weight, over_lanes, preferred_element_type=F32)
        move(7 - k)
    given_back[...] = residue + carried

    filled = 0

    def put(value):
        nonlocal filled
        grads[0, filled : filled + value.shape[0], :] = value.astype(BF16)
        filled += value.shape[0]

    tail = pack_rows(
        put, weight_grads[1:], weight_grads[0][:levels], last_grad, [(bias_grads, last_bias)]
    )
    tail.append(jnp.zeros((grads.shape[1] - filled - len(tail), LANES), F32))
    put(jnp.concatenate(tail, axis=0))

    @pl.when(block == blocks - 1)
    def _():
        def step(index, carry):
            for u in range(UNROLL):
                slot = index * UNROLL + u
                back[pl.ds(cells_of[here + slot], 1), :] = given_back[pl.ds(slot, 1), :]
            return carry

        lax.fori_loop(0, packet // UNROLL, step, 0)


def network(cells_of, packs, rows, back, shift_block, levels, width, subs):
    cells, doubled = rows.shape
    packet = cells // subs
    blocks, pack_rows_count, _ = packs.shape
    body = functools.partial(network_body, levels, width, packet, shift_block)
    operands = [cells_of, packs, rows]
    in_specs = [SMEM, pl.BlockSpec((1, pack_rows_count, LANES), lambda i: (i, 0, 0)), VMEM]
    aliases = {}
    if back is None:
        body = lambda a, b, c, *rest: network_body(
            levels, width, packet, shift_block, a, b, c, None, *rest
        )
    else:
        operands.append(back)
        in_specs.append(VMEM)
        aliases = {3: 0}
    return pl.pallas_call(
        body,
        grid=(blocks,),
        out_shape=[
            jax.ShapeDtypeStruct((cells, doubled), F32),
            jax.ShapeDtypeStruct(packs.shape, BF16),
        ],
        in_specs=in_specs,
        out_specs=[VMEM, pl.BlockSpec((1, pack_rows_count, LANES), lambda i: (i, 0, 0))],
        scratch_shapes=[
            pltpu.VMEM((packet, doubled), F32),
            pltpu.VMEM((packet, doubled), F32),
            pltpu.VMEM((doubled, width), BF16),
            pltpu.VMEM((doubled, width), BF16),
            pltpu.VMEM((3, width, width), BF16),
            pltpu.VMEM((width, doubled), BF16),
            pltpu.VMEM((width, doubled), BF16),
            pltpu.VMEM((4, width), F32),
            pltpu.VMEM((1, doubled), F32),
        ],
        input_output_aliases=aliases,
        compiler_params=PARAMS,
        name="network",
    )(*operands)


def add_body(first, other, out):
    out[...] = (first[...].astype(F32) + other[...].astype(F32)).astype(BF16)


def add_pair(first, other):
    return pl.pallas_call(
        add_body,
        out_shape=jax.ShapeDtypeStruct(first.shape, BF16),
        in_specs=[VMEM] * 2,
        out_specs=VMEM,
        compiler_params=PARAMS,
        name="add_pair",
    )(first, other)


def sum_body(copies, parts, out):
    total = parts[0].astype(F32)
    for index in range(1, parts.shape[0]):
        total = total + parts[index].astype(F32)
    total = total.astype(BF16)
    if copies == 0:
        out[...] = total
    for index in range(copies):
        out[index] = total


def sum_parts(parts, copies):
    shape = ((copies,) if copies else ()) + parts.shape[1:]
    return pl.pallas_call(
        functools.partial(sum_body, copies),
        out_shape=jax.ShapeDtypeStruct(shape, BF16),
        in_specs=[VMEM],
        out_specs=VMEM,
        compiler_params=PARAMS,
        name="sum_parts",
    )(parts)


def steps_body(levels, width, count, whole, first, inner, last, bias, bias_last):
    def squares(index, total):
        part = whole[pl.ds(pl.multiple_of(index * 16, 16), 16), :].astype(F32)
        return total + part * part

    total = lax.fori_loop(0, whole.shape[0] // 16, squares, jnp.zeros((16, LANES), F32), unroll=4)
    factor = 1.0 / jnp.sqrt(jnp.broadcast_to(jnp.sum(total), (1, LANES)) / count + 1e-06)
    row = 0

    def take(size):
        nonlocal row
        value = whole[row : row + size, :].astype(F32) * factor
        row += size
        return value

    half = LANES // 2
    for k in range(3):
        inner[k, :, :LANES] = take(width)
    narrow = take(width)
    inner[0, :, LANES:] = narrow[:, :half]
    inner[1, :, LANES:] = swap_halves(narrow)[:, :half]
    narrow = take(width)
    inner[2, :, LANES:] = narrow[:, :half]
    last[...] = swap_halves(narrow)[:, :half]
    first[:, :LANES] = take(levels)
    narrow = take(levels // 2)
    first[: levels // 2, LANES:] = narrow[:, :half]
    first[levels // 2 :, LANES:] = swap_halves(narrow)[:, :half]
    tail = take(16)
    bias[:, :LANES] = tail[0:4]
    for k in (0, 2):
        pair = tail[4 + k // 2 : 5 + k // 2]
        bias[k : k + 1, LANES:] = pair[:, :half]
        bias[k + 1 : k + 2, LANES:] = swap_halves(pair)[:, :half]
    bias_last[...] = swap_halves(tail[6:7])[:, :half]


def make_steps(whole, levels, width):
    count = 2 * levels * width + 3 * width * width + 4 * width + levels
    return pl.pallas_call(
        functools.partial(steps_body, levels, width, float(count)),
        out_shape=[
            jax.ShapeDtypeStruct((levels, width), F32),
            jax.ShapeDtypeStruct((3, width, width), F32),
            jax.ShapeDtypeStruct((width, levels), F32),
            jax.ShapeDtypeStruct((4, width), F32),
            jax.ShapeDtypeStruct((1, levels), F32),
        ],
        in_specs=[VMEM],
        out_specs=[VMEM] * 5,
        compiler_params=PARAMS,
        name="make_steps",
    )(whole)


def collect_body(levels, width_x, width_y, rows, grid, top, bottom, low, high):
    cells = width_x * width_y

    def turn(tile, carry):
        span = pl.ds(pl.multiple_of(tile * LANES, LANES), LANES)
        grid[:, span] = rows[span, :].T[levels:].astype(BF16).astype(F32)
        return carry

    lax.fori_loop(0, cells // LANES, turn, 0, unroll=2)

    lows, highs = [], []
    for group in range(levels // SUBLANES):
        where = slice(group * SUBLANES, (group + 1) * SUBLANES)
        low_value, high_value = compact_edges(
            lambda x: grid[where, x * width_y : (x + 1) * width_y], width_x, width_y
        )
        lows.append(low_value)
        highs.append(high_value)
    low[...] = jnp.concatenate(lows, axis=0).astype(BF16)
    high[...] = jnp.concatenate(highs, axis=0).astype(BF16)
    top[...] = grid[:, : 2 * width_y].astype(BF16)
    bottom[...] = grid[:, cells - 2 * width_y :].astype(BF16)


def collect(rows, sizes):
    levels, width_x, width_y, _, _ = sizes
    cells = width_x * width_y
    return pl.pallas_call(
        functools.partial(collect_body, levels, width_x, width_y),
        out_shape=[
            jax.ShapeDtypeStruct((levels, cells), F32),
            jax.ShapeDtypeStruct((levels, 2 * width_y), BF16),
            jax.ShapeDtypeStruct((levels, 2 * width_y), BF16),
            jax.ShapeDtypeStruct((levels, LANES), BF16),
            jax.ShapeDtypeStruct((levels, LANES), BF16),
        ],
        in_specs=[VMEM],
        out_specs=[VMEM] * 5,
        compiler_params=PARAMS,
        name="collect",
    )(rows)


def adjoint_body(
    levels, width_x, width_y,
    grid, diff, own_low, own_high, diff_own_low, diff_own_high,
    up, down, left, right, up_left, up_right, down_left, down_right,
    diff_up, diff_down, diff_left, diff_right,
    diff_up_left, diff_up_right, diff_down_left, diff_down_right,
    out, wide, flow, e1,
):
    y_tiles = width_y // LANES
    stride = width_x * y_tiles

    def at(x):
        return slice((x + 2) * width_y, (x + 3) * width_y)

    last = pl.ds(levels, SUBLANES)
    for x in range(width_x):
        wide[:, at(x)] = load_wide(diff, x, width_y)
    for k in range(2):
        wide[:, at(k - 2)] = diff_up[last, k * width_y : (k + 1) * width_y]
        wide[:, at(width_x + k)] = diff_down[last, k * width_y : (k + 1) * width_y]
    rate_left = with_corners(
        diff_left[last, :], diff_up_left[last, :], diff_down_left[last, :], width_x
    )
    rate_right = with_corners(
        diff_right[last, :], diff_up_right[last, :], diff_down_right[last, :], width_x
    )

    def pair(value, which):
        return value.astype(F32)[which * SUBLANES : (which + 1) * SUBLANES]

    def step(double, carry):
        where = pl.ds(pl.multiple_of(double * 2 * SUBLANES, 2 * SUBLANES), 2 * SUBLANES)
        packed = [
            ref[where, :]
            for ref in (
                own_low, own_high, up, down, left, right,
                up_left, up_right, down_left, down_right,
            )
        ]
        for which in range(2):
            group = double * 2 + which
            own = groups_at(group)
            (
                own_l, own_h, above, below, at_left, at_right, at_ul, at_ur, at_dl, at_dr
            ) = [pair(value, which) for value in packed]
            side_left = with_corners(at_left, at_ul, at_dl, width_x)
            side_right = with_corners(at_right, at_ur, at_dr, width_x)

            def next_side(side, rate, outer, outer_rate, mine, mine_rate):
                product = side * rate
                return product, side + (
                    around(product)
                    + second(outer) * second(outer_rate)
                    + mine * mine_rate
                    - 4.0 * product
                )

            flow_left, next_left = next_side(
                side_left, rate_left, at_left, diff_left[last, :], own_l, diff_own_low[last, :]
            )
            flow_right, next_right = next_side(
                side_right, rate_right, at_right, diff_right[last, :], own_h, diff_own_high[last, :]
            )

            def value(x):
                if x < 0:
                    return above[:, (x + 2) * width_y : (x + 3) * width_y]
                if x >= width_x:
                    return below[:, (x - width_x) * width_y : (x - width_x + 1) * width_y]
                return grid[own, x * width_y : (x + 1) * width_y]

            for x in range(-2, width_x + 2):
                flow[:, at(x)] = value(x) * wide[:, at(x)]
            for x in range(-1, width_x + 1):
                row = flow[:, at(x)]
                near = flow[:, at(x - 1)] + flow[:, at(x + 1)]
                near = near + beside(row, flow_left, flow_right, x)
                e1[:, at(x)] = value(x) + near - 4.0 * row
            for x in range(-1, width_x + 1):
                flow[:, at(x)] = e1[:, at(x)] * wide[:, at(x)]
            flow_left = next_left * rate_left
            flow_right = next_right * rate_right
            for x in range(width_x):
                row = flow[:, at(x)]
                near = flow[:, at(x - 1)] + flow[:, at(x + 1)]
                near = near + beside(row, flow_left, flow_right, x)
                result = e1[:, at(x)] + near - 4.0 * row
                for y_tile in range(y_tiles):
                    offset = group * (SUBLANES * stride) + row_offset(x, y_tile, y_tiles)
                    out[pl.ds(offset, SUBLANES, stride=stride), :] = result[
                        :, y_tile * LANES : (y_tile + 1) * LANES
                    ]
        return carry

    lax.fori_loop(0, levels // (2 * SUBLANES), step, 0)


def adjoint(grid, diff_rows, own, diff_own, halos, diff_halos, sizes):
    levels, width_x, width_y, _, _ = sizes
    extended = (SUBLANES, (width_x + 4) * width_y)
    return pl.pallas_call(
        functools.partial(adjoint_body, levels, width_x, width_y),
        out_shape=jax.ShapeDtypeStruct((levels * width_x * width_y // LANES, LANES), F32),
        in_specs=[VMEM] * 22,
        out_specs=VMEM,
        scratch_shapes=[pltpu.VMEM(extended, F32)] * 3,
        compiler_params=PARAMS,
        name="adjoint",
    )(grid, diff_rows, *own, *diff_own, *halos, *diff_halos)


def per_device(
    initial, targets, diffusivity, column_order, send_counts,
    w_first, w_inner, w_last, b_inner, b_last,
):
    levels, width_x, width_y = initial.shape
    tiles, subs = lax.axis_size("tile"), lax.axis_size("sub")
    cells = width_x * width_y
    sizes = (levels, width_x, width_y, tiles, subs)
    field_rows = tile_rows(initial)
    target_rows = tile_rows(targets)
    diff_rows = tile_rows(diffusivity[None])
    width = w_first.shape[2]
    half = subs // 2
    parity = lax.rem(lax.axis_index("sub"), 2).reshape(1)
    same_core = [list(range(core, subs, 2)) for core in range(2)]
    partner = [(i, i ^ 1) for i in range(subs)]

    def spread(packs):
        return lax.all_to_all(
            packs, "sub", split_axis=0, concat_axis=0, tiled=True, axis_index_groups=same_core
        )

    top, bottom, low, high = pack_edges(field_rows, diff_rows, levels, width_x, width_y)
    weights = pack_weights(
        w_first[0], w_inner[0], w_last[0], b_inner[0], b_last, tiles, half
    )
    halos = exchange(top, bottom, low, high)
    own_weights = spread(weights)
    other_weights = lax.ppermute(own_weights, "sub", partner)
    cells_of = slot_cells(parity, send_counts[0], column_order[0], sizes)
    rows = forward(field_rows, target_rows, diff_rows, low, high, halos, sizes)
    back, other_grads = network(cells_of, other_weights, rows, None, 0, levels, width, subs)
    partner_grads = lax.ppermute(other_grads, "sub", partner)
    back, own_grads = network(cells_of, own_weights, rows, back, half, levels, width, subs)
    mine = sum_parts(spread(add_pair(own_grads, partner_grads)), 0)
    parts = lax.all_to_all(
        mine.reshape(tiles, -1, LANES), "tile", split_axis=0, concat_axis=0, tiled=True
    )
    whole = lax.all_to_all(
        sum_parts(parts, tiles), "tile", split_axis=0, concat_axis=0, tiled=True
    ).reshape(-1, LANES)
    steps = make_steps(whole, levels, width)
    grid, g_top, g_bottom, g_low, g_high = collect(back, sizes)
    g_halos = exchange(g_top, g_bottom, g_low, g_high)
    result = adjoint(grid, diff_rows, (g_low, g_high), (low, high), g_halos, halos, sizes)
    return (
        untile_rows(result, levels, width_x, width_y),
        steps[0][None], steps[1][None], steps[2][None], steps[3][None], steps[4],
    )


def solution(mesh):
    placed = (
        P(None, "tile", "sub"),
        P(None, "tile", "sub"),
        P("tile", "sub"),
        P(("tile", "sub"), None),
        P(("tile", "sub"), None),
        P("sub", None, None),
        P("sub", None, None, None),
        P("sub", None, None),
        P("sub", None, None),
        P("sub", None),
    )
    return jax.shard_map(
        per_device,
        mesh=mesh,
        in_specs=placed,
        out_specs=(
            P(None, "tile", "sub"),
            P("sub", None, None),
            P("sub", None, None, None),
            P("sub", None, None),
            P("sub", None, None),
            P("sub", None),
        ),
        check_vma=False,
    )
```

```python
import functools
import jax
import jax.numpy as jnp
from jax import lax
from jax.experimental import pallas as pl
from jax.experimental.pallas import tpu as pltpu
from jax.sharding import PartitionSpec as P

LANES = 128
SUBLANES = 8
SECOND = 32
VMEM = pl.BlockSpec(memory_space=pltpu.VMEM)
ANY = pl.BlockSpec(memory_space=pl.ANY)
SMEM = pl.BlockSpec(memory_space=pltpu.SMEM)


def params(mebibytes):
    return pltpu.CompilerParams(vmem_limit_bytes=mebibytes * 1024 * 1024)


def cost(microseconds):
    moved = int(microseconds * 3e6)
    return pl.CostEstimate(flops=0, transcendentals=0, bytes_accessed=moved)


F32 = jnp.float32
BF16 = jnp.bfloat16


def load_all(sources, targets, semaphores, first=0):
    copies = [
        pltpu.make_async_copy(source, target, semaphores.at[first + index])
        for index, (source, target) in enumerate(zip(sources, targets))
    ]
    for copy in copies:
        copy.start()
    return copies


def wait_all(copies):
    for copy in copies:
        copy.wait()


def buffers(operands):
    return [pltpu.VMEM(operand.shape, operand.dtype) for operand in operands]


def tile_rows(cells):
    levels, width_x, width_y = cells.shape
    split = cells.reshape(levels, width_x // SUBLANES, SUBLANES, width_y // LANES, LANES)
    return split.transpose(0, 1, 3, 2, 4).reshape(-1, LANES)


def untile_rows(rows, levels, width_x, width_y):
    split = rows.reshape(levels, width_x // SUBLANES, width_y // LANES, SUBLANES, LANES)
    return split.transpose(0, 1, 3, 2, 4).reshape(levels, width_x, width_y)


def row_offset(x, y_tile, y_tiles):
    return (x // SUBLANES * y_tiles + y_tile) * SUBLANES + x % SUBLANES


def load_row(ref, group, x, width_x, width_y):
    y_tiles = width_y // LANES
    stride = width_x * y_tiles
    base = group * (SUBLANES * stride)
    return jnp.concatenate(
        [
            ref[pl.ds(base + row_offset(x, y_tile, y_tiles), SUBLANES, stride=stride), :]
            for y_tile in range(y_tiles)
        ],
        axis=1,
    )


def load_wide(ref, x, width_y):
    y_tiles = width_y // LANES
    return jnp.concatenate(
        [
            jnp.broadcast_to(ref[pl.ds(row_offset(x, y_tile, y_tiles), 1), :], (SUBLANES, LANES))
            for y_tile in range(y_tiles)
        ],
        axis=1,
    )


def lane_ids(width):
    return lax.broadcasted_iota(jnp.int32, (SUBLANES, width), 1)


def compact_edges(row_of, width_x, width_y):
    lane = lane_ids(LANES)
    low = jnp.zeros((SUBLANES, LANES), F32)
    high = jnp.zeros((SUBLANES, LANES), F32)
    for x in range(width_x):
        row = row_of(x)
        low = jnp.where(lane == 1 + x, row[:, 0:1], low)
        low = jnp.where(lane == SECOND + 1 + x, row[:, 1:2], low)
        high = jnp.where(lane == 1 + x, row[:, width_y - 1 : width_y], high)
        high = jnp.where(lane == SECOND + 1 + x, row[:, width_y - 2 : width_y - 1], high)
    return low, high


def groups_at(group):
    return pl.ds(pl.multiple_of(group * SUBLANES, SUBLANES), SUBLANES)


def pack_body(levels, width_x, width_y, field, diff, top, bottom, low, high):
    def emit(where, row_of):
        for k in range(2):
            top[where, k * width_y : (k + 1) * width_y] = row_of(k)
            bottom[where, k * width_y : (k + 1) * width_y] = row_of(width_x - 2 + k)
        low_value, high_value = compact_edges(row_of, width_x, width_y)
        low[where, :] = low_value
        high[where, :] = high_value

    def step(group, carry):
        emit(groups_at(group), lambda x: load_row(field, group, x, width_x, width_y))
        return carry

    lax.fori_loop(0, levels // SUBLANES, step, 0)
    emit(pl.ds(levels, SUBLANES), lambda x: load_wide(diff, x, width_y))


def pack_edges(field_rows, diff_rows, levels, width_x, width_y):
    tall = levels + SUBLANES
    return pl.pallas_call(
        functools.partial(pack_body, levels, width_x, width_y),
        out_shape=[
            jax.ShapeDtypeStruct((tall, 2 * width_y), F32),
            jax.ShapeDtypeStruct((tall, 2 * width_y), F32),
            jax.ShapeDtypeStruct((tall, LANES), F32),
            jax.ShapeDtypeStruct((tall, LANES), F32),
        ],
        in_specs=[VMEM] * 2,
        out_specs=[VMEM] * 4,
        compiler_params=params(8),
        cost_estimate=cost(2),
        name="pack_edges",
    )(field_rows, diff_rows)


def shifted(array, shift_tile, shift_sub):
    tiles, subs = lax.axis_size("tile"), lax.axis_size("sub")
    if shift_tile == 0:
        return lax.ppermute(array, "sub", [(i, (i + shift_sub) % subs) for i in range(subs)])
    if shift_sub == 0:
        return lax.ppermute(array, "tile", [(i, (i + shift_tile) % tiles) for i in range(tiles)])
    pairs = []
    for t in range(tiles):
        for s in range(subs):
            target = (t + shift_tile) % tiles * subs + (s + shift_sub) % subs
            pairs.append((t * subs + s, target))
    return lax.ppermute(array, ("tile", "sub"), pairs)


def exchange(top, bottom, low, high):
    moves = (
        (bottom, 1, 0), (top, -1, 0), (high, 0, 1), (low, 0, -1),
        (high, 1, 1), (low, 1, -1), (high, -1, 1), (low, -1, -1),
    )
    result = []
    for move in moves:
        result.append(shifted(*move))
    return tuple(result)


def with_corners(side, before, after, width_x):
    lane = lane_ids(LANES)
    value = jnp.where(lane == 0, pltpu.roll(before, LANES - width_x, 1), side)
    return jnp.where(lane == width_x + 1, pltpu.roll(after, width_x, 1), value)


def around(side):
    return pltpu.roll(side, 1, 1) + pltpu.roll(side, LANES - 1, 1)


def second(side):
    return pltpu.roll(side, LANES - SECOND, 1)


def beside(row, left, right, x):
    width = row.shape[1]
    lane = lane_ids(width)
    return jnp.where(lane == 0, left[:, x + 1 : x + 2], pltpu.roll(row, 1, 1)) + jnp.where(
        lane == width - 1, right[:, x + 1 : x + 2], pltpu.roll(row, width - 1, 1)
    )


def forward_body(levels, width_x, width_y, *refs):
    cells = width_x * width_y
    sources, refs = refs[:13], refs[13:]
    rows, rates, rate_sides = refs[:3]
    targets = refs[3:16]
    semaphores, e0, e1, wide, both = refs[16:]
    copies = load_all(sources, targets, semaphores)
    (
        field, target, diff, own_low, own_high, up, down, left, right,
        up_left, up_right, down_left, down_right,
    ) = targets
    wait_all(copies[:1] + copies[2:])

    def at(x):
        return slice((x + 2) * width_y, (x + 3) * width_y)

    def sides(where):
        return (
            with_corners(left[where, :], up_left[where, :], down_left[where, :], width_x),
            with_corners(right[where, :], up_right[where, :], down_right[where, :], width_x),
        )

    last = pl.ds(levels, SUBLANES)
    for x in range(width_x):
        wide[:, at(x)] = load_wide(diff, x, width_y)
    for k in range(2):
        wide[:, at(k - 2)] = up[last, k * width_y : (k + 1) * width_y]
        wide[:, at(width_x + k)] = down[last, k * width_y : (k + 1) * width_y]
    diff_left, diff_right = sides(last)
    rates[...] = wide[...]
    for index, value in enumerate(
        (
            diff_left, diff_right, second(left[last, :]), second(right[last, :]),
            own_low[last, :], own_high[last, :],
        )
    ):
        rate_sides[index * SUBLANES : (index + 1) * SUBLANES, :] = value
    wait_all(copies[1:2])

    def step(group, carry):
        where = groups_at(group)
        for x in range(width_x):
            e0[:, at(x)] = load_row(field, group, x, width_x, width_y)
        for k in range(2):
            e0[:, at(k - 2)] = up[where, k * width_y : (k + 1) * width_y]
            e0[:, at(width_x + k)] = down[where, k * width_y : (k + 1) * width_y]
        side_left, side_right = sides(where)

        def next_side(side, outer, own, coefficient):
            return side + coefficient * (around(side) + second(outer) + own - 4.0 * side)

        next_left = next_side(side_left, left[where, :], own_low[where, :], diff_left)
        next_right = next_side(side_right, right[where, :], own_high[where, :], diff_right)
        for x in range(-1, width_x + 1):
            row = e0[:, at(x)]
            near = e0[:, at(x - 1)] + e0[:, at(x + 1)] + beside(row, side_left, side_right, x)
            e1[:, at(x)] = row + wide[:, at(x)] * (near - 4.0 * row)
        for x in range(width_x):
            row = e1[:, at(x)]
            near = e1[:, at(x - 1)] + e1[:, at(x + 1)] + beside(row, next_left, next_right, x)
            value = row + wide[:, at(x)] * (near - 4.0 * row)
            both[where, x * width_y : (x + 1) * width_y] = value
            both[
                pl.ds(pl.multiple_of(levels + group * SUBLANES, SUBLANES), SUBLANES),
                x * width_y : (x + 1) * width_y,
            ] = value - load_row(target, group, x, width_x, width_y)
        return carry

    lax.fori_loop(0, levels // SUBLANES, step, 0)

    def turn(tile, carry):
        span = pl.ds(pl.multiple_of(tile * LANES, LANES), LANES)
        rows[span, :] = both[:, span].T
        return carry

    lax.fori_loop(0, cells // LANES, turn, 0, unroll=2)


def forward(field_rows, target_rows, diff_rows, own_low, own_high, halos, sizes):
    levels, width_x, width_y, _, _ = sizes
    cells = width_x * width_y
    operands = (field_rows, target_rows, diff_rows, own_low, own_high, *halos)
    extended = (SUBLANES, (width_x + 4) * width_y)
    return pl.pallas_call(
        functools.partial(forward_body, levels, width_x, width_y),
        out_shape=[
            jax.ShapeDtypeStruct((cells, 2 * levels), F32),
            jax.ShapeDtypeStruct(extended, F32),
            jax.ShapeDtypeStruct((6 * SUBLANES, LANES), F32),
        ],
        in_specs=[ANY] * 13,
        out_specs=[VMEM] * 3,
        scratch_shapes=buffers(operands)
        + [
            pltpu.SemaphoreType.DMA((13,)),
            pltpu.VMEM(extended, F32),
            pltpu.VMEM(extended, F32),
            pltpu.VMEM(extended, F32),
            pltpu.VMEM((2 * levels, cells), F32),
        ],
        compiler_params=params(12),
        cost_estimate=cost(8),
        name="forward",
    )(*operands)


def index_body(tiles, subs, lead, rows_each, parity, counts, order, out, starts):
    devices = tiles * subs

    def begin(index, total):
        starts[index] = total
        return total + counts[index]

    lax.fori_loop(0, devices, begin, jnp.int32(0))
    half = subs // 2
    flip = parity[0]
    lane = lax.broadcasted_iota(jnp.int32, (SUBLANES, LANES), 1)
    slot = lax.broadcasted_iota(jnp.int32, (SUBLANES, LANES), 0) * LANES + lane

    def expert(block, carry):
        second_half = block // half
        network_id = (block - second_half * half) * 2 + flip * (1 - second_half) + (1 - flip) * second_half
        value = jnp.zeros((SUBLANES, LANES), jnp.int32)
        base = jnp.int32(0)
        for t in range(tiles):
            device = t * subs + network_id
            count = counts[device]
            offset = starts[device] - base + lead
            shift = lax.rem(offset, LANES)
            window = order[pl.ds(lax.div(offset, LANES), SUBLANES), :]
            turned = pltpu.roll(window, lax.rem(LANES - shift, LANES), 1)
            following = jnp.concatenate([turned[1:], turned[:1]], axis=0)
            moved = jnp.where(lane < LANES - shift, turned, following)
            value = jnp.where((slot >= base) & (slot < base + count), moved, value)
            base = base + count
        out[pl.ds(block * rows_each, rows_each), :] = value[:rows_each]
        return carry

    lax.fori_loop(0, subs, expert, 0)


def slot_cells(parity, counts, column_order, sizes):
    _, width_x, width_y, tiles, subs = sizes
    cells = width_x * width_y
    packet = cells // subs
    rows_each = packet // LANES
    lead = packet
    order = jnp.pad(column_order, (lead, SUBLANES * LANES)).reshape(-1, LANES)
    return pl.pallas_call(
        functools.partial(index_body, tiles, subs, lead, rows_each),
        out_shape=jax.ShapeDtypeStruct((cells // LANES, LANES), jnp.int32),
        in_specs=[SMEM] * 2 + [VMEM],
        out_specs=VMEM,
        scratch_shapes=[pltpu.SMEM((tiles * subs,), jnp.int32)],
        compiler_params=params(4),
        cost_estimate=cost(2),
        name="slot_cells",
    )(parity, counts, order).reshape(subs, 1, packet)


def widen(value):
    missing = LANES - value.shape[1]
    return jnp.concatenate([value, jnp.zeros((value.shape[0], missing), value.dtype)], axis=1)


def lower_half(rows):
    return lax.broadcasted_iota(jnp.int32, (rows, LANES), 1) < LANES // 2


def swap_halves(value):
    return pltpu.roll(value, LANES // 2, 1)


def squeeze_rows(value):
    count = value.shape[0] // 2
    return jnp.where(lower_half(count), value[:count], swap_halves(value[count:]))


def pack_rows(put, inner, first, last, biases):
    width = first.shape[1]
    for k in range(3):
        put(inner[k][:, :LANES])
    low = lower_half(width)
    put(jnp.where(low, widen(inner[0][:, LANES:]), swap_halves(widen(inner[1][:, LANES:]))))
    put(jnp.where(low, widen(inner[2][:, LANES:]), last))
    put(first[:, :LANES])
    put(squeeze_rows(widen(first[:, LANES:])))
    tail = []
    for bias, bias_last in biases:
        tail += [piece[:, :LANES] for piece in bias]
        tail += [
            jnp.where(
                lower_half(1), widen(bias[k][:, LANES:]), swap_halves(widen(bias[k + 1][:, LANES:]))
            )
            for k in (0, 2)
        ]
        tail.append(bias_last)
    return tail


def pack_size(levels, width, tiles):
    rows = 5 * width + levels + levels // 2 + 16
    unit = 16 * tiles
    return (rows + unit - 1) // unit * unit


def weights_body(*refs):
    sources, out, targets, semaphores = refs[:5], refs[5], refs[6:11], refs[11]
    wait_all(load_all(sources, targets, semaphores))
    w_first, w_inner, w_last, b_inner, b_last = targets
    row = 0

    def put(value):
        nonlocal row
        value = value.astype(BF16)
        for copy in range(out.shape[0]):
            out[copy, row : row + value.shape[0], :] = value
        row += value.shape[0]

    bias = b_inner[...]
    bias_last = swap_halves(widen(b_last[...]))
    bias_high = bias.astype(BF16).astype(F32)
    last_high = bias_last.astype(BF16).astype(F32)
    bias_low = bias - bias_high
    last_low = bias_last - last_high
    tail = pack_rows(
        put,
        [w_inner[k].astype(F32) for k in range(3)],
        w_first[...].astype(F32),
        swap_halves(widen(w_last[...].astype(F32).T)),
        [
            ([bias_high[k : k + 1] for k in range(4)], last_high),
            ([bias_low[k : k + 1] for k in range(4)], last_low),
        ],
    )
    tail.append(jnp.zeros((out.shape[1] - row - len(tail), LANES), F32))
    put(jnp.concatenate(tail, axis=0))


def pack_weights(w_first, w_inner, w_last, b_inner, b_last, tiles, copies):
    levels, width = w_first.shape
    operands = (w_first, w_inner, w_last.T, b_inner, b_last)
    return pl.pallas_call(
        weights_body,
        out_shape=jax.ShapeDtypeStruct((copies, pack_size(levels, width, tiles), LANES), BF16),
        in_specs=[ANY] * 5,
        out_specs=VMEM,
        scratch_shapes=buffers(operands) + [pltpu.SemaphoreType.DMA((5,))],
        compiler_params=params(8),
        cost_estimate=cost(1),
        name="pack_weights",
    )(*operands)


def network_body(
    levels, width, packet,
    behind, ahead, packs, rows, back_in, back, grads,
    taken, given_back, first_in, first_out, inner, last, last_half,
    kept, feeds, slopes, residues,
):
    certain = behind[0, 0, 0] >= 0
    block = pl.program_id(0)
    blocks = pl.num_programs(0)
    narrow = width - LANES
    wide = 2 * LANES
    half = packet // 2

    def fetch(cells_of, first_slot, count):
        for u in range(first_slot, first_slot + count):
            taken[u : u + 1, :] = rows[pl.ds(cells_of[0, 0, u], 1), :]

    def deliver(cells_of, first_slot, count):
        for u in range(first_slot, first_slot + count):
            back[pl.ds(cells_of[0, 0, u], 1), :] = given_back[u : u + 1, :]

    @pl.when(block == 0)
    def _():
        fetch(behind, 0, packet)
        first_in[levels:, :] = jnp.zeros((wide - levels, wide), BF16)
        first_out[...] = jnp.zeros((LANES, wide), BF16)
        first_in[:levels, LANES:] = jnp.zeros((levels, LANES), BF16)
        inner[:, :, LANES:] = jnp.zeros((3, wide, LANES), BF16)
        inner[:, width:, :] = jnp.zeros((3, wide - width, wide), BF16)
        last[...] = jnp.zeros((wide, LANES), BF16)
        last_half[...] = jnp.zeros((wide, LANES), BF16)

    row = 0

    def take(size):
        nonlocal row
        value = packs[0, row : row + size, :].astype(F32)
        row += size
        return value

    def halves(value):
        return value[:, :narrow], swap_halves(value)[:, :narrow]

    for k in range(3):
        inner[k, :width, :LANES] = (0.5 * take(width)).astype(BF16)
    narrow_a, narrow_b = halves(0.5 * take(width))
    inner[0, :width, LANES:width] = narrow_a.astype(BF16)
    inner[1, :width, LANES:width] = narrow_b.astype(BF16)
    mixed = take(width)
    inner[2, :width, LANES:width] = (0.5 * mixed[:, :narrow]).astype(BF16)
    out_weight = jnp.where(lower_half(width), 0.0, mixed)
    last[:width, :] = out_weight.astype(BF16)
    last_half[:width, :] = (0.5 * out_weight).astype(BF16)
    wide_first = take(levels)
    narrow_a, narrow_b = halves(take(levels // 2))
    half_levels = levels // 2
    first_in[:levels, :LANES] = (0.5 * wide_first).astype(BF16)
    first_in[:half_levels, LANES:width] = (0.5 * narrow_a).astype(BF16)
    first_in[half_levels:levels, LANES:width] = (0.5 * narrow_b).astype(BF16)
    first_out[levels:, :LANES] = wide_first.astype(BF16)
    first_out[levels : levels + half_levels, LANES:width] = narrow_a.astype(BF16)
    first_out[levels + half_levels :, LANES:width] = narrow_b.astype(BF16)
    tail = take(16)

    def bias_rows(k):
        parts = []
        for base in (0, 7):
            mixed = 0.5 * tail[base + 4 + k // 2 : base + 5 + k // 2]
            side = mixed if k % 2 == 0 else swap_halves(mixed)
            side = jnp.where(lower_half(1), side, 0.0)
            parts.append(jnp.concatenate([0.5 * tail[base + k : base + k + 1], side], axis=1))
        parts.append(jnp.zeros((14, wide), F32))
        return jnp.concatenate(parts, axis=0).astype(BF16)

    first_in[LANES : LANES + 16, :] = bias_rows(0)
    for k in range(3):
        inner[k, width : width + 16, :] = bias_rows(k + 1)
    last[width : width + 16, :] = jnp.concatenate(
        [tail[6:7], tail[13:14], jnp.zeros((14, LANES), F32)], axis=0
    ).astype(BF16)

    over_rows = (((0,), (0,)), ((), ()))
    over_lanes = (((1,), (1,)), ((), ()))
    sides = (0, 1)
    lower = lower_half(half)
    ones = jnp.ones((half, LANES), BF16)

    def span(side):
        return slice(side * half, (side + 1) * half)

    for side in sides:
        kept[span(side), :] = taken[span(side), :].astype(BF16)

    def layers(chosen, current, delivered, share):
        for k in chosen:
            for side in sides:
                weight = first_in[...] if k == 0 else inner[k - 1]
                u = jnp.dot(current[side], weight, preferred_element_type=F32)
                turn = jnp.tanh(u)
                plus = 1.0 + turn
                active = u * plus
                slopes[k, span(side), :] = plus + active * (1.0 - turn)
                current[side] = jnp.concatenate(
                    [active[:, :LANES], jnp.where(lower, active[:, LANES:], 1.0)], axis=1
                ).astype(BF16)
                feeds[k, span(side), :] = current[side]
                deliver(behind, delivered, share)
                delivered += share
        return current

    layers(
        (0, 1), [jnp.concatenate([kept[span(side), :], ones], axis=1) for side in sides], 0, packet // 8
    )

    @pl.when(certain)
    def _():
        current = layers((2, 3), [feeds[1, span(side), :] for side in sides], packet // 2, packet // 8)
        for side in sides:
            output = jnp.dot(current[side], last[...], preferred_element_type=F32)
            residues[span(side), :] = jnp.where(
                lower, 0.0, kept[span(side), :].astype(F32) + output
            )

    @pl.when(certain)
    def _():
        fetched = 0
        share = packet // 10
        errors = [residues[span(side), :].astype(BF16) for side in sides]

        def weight_grad(k):
            products = []
            for side in sides:
                if k == 0:
                    feed = jnp.concatenate([kept[span(side), :], ones], axis=1)[:, : LANES + 16]
                else:
                    feed = feeds[k - 1, span(side), : width + 16]
                products.append(
                    lax.dot_general(feed, errors[side], over_rows, preferred_element_type=F32)
                )
            return products[0] + products[1]

        grad_sums = [None] * 5
        carried = [
            lax.dot_general(errors[side], last_half[...], over_lanes, preferred_element_type=F32)
            for side in sides
        ]
        grad_sums[4] = weight_grad(4)
        for k in (3, 2, 1, 0):
            for side in sides:
                errors[side] = (carried[side] * slopes[k, span(side), :]).astype(BF16)
                weight = inner[k - 1] if k > 0 else first_out[...]
                carried[side] = lax.dot_general(
                    errors[side], weight, over_lanes, preferred_element_type=F32
                )
                fetch(ahead, fetched, share)
                fetched += share
            grad_sums[k] = weight_grad(k)
        fetch(ahead, fetched, packet - fetched)
        for side in sides:
            given_back[span(side), :] = residues[span(side), :] + carried[side]

        filled = 0

        def put(value):
            nonlocal filled
            grads[0, filled : filled + value.shape[0], :] = value.astype(BF16)
            filled += value.shape[0]

        tail = pack_rows(
            put,
            [grad_sums[k][:width, :width] for k in (1, 2, 3)],
            grad_sums[0][:levels, :width],
            grad_sums[4][:width],
            [
                (
                    [grad_sums[0][LANES : LANES + 1, :width]]
                    + [grad_sums[k][width : width + 1, :width] for k in (1, 2, 3)],
                    grad_sums[4][width : width + 1],
                )
            ],
        )
        tail.append(jnp.zeros((grads.shape[1] - filled - len(tail), LANES), F32))
        put(jnp.concatenate(tail, axis=0))

    @pl.when(block == blocks - 1)
    def _():
        deliver(ahead, 0, packet)


def network(cells_of, packs, rows, back, shift, levels, width, subs):
    cells, doubled = rows.shape
    packet = cells // subs
    blocks, pack_rows_count, _ = packs.shape
    body = functools.partial(network_body, levels, width, packet)
    operands = [cells_of, cells_of, packs, rows]
    in_specs = [
        pl.BlockSpec(
            (1, 1, packet), lambda i: (jnp.maximum(i - 1, 0) + shift, 0, 0), memory_space=pltpu.SMEM
        ),
        pl.BlockSpec(
            (1, 1, packet),
            lambda i: (jnp.minimum(i + 1, blocks - 1) + shift, 0, 0),
            memory_space=pltpu.SMEM,
        ),
        pl.BlockSpec((1, pack_rows_count, LANES), lambda i: (i, 0, 0)),
        VMEM,
    ]
    aliases = {}
    if back is None:
        body = lambda a, b, c, d, *rest: network_body(
            levels, width, packet, a, b, c, d, None, *rest
        )
    else:
        operands.append(back)
        in_specs.append(VMEM)
        aliases = {4: 0}
    wide = 2 * LANES
    return pl.pallas_call(
        body,
        grid=(blocks,),
        out_shape=[
            jax.ShapeDtypeStruct((cells, doubled), F32),
            jax.ShapeDtypeStruct(packs.shape, BF16),
        ],
        in_specs=in_specs,
        out_specs=[VMEM, pl.BlockSpec((1, pack_rows_count, LANES), lambda i: (i, 0, 0))],
        scratch_shapes=[
            pltpu.VMEM((packet, doubled), F32),
            pltpu.VMEM((packet, doubled), F32),
            pltpu.VMEM((wide, wide), BF16),
            pltpu.VMEM((LANES, wide), BF16),
            pltpu.VMEM((3, wide, wide), BF16),
            pltpu.VMEM((wide, LANES), BF16),
            pltpu.VMEM((wide, LANES), BF16),
            pltpu.VMEM((packet, LANES), BF16),
            pltpu.VMEM((4, packet, wide), BF16),
            pltpu.VMEM((4, packet, wide), F32),
            pltpu.VMEM((packet, LANES), F32),
        ],
        input_output_aliases=aliases,
        compiler_params=params(24),
        cost_estimate=cost(12),
        name="network",
    )(*operands)


def add_body(first, other, out):
    out[...] = (first[...].astype(F32) + other[...].astype(F32)).astype(BF16)


def add_pair(first, other):
    return pl.pallas_call(
        add_body,
        out_shape=jax.ShapeDtypeStruct(first.shape, BF16),
        in_specs=[VMEM] * 2,
        out_specs=VMEM,
        compiler_params=params(8),
        cost_estimate=cost(1),
        name="add_pair",
    )(first, other)


def sum_body(copies, parts, out):
    total = parts[0].astype(F32)
    for index in range(1, parts.shape[0]):
        total = total + parts[index].astype(F32)
    total = total.astype(BF16)
    if copies == 0:
        out[...] = total
    for index in range(copies):
        out[index] = total


def sum_parts(parts, copies):
    shape = ((copies,) if copies else ()) + parts.shape[1:]
    return pl.pallas_call(
        functools.partial(sum_body, copies),
        out_shape=jax.ShapeDtypeStruct(shape, BF16),
        in_specs=[VMEM],
        out_specs=VMEM,
        compiler_params=params(8),
        cost_estimate=cost(1),
        name="sum_parts",
    )(parts)


def steps_body(levels, width, count, whole, first, inner, last, bias, bias_last):
    def squares(index, total):
        part = whole[pl.ds(pl.multiple_of(index * 16, 16), 16), :].astype(F32)
        return total + part * part

    total = lax.fori_loop(0, whole.shape[0] // 16, squares, jnp.zeros((16, LANES), F32), unroll=4)
    factor = 1.0 / jnp.sqrt(jnp.broadcast_to(jnp.sum(total), (1, LANES)) / count + 1e-06)
    row = 0

    def take(size):
        nonlocal row
        value = whole[row : row + size, :].astype(F32) * factor
        row += size
        return value

    half = LANES // 2
    for k in range(3):
        inner[k, :, :LANES] = take(width)
    narrow = take(width)
    inner[0, :, LANES:] = narrow[:, :half]
    inner[1, :, LANES:] = swap_halves(narrow)[:, :half]
    narrow = take(width)
    inner[2, :, LANES:] = narrow[:, :half]
    last[...] = swap_halves(narrow).T[:half]
    first[:, :LANES] = take(levels)
    narrow = take(levels // 2)
    first[: levels // 2, LANES:] = narrow[:, :half]
    first[levels // 2 :, LANES:] = swap_halves(narrow)[:, :half]
    tail = take(16)
    bias[:, :LANES] = tail[0:4]
    for k in (0, 2):
        pair = tail[4 + k // 2 : 5 + k // 2]
        bias[k : k + 1, LANES:] = pair[:, :half]
        bias[k + 1 : k + 2, LANES:] = swap_halves(pair)[:, :half]
    bias_last[...] = swap_halves(tail[6:7])[:, :half]


def make_steps(whole, levels, width):
    count = 2 * levels * width + 3 * width * width + 4 * width + levels
    return pl.pallas_call(
        functools.partial(steps_body, levels, width, float(count)),
        out_shape=[
            jax.ShapeDtypeStruct((levels, width), F32),
            jax.ShapeDtypeStruct((3, width, width), F32),
            jax.ShapeDtypeStruct((levels, width), F32),
            jax.ShapeDtypeStruct((4, width), F32),
            jax.ShapeDtypeStruct((1, levels), F32),
        ],
        in_specs=[VMEM],
        out_specs=[VMEM] * 5,
        compiler_params=params(8),
        cost_estimate=cost(2),
        name="make_steps",
    )(whole)


def collect_body(levels, width_x, width_y, rows, grid, top, bottom, low, high):
    cells = width_x * width_y

    def turn(tile, carry):
        span = pl.ds(pl.multiple_of(tile * LANES, LANES), LANES)
        grid[:, span] = rows[span, :].T[levels:].astype(BF16).astype(F32)
        return carry

    lax.fori_loop(0, cells // LANES, turn, 0, unroll=2)

    lows, highs = [], []
    for group in range(levels // SUBLANES):
        where = slice(group * SUBLANES, (group + 1) * SUBLANES)
        low_value, high_value = compact_edges(
            lambda x: grid[where, x * width_y : (x + 1) * width_y], width_x, width_y
        )
        lows.append(low_value)
        highs.append(high_value)
    low[...] = jnp.concatenate(lows, axis=0).astype(BF16)
    high[...] = jnp.concatenate(highs, axis=0).astype(BF16)
    top[...] = grid[:, : 2 * width_y].astype(BF16)
    bottom[...] = grid[:, cells - 2 * width_y :].astype(BF16)


def collect(rows, sizes):
    levels, width_x, width_y, _, _ = sizes
    cells = width_x * width_y
    return pl.pallas_call(
        functools.partial(collect_body, levels, width_x, width_y),
        out_shape=[
            jax.ShapeDtypeStruct((levels, cells), F32),
            jax.ShapeDtypeStruct((levels, 2 * width_y), BF16),
            jax.ShapeDtypeStruct((levels, 2 * width_y), BF16),
            jax.ShapeDtypeStruct((levels, LANES), BF16),
            jax.ShapeDtypeStruct((levels, LANES), BF16),
        ],
        in_specs=[VMEM],
        out_specs=[VMEM] * 5,
        compiler_params=params(8),
        cost_estimate=cost(3),
        name="collect",
    )(rows)


def adjoint_body(levels, width_x, width_y, *refs):
    sources, out, targets = refs[:13], refs[13], refs[14:27]
    semaphores, flow, e1 = refs[27:]
    wait_all(load_all(sources, targets, semaphores))
    (
        grid, wide, rate_sides, own_low, own_high, up, down, left, right,
        up_left, up_right, down_left, down_right,
    ) = targets
    y_tiles = width_y // LANES
    stride = width_x * y_tiles

    def at(x):
        return slice((x + 2) * width_y, (x + 3) * width_y)

    rate_left, rate_right, outer_left, outer_right, mine_left, mine_right = [
        rate_sides[index * SUBLANES : (index + 1) * SUBLANES, :] for index in range(6)
    ]

    def pair(value, which):
        return value.astype(F32)[which * SUBLANES : (which + 1) * SUBLANES]

    def step(double, carry):
        where = pl.ds(pl.multiple_of(double * 2 * SUBLANES, 2 * SUBLANES), 2 * SUBLANES)
        packed = [
            ref[where, :]
            for ref in (
                own_low, own_high, up, down, left, right,
                up_left, up_right, down_left, down_right,
            )
        ]
        for which in range(2):
            group = double * 2 + which
            own = groups_at(group)
            (
                own_l, own_h, above, below, at_left, at_right, at_ul, at_ur, at_dl, at_dr
            ) = [pair(value, which) for value in packed]
            side_left = with_corners(at_left, at_ul, at_dl, width_x)
            side_right = with_corners(at_right, at_ur, at_dr, width_x)

            def next_side(side, rate, outer, outer_rate, mine, mine_rate):
                product = side * rate
                return product, side + (
                    around(product)
                    + second(outer) * outer_rate
                    + mine * mine_rate
                    - 4.0 * product
                )

            flow_left, next_left = next_side(
                side_left, rate_left, at_left, outer_left, own_l, mine_left
            )
            flow_right, next_right = next_side(
                side_right, rate_right, at_right, outer_right, own_h, mine_right
            )

            def value(x):
                if x < 0:
                    return above[:, (x + 2) * width_y : (x + 3) * width_y]
                if x >= width_x:
                    return below[:, (x - width_x) * width_y : (x - width_x + 1) * width_y]
                return grid[own, x * width_y : (x + 1) * width_y]

            for x in range(-2, width_x + 2):
                flow[:, at(x)] = value(x) * wide[:, at(x)]
            for x in range(-1, width_x + 1):
                row = flow[:, at(x)]
                near = flow[:, at(x - 1)] + flow[:, at(x + 1)]
                near = near + beside(row, flow_left, flow_right, x)
                e1[:, at(x)] = value(x) + near - 4.0 * row
            for x in range(-1, width_x + 1):
                flow[:, at(x)] = e1[:, at(x)] * wide[:, at(x)]
            flow_left = next_left * rate_left
            flow_right = next_right * rate_right
            for x in range(width_x):
                row = flow[:, at(x)]
                near = flow[:, at(x - 1)] + flow[:, at(x + 1)]
                near = near + beside(row, flow_left, flow_right, x)
                result = e1[:, at(x)] + near - 4.0 * row
                for y_tile in range(y_tiles):
                    offset = group * (SUBLANES * stride) + row_offset(x, y_tile, y_tiles)
                    out[pl.ds(offset, SUBLANES, stride=stride), :] = result[
                        :, y_tile * LANES : (y_tile + 1) * LANES
                    ]
        return carry

    lax.fori_loop(0, levels // (2 * SUBLANES), step, 0)


def adjoint(grid, rates, rate_sides, own, halos, sizes):
    levels, width_x, width_y, _, _ = sizes
    operands = (grid, rates, rate_sides, *own, *halos)
    extended = (SUBLANES, (width_x + 4) * width_y)
    return pl.pallas_call(
        functools.partial(adjoint_body, levels, width_x, width_y),
        out_shape=jax.ShapeDtypeStruct((levels * width_x * width_y // LANES, LANES), F32),
        in_specs=[ANY] * 13,
        out_specs=VMEM,
        scratch_shapes=buffers(operands)
        + [pltpu.SemaphoreType.DMA((13,)), pltpu.VMEM(extended, F32), pltpu.VMEM(extended, F32)],
        compiler_params=params(8),
        cost_estimate=cost(6),
        name="adjoint",
    )(*operands)


def local_program(
    initial, targets, diffusivity, column_order, send_counts,
    w_first, w_inner, w_last, b_inner, b_last,
):
    levels, width_x, width_y = initial.shape
    tiles, subs = lax.axis_size("tile"), lax.axis_size("sub")
    sizes = (levels, width_x, width_y, tiles, subs)
    field_rows = tile_rows(initial)
    target_rows = tile_rows(targets)
    diff_rows = tile_rows(diffusivity[None])
    width = w_first.shape[2]
    half = subs // 2
    parity = lax.rem(lax.axis_index("sub"), 2).reshape(1)
    same_core = [list(range(core, subs, 2)) for core in range(2)]
    partner = [(i, i ^ 1) for i in range(subs)]

    def spread(packs):
        return lax.all_to_all(
            packs, "sub", split_axis=0, concat_axis=0, tiled=True, axis_index_groups=same_core
        )

    def across(parts):
        return lax.all_to_all(parts, "tile", split_axis=0, concat_axis=0, tiled=True)

    def swap(packs):
        return lax.ppermute(packs, "sub", partner)

    top, bottom, low, high = pack_edges(field_rows, diff_rows, levels, width_x, width_y)
    weights = pack_weights(
        w_first[0], w_inner[0], w_last[0], b_inner[0], b_last, tiles, half
    )
    halos = exchange(top, bottom, low, high)
    own_weights = spread(weights)
    other_weights = swap(own_weights)
    cells_of = slot_cells(parity, send_counts[0], column_order[0], sizes)
    rows, rates, rate_sides = forward(field_rows, target_rows, diff_rows, low, high, halos, sizes)
    back, own_grads = network(cells_of, own_weights, rows, None, 0, levels, width, subs)
    back, other_grads = network(
        cells_of, other_weights, rows, back, half, levels, width, subs
    )
    partner_grads = swap(other_grads)
    grid, g_top, g_bottom, g_low, g_high = collect(back, sizes)
    both_grads = add_pair(own_grads, partner_grads)
    spread_grads = spread(both_grads)
    g_halos = exchange(g_top, g_bottom, g_low, g_high)
    mine = sum_parts(spread_grads, 0)
    parts = across(mine.reshape(tiles, -1, LANES))
    result = adjoint(grid, rates, rate_sides, (g_low, g_high), g_halos, sizes)
    summed = sum_parts(parts, tiles)
    whole = across(summed).reshape(-1, LANES)
    steps = make_steps(whole, levels, width)
    return (
        untile_rows(result, levels, width_x, width_y),
        steps[0][None], steps[1][None], steps[2].T[None], steps[3][None], steps[4],
    )


def solution(mesh):
    placed = (
        P(None, "tile", "sub"),
        P(None, "tile", "sub"),
        P("tile", "sub"),
        P(("tile", "sub"), None),
        P(("tile", "sub"), None),
        P("sub", None, None),
        P("sub", None, None, None),
        P("sub", None, None),
        P("sub", None, None),
        P("sub", None),
    )
    return jax.shard_map(
        local_program,
        mesh=mesh,
        in_specs=placed,
        out_specs=(
            P(None, "tile", "sub"),
            P("sub", None, None),
            P("sub", None, None, None),
            P("sub", None, None),
            P("sub", None, None),
            P("sub", None),
        ),
        check_vma=False,
    )
```

```python
import functools
import jax
import jax.numpy as jnp
from jax import lax
from jax.experimental import pallas as pl
from jax.experimental.pallas import tpu as pltpu
from jax.sharding import PartitionSpec as P

LANES = 128
SUBLANES = 8
SECOND = 32
VMEM = pl.BlockSpec(memory_space=pltpu.VMEM)
ANY = pl.BlockSpec(memory_space=pl.ANY)
SMEM = pl.BlockSpec(memory_space=pltpu.SMEM)


def params(mebibytes):
    return pltpu.CompilerParams(vmem_limit_bytes=mebibytes * 1024 * 1024)


def cost(microseconds):
    moved = int(microseconds * 3e6)
    return pl.CostEstimate(flops=0, transcendentals=0, bytes_accessed=moved)


F32 = jnp.float32
BF16 = jnp.bfloat16


def load_all(sources, targets, semaphores, first=0):
    copies = [
        pltpu.make_async_copy(source, target, semaphores.at[first + index])
        for index, (source, target) in enumerate(zip(sources, targets))
    ]
    for copy in copies:
        copy.start()
    return copies


def wait_all(copies):
    for copy in copies:
        copy.wait()


def buffers(operands):
    return [pltpu.VMEM(operand.shape, operand.dtype) for operand in operands]


def tile_rows(cells):
    levels, width_x, width_y = cells.shape
    split = cells.reshape(levels, width_x // SUBLANES, SUBLANES, width_y // LANES, LANES)
    return split.transpose(0, 1, 3, 2, 4).reshape(-1, LANES)


def untile_rows(rows, levels, width_x, width_y):
    split = rows.reshape(levels, width_x // SUBLANES, width_y // LANES, SUBLANES, LANES)
    return split.transpose(0, 1, 3, 2, 4).reshape(levels, width_x, width_y)


def row_offset(x, y_tile, y_tiles):
    return (x // SUBLANES * y_tiles + y_tile) * SUBLANES + x % SUBLANES


def load_row(ref, group, x, width_x, width_y):
    y_tiles = width_y // LANES
    stride = width_x * y_tiles
    base = group * (SUBLANES * stride)
    return jnp.concatenate(
        [
            ref[pl.ds(base + row_offset(x, y_tile, y_tiles), SUBLANES, stride=stride), :]
            for y_tile in range(y_tiles)
        ],
        axis=1,
    )


def load_wide(ref, x, width_y):
    y_tiles = width_y // LANES
    return jnp.concatenate(
        [
            jnp.broadcast_to(ref[pl.ds(row_offset(x, y_tile, y_tiles), 1), :], (SUBLANES, LANES))
            for y_tile in range(y_tiles)
        ],
        axis=1,
    )


def lane_ids(width):
    return lax.broadcasted_iota(jnp.int32, (SUBLANES, width), 1)


def groups_at(group):
    return pl.ds(pl.multiple_of(group * SUBLANES, SUBLANES), SUBLANES)


def pairs_at(double):
    return pl.ds(pl.multiple_of(double * 2 * SUBLANES, 2 * SUBLANES), 2 * SUBLANES)


def two(parts):
    return jnp.concatenate(parts, axis=0).astype(BF16)


def store_rows(where, row_of, width_x, width_y, flag, first, other):
    for k in range(2):
        span = slice(k * width_y, (k + 1) * width_y)
        top = two([row_of(which, k) for which in range(2)])
        bottom = two([row_of(which, width_x - 2 + k) for which in range(2)])
        first[where, span] = jnp.where(flag == 0, bottom.astype(F32), top.astype(F32)).astype(BF16)
        other[where, span] = jnp.where(flag == 0, top.astype(F32), bottom.astype(F32)).astype(BF16)


def store_columns(where, row_of, width_x, width_y, flag, first, other):
    lane = lane_ids(LANES)
    lows, highs = [], []
    for which in range(2):
        low = jnp.zeros((SUBLANES, LANES), F32)
        high = jnp.zeros((SUBLANES, LANES), F32)
        for x in range(-1, width_x + 1):
            row = row_of(which, x)
            low = jnp.where(lane == 1 + x, row[:, 0:1], low)
            high = jnp.where(lane == 1 + x, row[:, width_y - 1 : width_y], high)
            if 0 <= x < width_x:
                low = jnp.where(lane == SECOND + 1 + x, row[:, 1:2], low)
                high = jnp.where(
                    lane == SECOND + 1 + x, row[:, width_y - 2 : width_y - 1], high
                )
        lows.append(low)
        highs.append(high)
    low = jnp.concatenate(lows, axis=0)
    high = jnp.concatenate(highs, axis=0)
    first[where, :] = jnp.where(flag == 0, high, low).astype(BF16)
    other[where, :] = jnp.where(flag == 0, low, high).astype(BF16)


def row_pack_body(levels, width_x, width_y, flags, field, diff, first, other):
    def step(double, carry):
        store_rows(
            pairs_at(double),
            lambda which, x: load_row(field, double * 2 + which, x, width_x, width_y),
            width_x, width_y, flags[0], first, other,
        )
        return carry

    lax.fori_loop(0, levels // (2 * SUBLANES), step, 0)
    store_rows(
        pl.ds(levels, 2 * SUBLANES), lambda which, x: load_wide(diff, x, width_y),
        width_x, width_y, flags[0], first, other,
    )


def pack_rows_out(flags, field_rows, diff_rows, levels, width_x, width_y):
    shape = jax.ShapeDtypeStruct((levels + 2 * SUBLANES, 2 * width_y), BF16)
    return pl.pallas_call(
        functools.partial(row_pack_body, levels, width_x, width_y),
        out_shape=[shape] * 2,
        in_specs=[SMEM] + [VMEM] * 2,
        out_specs=[VMEM] * 2,
        compiler_params=params(8),
        cost_estimate=cost(1),
        name="pack_rows",
    )(flags, field_rows, diff_rows)


def outer_row(flag, first, other, where, which, x, width_x, width_y):
    even, odd = (other, first) if x < 0 else (first, other)
    start = (x + 2 if x < 0 else x - width_x) * width_y
    span = slice(start, start + width_y)
    value = jnp.where(flag == 0, even[where, span].astype(F32), odd[where, span].astype(F32))
    return value[which * SUBLANES : (which + 1) * SUBLANES]


def column_pack_body(levels, width_x, width_y, flags, field, diff, near, far, first, other):
    def step(double, carry):
        where = pairs_at(double)

        def row_of(which, x):
            if 0 <= x < width_x:
                return load_row(field, double * 2 + which, x, width_x, width_y)
            return outer_row(flags[0], near, far, where, which, x, width_x, width_y)

        store_columns(where, row_of, width_x, width_y, flags[1], first, other)
        return carry

    lax.fori_loop(0, levels // (2 * SUBLANES), step, 0)
    last = pl.ds(levels, 2 * SUBLANES)

    def rate_of(which, x):
        if 0 <= x < width_x:
            return load_wide(diff, x, width_y)
        return outer_row(flags[0], near, far, last, which, x, width_x, width_y)

    store_columns(last, rate_of, width_x, width_y, flags[1], first, other)


def pack_columns_out(flags, field_rows, diff_rows, near, far, levels, width_x, width_y):
    shape = jax.ShapeDtypeStruct((levels + 2 * SUBLANES, LANES), BF16)
    return pl.pallas_call(
        functools.partial(column_pack_body, levels, width_x, width_y),
        out_shape=[shape] * 2,
        in_specs=[SMEM] + [VMEM] * 4,
        out_specs=[VMEM] * 2,
        compiler_params=params(8),
        cost_estimate=cost(1),
        name="pack_columns",
    )(flags, field_rows, diff_rows, near, far)


def back_pack_body(levels, width_x, width_y, flags, grid, near, far, first, other):
    def step(double, carry):
        where = pairs_at(double)

        def row_of(which, x):
            if 0 <= x < width_x:
                return grid[groups_at(double * 2 + which), x * width_y : (x + 1) * width_y]
            return outer_row(flags[0], near, far, where, which, x, width_x, width_y)

        store_columns(where, row_of, width_x, width_y, flags[1], first, other)
        return carry

    lax.fori_loop(0, levels // (2 * SUBLANES), step, 0)


def pack_columns_back(flags, grid, near, far, levels, width_x, width_y):
    shape = jax.ShapeDtypeStruct((levels, LANES), BF16)
    return pl.pallas_call(
        functools.partial(back_pack_body, levels, width_x, width_y),
        out_shape=[shape] * 2,
        in_specs=[SMEM] + [VMEM] * 3,
        out_specs=[VMEM] * 2,
        compiler_params=params(8),
        cost_estimate=cost(1),
        name="pack_back",
    )(flags, grid, near, far)


def partners(size, offset):
    return [(i, i ^ offset) for i in range(size)]


def beyond(size):
    return [(i, (i - 1) % size if i % 2 == 0 else (i + 1) % size) for i in range(size)]


def trade_sides(first, other, axis):
    size = lax.axis_size(axis)
    return (lax.ppermute(first, axis, partners(size, 1)), lax.ppermute(other, axis, beyond(size)))


def around(side):
    return pltpu.roll(side, 1, 1) + pltpu.roll(side, LANES - 1, 1)


def second(side):
    return pltpu.roll(side, LANES - SECOND, 1)


def beside(row, left, right, x):
    width = row.shape[1]
    lane = lane_ids(width)
    return jnp.where(lane == 0, left[:, x + 1 : x + 2], pltpu.roll(row, 1, 1)) + jnp.where(
        lane == width - 1, right[:, x + 1 : x + 2], pltpu.roll(row, width - 1, 1)
    )


def split_sides(flag, first, other, where):
    near = first[where, :].astype(F32)
    far = other[where, :].astype(F32)
    return jnp.where(flag == 0, far, near), jnp.where(flag == 0, near, far)


def forward_body(
    levels, width_x, width_y,
    flags, field, target, diff, near, far, own_near, own_far, side_near, side_far,
    rows, rates, rate_sides, e0, e1, wide, both,
):
    cells = width_x * width_y

    def at(x):
        return slice((x + 2) * width_y, (x + 3) * width_y)

    last = pl.ds(levels, 2 * SUBLANES)
    for x in range(width_x):
        wide[:, at(x)] = load_wide(diff, x, width_y)
    for x in (-2, -1, width_x, width_x + 1):
        wide[:, at(x)] = outer_row(flags[0], near, far, last, 0, x, width_x, width_y)
    rates[...] = wide[...]

    diff_left, diff_right = [v[:SUBLANES] for v in split_sides(flags[1], side_near, side_far, last)]
    mine_low, mine_high = [v[:SUBLANES] for v in split_sides(flags[1], own_near, own_far, last)]
    for index, value in enumerate(
        (diff_left, diff_right, second(diff_left), second(diff_right), mine_low, mine_high)
    ):
        rate_sides[index * SUBLANES : (index + 1) * SUBLANES, :] = value

    def step(double, carry):
        where = pairs_at(double)
        sides = split_sides(flags[1], side_near, side_far, where)
        own = split_sides(flags[1], own_near, own_far, where)
        for which in range(2):
            group = double * 2 + which
            part = slice(which * SUBLANES, (which + 1) * SUBLANES)
            for x in range(width_x):
                e0[:, at(x)] = load_row(field, group, x, width_x, width_y)
            for x in (-2, -1, width_x, width_x + 1):
                e0[:, at(x)] = outer_row(flags[0], near, far, where, which, x, width_x, width_y)
            side_left, side_right = sides[0][part], sides[1][part]

            def next_side(side, mine, coefficient):
                return side + coefficient * (around(side) + second(side) + mine - 4.0 * side)

            next_left = next_side(side_left, own[0][part], diff_left)
            next_right = next_side(side_right, own[1][part], diff_right)
            for x in range(-1, width_x + 1):
                row = e0[:, at(x)]
                close = e0[:, at(x - 1)] + e0[:, at(x + 1)] + beside(row, side_left, side_right, x)
                e1[:, at(x)] = row + wide[:, at(x)] * (close - 4.0 * row)
            for x in range(width_x):
                row = e1[:, at(x)]
                close = e1[:, at(x - 1)] + e1[:, at(x + 1)] + beside(row, next_left, next_right, x)
                value = row + wide[:, at(x)] * (close - 4.0 * row)
                span = slice(x * width_y, (x + 1) * width_y)
                both[groups_at(group), span] = value
                both[
                    pl.ds(pl.multiple_of(levels + group * SUBLANES, SUBLANES), SUBLANES), span
                ] = value - load_row(target, group, x, width_x, width_y)
        return carry

    lax.fori_loop(0, levels // (2 * SUBLANES), step, 0)

    def turn(tile, carry):
        span = pl.ds(pl.multiple_of(tile * LANES, LANES), LANES)
        rows[span, :] = both[:, span].T
        return carry

    lax.fori_loop(0, cells // LANES, turn, 0, unroll=2)


def forward(flags, field_rows, target_rows, diff_rows, near, own, sides, sizes):
    levels, width_x, width_y, _, _ = sizes
    cells = width_x * width_y
    extended = (SUBLANES, (width_x + 4) * width_y)
    return pl.pallas_call(
        functools.partial(forward_body, levels, width_x, width_y),
        out_shape=[
            jax.ShapeDtypeStruct((cells, 2 * levels), F32),
            jax.ShapeDtypeStruct(extended, F32),
            jax.ShapeDtypeStruct((6 * SUBLANES, LANES), F32),
        ],
        in_specs=[SMEM] + [VMEM] * 9,
        out_specs=[VMEM] * 3,
        scratch_shapes=[
            pltpu.VMEM(extended, F32),
            pltpu.VMEM(extended, F32),
            pltpu.VMEM(extended, F32),
            pltpu.VMEM((2 * levels, cells), F32),
        ],
        compiler_params=params(8),
        cost_estimate=cost(8),
        name="forward",
    )(flags, field_rows, target_rows, diff_rows, *near, *own, *sides)


def index_body(tiles, subs, lead, rows_each, flags, counts, order, out, starts):
    devices = tiles * subs

    def begin(index, total):
        starts[index] = total
        return total + counts[index]

    lax.fori_loop(0, devices, begin, jnp.int32(0))
    half = subs // 2
    mine = flags[3]
    lane = lax.broadcasted_iota(jnp.int32, (SUBLANES, LANES), 1)
    slot = lax.broadcasted_iota(jnp.int32, (SUBLANES, LANES), 0) * LANES + lane

    def expert(block, carry):
        second_half = block // half
        network_id = mine ^ ((block - second_half * half) * 2 + second_half)
        value = jnp.zeros((SUBLANES, LANES), jnp.int32)
        base = jnp.int32(0)
        for t in range(tiles):
            device = t * subs + network_id
            count = counts[device]
            offset = starts[device] - base + lead
            shift = lax.rem(offset, LANES)
            window = order[pl.ds(lax.div(offset, LANES), SUBLANES), :]
            turned = pltpu.roll(window, lax.rem(LANES - shift, LANES), 1)
            following = jnp.concatenate([turned[1:], turned[:1]], axis=0)
            moved = jnp.where(lane < LANES - shift, turned, following)
            value = jnp.where((slot >= base) & (slot < base + count), moved, value)
            base = base + count
        out[pl.ds(block * rows_each, rows_each), :] = value[:rows_each]
        return carry

    lax.fori_loop(0, subs, expert, 0)


def slot_cells(flags, counts, column_order, sizes):
    _, width_x, width_y, tiles, subs = sizes
    cells = width_x * width_y
    packet = cells // subs
    rows_each = packet // LANES
    lead = packet
    order = jnp.pad(column_order, (lead, SUBLANES * LANES)).reshape(-1, LANES)
    return pl.pallas_call(
        functools.partial(index_body, tiles, subs, lead, rows_each),
        out_shape=jax.ShapeDtypeStruct((cells // LANES, LANES), jnp.int32),
        in_specs=[SMEM] * 2 + [VMEM],
        out_specs=VMEM,
        scratch_shapes=[pltpu.SMEM((tiles * subs,), jnp.int32)],
        compiler_params=params(4),
        cost_estimate=cost(2),
        name="slot_cells",
    )(flags, counts, order).reshape(subs, 1, packet)


def widen(value):
    missing = LANES - value.shape[1]
    return jnp.concatenate([value, jnp.zeros((value.shape[0], missing), value.dtype)], axis=1)


def lower_half(rows):
    return lax.broadcasted_iota(jnp.int32, (rows, LANES), 1) < LANES // 2


def swap_halves(value):
    return pltpu.roll(value, LANES // 2, 1)


def squeeze_rows(value):
    count = value.shape[0] // 2
    return jnp.where(lower_half(count), value[:count], swap_halves(value[count:]))


def pack_rows(put, inner, first, last, biases):
    width = first.shape[1]
    for k in range(3):
        put(inner[k][:, :LANES])
    low = lower_half(width)
    put(jnp.where(low, widen(inner[0][:, LANES:]), swap_halves(widen(inner[1][:, LANES:]))))
    put(jnp.where(low, widen(inner[2][:, LANES:]), last))
    put(first[:, :LANES])
    put(squeeze_rows(widen(first[:, LANES:])))
    tail = []
    for bias, bias_last in biases:
        tail += [piece[:, :LANES] for piece in bias]
        tail += [
            jnp.where(
                lower_half(1), widen(bias[k][:, LANES:]), swap_halves(widen(bias[k + 1][:, LANES:]))
            )
            for k in (0, 2)
        ]
        tail.append(bias_last)
    return tail


def pack_size(levels, width, tiles):
    rows = 5 * width + levels + levels // 2 + 16
    unit = 16 * tiles
    return (rows + unit - 1) // unit * unit


def weights_body(*refs):
    sources, out, targets, semaphores = refs[:5], refs[5], refs[6:11], refs[11]
    wait_all(load_all(sources, targets, semaphores))
    w_first, w_inner, w_last, b_inner, b_last = targets
    row = 0

    def put(value):
        nonlocal row
        out[row : row + value.shape[0], :] = value.astype(BF16)
        row += value.shape[0]

    bias = b_inner[...]
    bias_last = swap_halves(widen(b_last[...]))
    bias_high = bias.astype(BF16).astype(F32)
    last_high = bias_last.astype(BF16).astype(F32)
    bias_low = bias - bias_high
    last_low = bias_last - last_high
    tail = pack_rows(
        put,
        [w_inner[k].astype(F32) for k in range(3)],
        w_first[...].astype(F32),
        swap_halves(widen(w_last[...].astype(F32).T)),
        [
            ([bias_high[k : k + 1] for k in range(4)], last_high),
            ([bias_low[k : k + 1] for k in range(4)], last_low),
        ],
    )
    tail.append(jnp.zeros((out.shape[0] - row - len(tail), LANES), F32))
    put(jnp.concatenate(tail, axis=0))


def pack_weights(w_first, w_inner, w_last, b_inner, b_last, tiles):
    levels, width = w_first.shape
    operands = (w_first, w_inner, w_last.T, b_inner, b_last)
    return pl.pallas_call(
        weights_body,
        out_shape=jax.ShapeDtypeStruct((pack_size(levels, width, tiles), LANES), BF16),
        in_specs=[pl.BlockSpec(memory_space=pltpu.HBM)] * 5,
        out_specs=VMEM,
        scratch_shapes=buffers(operands) + [pltpu.SemaphoreType.DMA((5,))],
        compiler_params=params(8),
        cost_estimate=cost(1),
        name="pack_weights",
    )(*operands)


def network_body(
    levels, width, packet,
    behind, ahead, pack_list, rows, back, grads, packs,
    taken, given_back, first_in, first_out, inner, last, last_half,
    kept, feeds, slopes, residues,
):
    certain = behind[0, 0, 0] >= 0
    block = pl.program_id(0)
    blocks = pl.num_programs(0)
    narrow = width - LANES
    wide = 2 * LANES
    half = packet // 2

    def fetch(cells_of, first_slot, count):
        for u in range(first_slot, first_slot + count):
            taken[u : u + 1, :] = rows[pl.ds(cells_of[0, 0, u], 1), :]

    def deliver(cells_of, first_slot, count):
        for u in range(first_slot, first_slot + count):
            back[pl.ds(cells_of[0, 0, u], 1), :] = given_back[u : u + 1, :]

    @pl.when(block == 0)
    def _():
        fetch(behind, 0, packet)
        first_in[levels:, :] = jnp.zeros((wide - levels, wide), BF16)
        first_out[...] = jnp.zeros((LANES, wide), BF16)
        first_in[:levels, LANES:] = jnp.zeros((levels, LANES), BF16)
        inner[:, :, LANES:] = jnp.zeros((3, wide, LANES), BF16)
        inner[:, width:, :] = jnp.zeros((3, wide - width, wide), BF16)
        last[...] = jnp.zeros((wide, LANES), BF16)
        last_half[...] = jnp.zeros((wide, LANES), BF16)

    for index, source in enumerate(pack_list):

        @pl.when(block == index)
        def _():
            packs[...] = source[...]

    row = 0

    def take(size):
        nonlocal row
        value = packs[row : row + size, :].astype(F32)
        row += size
        return value

    def halves(value):
        return value[:, :narrow], swap_halves(value)[:, :narrow]

    for k in range(3):
        inner[k, :width, :LANES] = (0.5 * take(width)).astype(BF16)
    narrow_a, narrow_b = halves(0.5 * take(width))
    inner[0, :width, LANES:width] = narrow_a.astype(BF16)
    inner[1, :width, LANES:width] = narrow_b.astype(BF16)
    mixed = take(width)
    inner[2, :width, LANES:width] = (0.5 * mixed[:, :narrow]).astype(BF16)
    out_weight = jnp.where(lower_half(width), 0.0, mixed)
    last[:width, :] = out_weight.astype(BF16)
    last_half[:width, :] = (0.5 * out_weight).astype(BF16)
    wide_first = take(levels)
    narrow_a, narrow_b = halves(take(levels // 2))
    half_levels = levels // 2
    first_in[:levels, :LANES] = (0.5 * wide_first).astype(BF16)
    first_in[:half_levels, LANES:width] = (0.5 * narrow_a).astype(BF16)
    first_in[half_levels:levels, LANES:width] = (0.5 * narrow_b).astype(BF16)
    first_out[levels:, :LANES] = wide_first.astype(BF16)
    first_out[levels : levels + half_levels, LANES:width] = narrow_a.astype(BF16)
    first_out[levels + half_levels :, LANES:width] = narrow_b.astype(BF16)
    tail = take(16)

    def bias_rows(k):
        parts = []
        for base in (0, 7):
            mixed = 0.5 * tail[base + 4 + k // 2 : base + 5 + k // 2]
            side = mixed if k % 2 == 0 else swap_halves(mixed)
            side = jnp.where(lower_half(1), side, 0.0)
            parts.append(jnp.concatenate([0.5 * tail[base + k : base + k + 1], side], axis=1))
        parts.append(jnp.zeros((14, wide), F32))
        return jnp.concatenate(parts, axis=0).astype(BF16)

    first_in[LANES : LANES + 16, :] = bias_rows(0)
    for k in range(3):
        inner[k, width : width + 16, :] = bias_rows(k + 1)
    last[width : width + 16, :] = jnp.concatenate(
        [tail[6:7], tail[13:14], jnp.zeros((14, LANES), F32)], axis=0
    ).astype(BF16)

    over_rows = (((0,), (0,)), ((), ()))
    over_lanes = (((1,), (1,)), ((), ()))
    sides = (0, 1)
    lower = lower_half(half)
    ones = jnp.ones((half, LANES), BF16)

    def span(side):
        return slice(side * half, (side + 1) * half)

    for side in sides:
        kept[span(side), :] = taken[span(side), :].astype(BF16)

    def layers(chosen, current, delivered, share):
        for k in chosen:
            for side in sides:
                weight = first_in[...] if k == 0 else inner[k - 1]
                u = jnp.dot(current[side], weight, preferred_element_type=F32)
                turn = jnp.tanh(u)
                plus = 1.0 + turn
                active = u * plus
                slopes[k, span(side), :] = plus + active * (1.0 - turn)
                current[side] = jnp.concatenate(
                    [active[:, :LANES], jnp.where(lower, active[:, LANES:], 1.0)], axis=1
                ).astype(BF16)
                feeds[k, span(side), :] = current[side]
                deliver(behind, delivered, share)
                delivered += share
        return current

    layers(
        (0, 1), [jnp.concatenate([kept[span(side), :], ones], axis=1) for side in sides], 0, packet // 8
    )

    @pl.when(certain)
    def _():
        current = layers((2, 3), [feeds[1, span(side), :] for side in sides], packet // 2, packet // 8)
        for side in sides:
            output = jnp.dot(current[side], last[...], preferred_element_type=F32)
            residues[span(side), :] = jnp.where(
                lower, 0.0, kept[span(side), :].astype(F32) + output
            )

    @pl.when(certain)
    def _():
        fetched = 0
        share = packet // 10
        errors = [residues[span(side), :].astype(BF16) for side in sides]

        def weight_grad(k):
            products = []
            for side in sides:
                if k == 0:
                    feed = jnp.concatenate([kept[span(side), :], ones], axis=1)[:, : LANES + 16]
                else:
                    feed = feeds[k - 1, span(side), : width + 16]
                products.append(
                    lax.dot_general(feed, errors[side], over_rows, preferred_element_type=F32)
                )
            return products[0] + products[1]

        grad_sums = [None] * 5
        carried = [
            lax.dot_general(errors[side], last_half[...], over_lanes, preferred_element_type=F32)
            for side in sides
        ]
        grad_sums[4] = weight_grad(4)
        for k in (3, 2, 1, 0):
            for side in sides:
                errors[side] = (carried[side] * slopes[k, span(side), :]).astype(BF16)
                weight = inner[k - 1] if k > 0 else first_out[...]
                carried[side] = lax.dot_general(
                    errors[side], weight, over_lanes, preferred_element_type=F32
                )
                fetch(ahead, fetched, share)
                fetched += share
            grad_sums[k] = weight_grad(k)
        fetch(ahead, fetched, packet - fetched)
        for side in sides:
            given_back[span(side), :] = residues[span(side), :] + carried[side]

        filled = 0

        def put(value):
            nonlocal filled
            grads[0, filled : filled + value.shape[0], :] = value.astype(BF16)
            filled += value.shape[0]

        tail = pack_rows(
            put,
            [grad_sums[k][:width, :width] for k in (1, 2, 3)],
            grad_sums[0][:levels, :width],
            grad_sums[4][:width],
            [
                (
                    [grad_sums[0][LANES : LANES + 1, :width]]
                    + [grad_sums[k][width : width + 1, :width] for k in (1, 2, 3)],
                    grad_sums[4][width : width + 1],
                )
            ],
        )
        tail.append(jnp.zeros((grads.shape[1] - filled - len(tail), LANES), F32))
        put(jnp.concatenate(tail, axis=0))

    @pl.when(block == blocks - 1)
    def _():
        deliver(ahead, 0, packet)


def network(cells_of, pack_list, rows, back, shift, levels, width, subs):
    cells, doubled = rows.shape
    packet = cells // subs
    blocks = len(pack_list)
    pack_shape = pack_list[0].shape

    def body(behind, ahead, *refs):
        names = refs[:blocks]
        rest = refs[blocks + 1 + (back is not None) :]
        network_body(levels, width, packet, behind, ahead, names, refs[blocks], *rest)

    operands = [cells_of, cells_of, *pack_list, rows]
    in_specs = [
        pl.BlockSpec(
            (1, 1, packet), lambda i: (jnp.maximum(i - 1, 0) + shift, 0, 0), memory_space=pltpu.SMEM
        ),
        pl.BlockSpec(
            (1, 1, packet),
            lambda i: (jnp.minimum(i + 1, blocks - 1) + shift, 0, 0),
            memory_space=pltpu.SMEM,
        ),
    ] + [VMEM] * (blocks + 1)
    aliases = {}
    if back is not None:
        aliases = {len(operands): 0}
        operands.append(back)
        in_specs.append(VMEM)
    wide = 2 * LANES
    return pl.pallas_call(
        body,
        grid=(blocks,),
        out_shape=[
            jax.ShapeDtypeStruct((cells, doubled), F32),
            jax.ShapeDtypeStruct((blocks, *pack_shape), BF16),
        ],
        in_specs=in_specs,
        out_specs=[VMEM, pl.BlockSpec((1, *pack_shape), lambda i: (i, 0, 0))],
        scratch_shapes=[
            pltpu.VMEM(pack_shape, BF16),
            pltpu.VMEM((packet, doubled), F32),
            pltpu.VMEM((packet, doubled), F32),
            pltpu.VMEM((wide, wide), BF16),
            pltpu.VMEM((LANES, wide), BF16),
            pltpu.VMEM((3, wide, wide), BF16),
            pltpu.VMEM((wide, LANES), BF16),
            pltpu.VMEM((wide, LANES), BF16),
            pltpu.VMEM((packet, LANES), BF16),
            pltpu.VMEM((4, packet, wide), BF16),
            pltpu.VMEM((4, packet, wide), F32),
            pltpu.VMEM((packet, LANES), F32),
        ],
        input_output_aliases=aliases,
        compiler_params=params(24),
        cost_estimate=cost(12),
        name="network",
    )(*operands)


def add_body(first, other, *outs):
    for index, out in enumerate(outs):
        out[...] = (first[index].astype(F32) + other[index].astype(F32)).astype(BF16)


def add_pair(first, other):
    return pl.pallas_call(
        add_body,
        out_shape=[jax.ShapeDtypeStruct(first.shape[1:], BF16)] * first.shape[0],
        in_specs=[VMEM] * 2,
        out_specs=[VMEM] * first.shape[0],
        compiler_params=params(8),
        cost_estimate=cost(1),
        name="add_pair",
    )(first, other)


def total_of(parts):
    total = parts[0][...].astype(F32)
    for part in parts[1:]:
        total = total + part[...].astype(F32)
    return total.astype(BF16)


def share_body(count, flags, *refs):
    parts, outs, whole = refs[:count], refs[count:-1], refs[-1]
    whole[...] = total_of(parts).astype(F32)
    rows = outs[0].shape[0]
    for offset, out in enumerate(outs):
        start = pl.multiple_of((flags[2] ^ offset) * rows, 16)
        out[...] = whole[pl.ds(start, rows), :].astype(BF16)


def sum_and_share(flags, parts, tiles):
    rows = parts[0].shape[0]
    return pl.pallas_call(
        functools.partial(share_body, len(parts)),
        out_shape=[jax.ShapeDtypeStruct((rows // tiles, LANES), BF16)] * tiles,
        in_specs=[SMEM] + [VMEM] * len(parts),
        out_specs=[VMEM] * tiles,
        scratch_shapes=[pltpu.VMEM((rows, LANES), F32)],
        compiler_params=params(8),
        cost_estimate=cost(1),
        name="sum_and_share",
    )(flags, *parts)


def sum_body(*refs):
    refs[-1][...] = total_of(refs[:-1])


def sum_parts(parts):
    return pl.pallas_call(
        sum_body,
        out_shape=jax.ShapeDtypeStruct(parts[0].shape, BF16),
        in_specs=[VMEM] * len(parts),
        out_specs=VMEM,
        compiler_params=params(8),
        cost_estimate=cost(1),
        name="sum_parts",
    )(*parts)


def steps_body(levels, width, count, tiles, flags, *refs):
    parts, (first, inner, last, bias, bias_last, whole) = refs[:tiles], refs[tiles:]
    share = parts[0].shape[0]
    for offset, part in enumerate(parts):
        whole[pl.ds(pl.multiple_of((flags[2] ^ offset) * share, 16), share), :] = part[...]

    def squares(index, total):
        part = whole[pl.ds(pl.multiple_of(index * 16, 16), 16), :].astype(F32)
        return total + part * part

    total = lax.fori_loop(0, whole.shape[0] // 16, squares, jnp.zeros((16, LANES), F32), unroll=4)
    factor = 1.0 / jnp.sqrt(jnp.broadcast_to(jnp.sum(total), (1, LANES)) / count + 1e-06)
    row = 0

    def take(size):
        nonlocal row
        value = whole[row : row + size, :].astype(F32) * factor
        row += size
        return value

    half = LANES // 2
    for k in range(3):
        inner[k, :, :LANES] = take(width)
    narrow = take(width)
    inner[0, :, LANES:] = narrow[:, :half]
    inner[1, :, LANES:] = swap_halves(narrow)[:, :half]
    narrow = take(width)
    inner[2, :, LANES:] = narrow[:, :half]
    last[...] = swap_halves(narrow).T[:half]
    first[:, :LANES] = take(levels)
    narrow = take(levels // 2)
    first[: levels // 2, LANES:] = narrow[:, :half]
    first[levels // 2 :, LANES:] = swap_halves(narrow)[:, :half]
    tail = take(16)
    bias[:, :LANES] = tail[0:4]
    for k in (0, 2):
        pair = tail[4 + k // 2 : 5 + k // 2]
        bias[k : k + 1, LANES:] = pair[:, :half]
        bias[k + 1 : k + 2, LANES:] = swap_halves(pair)[:, :half]
    bias_last[...] = swap_halves(tail[6:7])[:, :half]


def make_steps(flags, parts, levels, width):
    count = 2 * levels * width + 3 * width * width + 4 * width + levels
    return pl.pallas_call(
        functools.partial(steps_body, levels, width, float(count), len(parts)),
        out_shape=[
            jax.ShapeDtypeStruct((levels, width), F32),
            jax.ShapeDtypeStruct((3, width, width), F32),
            jax.ShapeDtypeStruct((levels, width), F32),
            jax.ShapeDtypeStruct((4, width), F32),
            jax.ShapeDtypeStruct((1, levels), F32),
        ],
        in_specs=[SMEM] + [VMEM] * len(parts),
        out_specs=[VMEM] * 5,
        scratch_shapes=[pltpu.VMEM((len(parts) * parts[0].shape[0], LANES), BF16)],
        compiler_params=params(8),
        cost_estimate=cost(2),
        name="make_steps",
    )(flags, *parts)


def collect_body(levels, width_x, width_y, flags, rows, grid, first, other):
    cells = width_x * width_y

    def turn(tile, carry):
        span = pl.ds(pl.multiple_of(tile * LANES, LANES), LANES)
        grid[:, span] = rows[span, :].T[levels:].astype(BF16).astype(F32)
        return carry

    lax.fori_loop(0, cells // LANES, turn, 0, unroll=2)

    def step(double, carry):
        store_rows(
            pairs_at(double),
            lambda which, x: grid[groups_at(double * 2 + which), x * width_y : (x + 1) * width_y],
            width_x, width_y, flags[0], first, other,
        )
        return carry

    lax.fori_loop(0, levels // (2 * SUBLANES), step, 0)


def collect(flags, rows, sizes):
    levels, width_x, width_y, _, _ = sizes
    cells = width_x * width_y
    shape = jax.ShapeDtypeStruct((levels, 2 * width_y), BF16)
    return pl.pallas_call(
        functools.partial(collect_body, levels, width_x, width_y),
        out_shape=[jax.ShapeDtypeStruct((levels, cells), F32), shape, shape],
        in_specs=[SMEM, VMEM],
        out_specs=[VMEM] * 3,
        compiler_params=params(8),
        cost_estimate=cost(3),
        name="collect",
    )(flags, rows)


def adjoint_body(
    levels, width_x, width_y,
    flags, grid, wide, rate_sides, near, far, own_near, own_far, side_near, side_far, out, flow, e1,
):
    y_tiles = width_y // LANES
    stride = width_x * y_tiles

    def at(x):
        return slice((x + 2) * width_y, (x + 3) * width_y)

    rate_left, rate_right, outer_left, outer_right, mine_left, mine_right = [
        rate_sides[index * SUBLANES : (index + 1) * SUBLANES, :] for index in range(6)
    ]

    def step(double, carry):
        where = pairs_at(double)
        sides = split_sides(flags[1], side_near, side_far, where)
        owns = split_sides(flags[1], own_near, own_far, where)
        for which in range(2):
            group = double * 2 + which
            own = groups_at(group)
            part = slice(which * SUBLANES, (which + 1) * SUBLANES)

            def next_side(side, rate, outer_rate, mine, mine_rate):
                product = side * rate
                return product, side + (
                    around(product) + second(side) * outer_rate + mine * mine_rate - 4.0 * product
                )

            flow_left, next_left = next_side(
                sides[0][part], rate_left, outer_left, owns[0][part], mine_left
            )
            flow_right, next_right = next_side(
                sides[1][part], rate_right, outer_right, owns[1][part], mine_right
            )

            def value(x):
                if 0 <= x < width_x:
                    return grid[own, x * width_y : (x + 1) * width_y]
                return outer_row(flags[0], near, far, where, which, x, width_x, width_y)

            for x in range(-2, width_x + 2):
                flow[:, at(x)] = value(x) * wide[:, at(x)]
            for x in range(-1, width_x + 1):
                row = flow[:, at(x)]
                close = flow[:, at(x - 1)] + flow[:, at(x + 1)]
                close = close + beside(row, flow_left, flow_right, x)
                e1[:, at(x)] = value(x) + close - 4.0 * row
            for x in range(-1, width_x + 1):
                flow[:, at(x)] = e1[:, at(x)] * wide[:, at(x)]
            flow_left = next_left * rate_left
            flow_right = next_right * rate_right
            for x in range(width_x):
                row = flow[:, at(x)]
                close = flow[:, at(x - 1)] + flow[:, at(x + 1)]
                close = close + beside(row, flow_left, flow_right, x)
                result = e1[:, at(x)] + close - 4.0 * row
                for y_tile in range(y_tiles):
                    offset = group * (SUBLANES * stride) + row_offset(x, y_tile, y_tiles)
                    out[pl.ds(offset, SUBLANES, stride=stride), :] = result[
                        :, y_tile * LANES : (y_tile + 1) * LANES
                    ]
        return carry

    lax.fori_loop(0, levels // (2 * SUBLANES), step, 0)


def adjoint(flags, grid, rates, rate_sides, near, own, sides, sizes):
    levels, width_x, width_y, _, _ = sizes
    extended = (SUBLANES, (width_x + 4) * width_y)
    return pl.pallas_call(
        functools.partial(adjoint_body, levels, width_x, width_y),
        out_shape=jax.ShapeDtypeStruct((levels * width_x * width_y // LANES, LANES), F32),
        in_specs=[SMEM] + [VMEM] * 9,
        out_specs=VMEM,
        scratch_shapes=[pltpu.VMEM(extended, F32), pltpu.VMEM(extended, F32)],
        compiler_params=params(8),
        cost_estimate=cost(6),
        name="adjoint",
    )(flags, grid, rates, rate_sides, *near, *own, *sides)


def local_program(
    initial, targets, diffusivity, column_order, send_counts,
    w_first, w_inner, w_last, b_inner, b_last,
):
    levels, width_x, width_y = initial.shape
    tiles, subs = lax.axis_size("tile"), lax.axis_size("sub")
    sizes = (levels, width_x, width_y, tiles, subs)
    field_rows = tile_rows(initial)
    target_rows = tile_rows(targets)
    diff_rows = tile_rows(diffusivity[None])
    width = w_first.shape[2]
    half = subs // 2
    tile_id, sub_id = lax.axis_index("tile"), lax.axis_index("sub")
    flags = jnp.stack([tile_id % 2, sub_id % 2, tile_id, sub_id]).astype(jnp.int32)
    area = (levels, width_x, width_y)

    first, other = pack_rows_out(flags, field_rows, diff_rows, *area)
    near = trade_sides(first, other, "tile")
    weights = pack_weights(w_first[0], w_inner[0], w_last[0], b_inner[0], b_last, tiles)
    own_weights = [weights] + [
        lax.ppermute(weights, "sub", partners(subs, 2 * c)) for c in range(1, half)
    ]
    own = pack_columns_out(flags, field_rows, diff_rows, *near, *area)
    sides = trade_sides(*own, "sub")
    cells_of = slot_cells(flags, send_counts[0], column_order[0], sizes)
    rows, rates, rate_sides = forward(
        flags, field_rows, target_rows, diff_rows, near, own, sides, sizes
    )
    other_weights = [lax.ppermute(pack, "sub", partners(subs, 1)) for pack in own_weights]
    back, own_grads = network(cells_of, own_weights, rows, None, 0, levels, width, subs)
    back, other_grads = network(cells_of, other_weights, rows, back, half, levels, width, subs)
    partner_grads = lax.ppermute(other_grads, "sub", partners(subs, 1))
    grid, g_first, g_other = collect(flags, back, sizes)
    g_near = trade_sides(g_first, g_other, "tile")
    both_grads = add_pair(own_grads, partner_grads)
    arrived = [both_grads[0]] + [
        lax.ppermute(both_grads[c], "sub", partners(subs, 2 * c)) for c in range(1, half)
    ]
    g_own = pack_columns_back(flags, grid, *g_near, *area)
    g_sides = trade_sides(*g_own, "sub")
    result = adjoint(flags, grid, rates, rate_sides, g_near, g_own, g_sides, sizes)
    shares = sum_and_share(flags, arrived, tiles)
    mine = [shares[0]] + [
        lax.ppermute(shares[d], "tile", partners(tiles, d)) for d in range(1, tiles)
    ]
    piece = sum_parts(mine)
    pieces = [piece] + [lax.ppermute(piece, "tile", partners(tiles, d)) for d in range(1, tiles)]
    steps = make_steps(flags, pieces, levels, width)
    return (
        untile_rows(result, levels, width_x, width_y),
        steps[0][None], steps[1][None], steps[2].T[None], steps[3][None], steps[4],
    )


def solution(mesh):
    placed = (
        P(None, "tile", "sub"),
        P(None, "tile", "sub"),
        P("tile", "sub"),
        P(("tile", "sub"), None),
        P(("tile", "sub"), None),
        P("sub", None, None),
        P("sub", None, None, None),
        P("sub", None, None),
        P("sub", None, None),
        P("sub", None),
    )
    return jax.shard_map(
        local_program,
        mesh=mesh,
        in_specs=placed,
        out_specs=(
            P(None, "tile", "sub"),
            P("sub", None, None),
            P("sub", None, None, None),
            P("sub", None, None),
            P("sub", None, None),
            P("sub", None),
        ),
        check_vma=False,
    )
```

```python
import functools
import jax
import jax.numpy as jnp
from jax import lax
from jax.experimental import pallas as pl
from jax.experimental.pallas import tpu as pltpu
from jax.sharding import PartitionSpec as P

LANES = 128
SUBLANES = 8
SECOND = 32
VMEM = pl.BlockSpec(memory_space=pltpu.VMEM)
ANY = pl.BlockSpec(memory_space=pl.ANY)
SMEM = pl.BlockSpec(memory_space=pltpu.SMEM)


def params(mebibytes):
    return pltpu.CompilerParams(vmem_limit_bytes=mebibytes * 1024 * 1024)


def cost(microseconds):
    moved = int(microseconds * 3e6)
    return pl.CostEstimate(flops=0, transcendentals=0, bytes_accessed=moved)


F32 = jnp.float32
BF16 = jnp.bfloat16


def load_all(sources, targets, semaphores, first=0):
    copies = [
        pltpu.make_async_copy(source, target, semaphores.at[first + index])
        for index, (source, target) in enumerate(zip(sources, targets))
    ]
    for copy in copies:
        copy.start()
    return copies


def wait_all(copies):
    for copy in copies:
        copy.wait()


def buffers(operands):
    return [pltpu.VMEM(operand.shape, operand.dtype) for operand in operands]


def tile_rows(cells):
    levels, width_x, width_y = cells.shape
    split = cells.reshape(levels, width_x // SUBLANES, SUBLANES, width_y // LANES, LANES)
    return split.transpose(0, 1, 3, 2, 4).reshape(-1, LANES)


def untile_rows(rows, levels, width_x, width_y):
    split = rows.reshape(levels, width_x // SUBLANES, width_y // LANES, SUBLANES, LANES)
    return split.transpose(0, 1, 3, 2, 4).reshape(levels, width_x, width_y)


def row_offset(x, y_tile, y_tiles):
    return (x // SUBLANES * y_tiles + y_tile) * SUBLANES + x % SUBLANES


def load_row(ref, group, x, width_x, width_y):
    y_tiles = width_y // LANES
    stride = width_x * y_tiles
    base = group * (SUBLANES * stride)
    return jnp.concatenate(
        [
            ref[pl.ds(base + row_offset(x, y_tile, y_tiles), SUBLANES, stride=stride), :]
            for y_tile in range(y_tiles)
        ],
        axis=1,
    )


def load_wide(ref, x, width_y):
    y_tiles = width_y // LANES
    return jnp.concatenate(
        [
            jnp.broadcast_to(ref[pl.ds(row_offset(x, y_tile, y_tiles), 1), :], (SUBLANES, LANES))
            for y_tile in range(y_tiles)
        ],
        axis=1,
    )


def lane_ids(width):
    return lax.broadcasted_iota(jnp.int32, (SUBLANES, width), 1)


def groups_at(group):
    return pl.ds(pl.multiple_of(group * SUBLANES, SUBLANES), SUBLANES)


def pairs_at(double):
    return pl.ds(pl.multiple_of(double * 2 * SUBLANES, 2 * SUBLANES), 2 * SUBLANES)


def two(parts):
    return jnp.concatenate(parts, axis=0).astype(BF16)


def store_rows(where, row_of, width_x, width_y, flag, first, other):
    for k in range(2):
        span = slice(k * width_y, (k + 1) * width_y)
        top = two([row_of(which, k) for which in range(2)])
        bottom = two([row_of(which, width_x - 2 + k) for which in range(2)])
        first[where, span] = jnp.where(flag == 0, bottom.astype(F32), top.astype(F32)).astype(BF16)
        other[where, span] = jnp.where(flag == 0, top.astype(F32), bottom.astype(F32)).astype(BF16)


def store_columns(where, row_of, width_x, width_y, flag, first, other):
    lane = lane_ids(LANES)
    lows, highs = [], []
    for which in range(2):
        low = jnp.zeros((SUBLANES, LANES), F32)
        high = jnp.zeros((SUBLANES, LANES), F32)
        for x in range(width_x):
            row = row_of(which, x)
            low = jnp.where(lane == 1 + x, row[:, 0:1], low)
            high = jnp.where(lane == 1 + x, row[:, width_y - 1 : width_y], high)
            low = jnp.where(lane == SECOND + 1 + x, row[:, 1:2], low)
            high = jnp.where(lane == SECOND + 1 + x, row[:, width_y - 2 : width_y - 1], high)
        lows.append(low)
        highs.append(high)
    low = jnp.concatenate(lows, axis=0)
    high = jnp.concatenate(highs, axis=0)
    first[where, :] = jnp.where(flag == 0, high, low).astype(BF16)
    other[where, :] = jnp.where(flag == 0, low, high).astype(BF16)


def row_pack_body(levels, width_x, width_y, flags, field, diff, first, other):
    def step(double, carry):
        store_rows(
            pairs_at(double),
            lambda which, x: load_row(field, double * 2 + which, x, width_x, width_y),
            width_x, width_y, flags[0], first, other,
        )
        return carry

    lax.fori_loop(0, levels // (2 * SUBLANES), step, 0)
    store_rows(
        pl.ds(levels, 2 * SUBLANES), lambda which, x: load_wide(diff, x, width_y),
        width_x, width_y, flags[0], first, other,
    )


def pack_rows_out(flags, field_rows, diff_rows, levels, width_x, width_y):
    shape = jax.ShapeDtypeStruct((levels + 2 * SUBLANES, 2 * width_y), BF16)
    return pl.pallas_call(
        functools.partial(row_pack_body, levels, width_x, width_y),
        out_shape=[shape] * 2,
        in_specs=[SMEM] + [VMEM] * 2,
        out_specs=[VMEM] * 2,
        compiler_params=params(8),
        cost_estimate=cost(8),
        name="pack_rows",
    )(flags, field_rows, diff_rows)


def outer_row(flag, first, other, where, which, x, width_x, width_y):
    even, odd = (other, first) if x < 0 else (first, other)
    start = (x + 2 if x < 0 else x - width_x) * width_y
    span = slice(start, start + width_y)
    value = jnp.where(flag == 0, even[where, span].astype(F32), odd[where, span].astype(F32))
    return value[which * SUBLANES : (which + 1) * SUBLANES]


def column_pack_body(levels, width_x, width_y, flags, field, diff, first, other):
    def step(double, carry):
        store_columns(
            pairs_at(double),
            lambda which, x: load_row(field, double * 2 + which, x, width_x, width_y),
            width_x, width_y, flags[1], first, other,
        )
        return carry

    lax.fori_loop(0, levels // (2 * SUBLANES), step, 0)
    store_columns(
        pl.ds(levels, 2 * SUBLANES), lambda which, x: load_wide(diff, x, width_y),
        width_x, width_y, flags[1], first, other,
    )


def pack_columns_out(flags, field_rows, diff_rows, levels, width_x, width_y):
    shape = jax.ShapeDtypeStruct((levels + 2 * SUBLANES, LANES), BF16)
    return pl.pallas_call(
        functools.partial(column_pack_body, levels, width_x, width_y),
        out_shape=[shape] * 2,
        in_specs=[SMEM] + [VMEM] * 2,
        out_specs=[VMEM] * 2,
        compiler_params=params(8),
        cost_estimate=cost(2),
        name="pack_columns",
    )(flags, field_rows, diff_rows)


def back_pack_body(levels, width_x, width_y, flags, grid, first, other):
    def step(double, carry):
        store_columns(
            pairs_at(double),
            lambda which, x: grid[groups_at(double * 2 + which), x * width_y : (x + 1) * width_y],
            width_x, width_y, flags[1], first, other,
        )
        return carry

    lax.fori_loop(0, levels // (2 * SUBLANES), step, 0)


def pack_columns_back(flags, grid, levels, width_x, width_y):
    shape = jax.ShapeDtypeStruct((levels, LANES), BF16)
    return pl.pallas_call(
        functools.partial(back_pack_body, levels, width_x, width_y),
        out_shape=[shape] * 2,
        in_specs=[SMEM] + [VMEM],
        out_specs=[VMEM] * 2,
        compiler_params=params(8),
        cost_estimate=cost(2),
        name="pack_back",
    )(flags, grid)


def corner_body(width_x, width_y, flags, near, far, first_in, other_in, first, other):
    rows = near.shape[0]
    lane = lax.broadcasted_iota(jnp.int32, (rows, LANES), 1)
    near_value = near[...].astype(F32)
    far_value = far[...].astype(F32)
    above = jnp.where(flags[0] == 0, far_value[:, width_y:], near_value[:, width_y:])
    below = jnp.where(flags[0] == 0, near_value[:, :width_y], far_value[:, :width_y])

    def insert(given, edge_of):
        value = given[...].astype(F32)
        value = jnp.where(lane == 0, edge_of(above), value)
        return jnp.where(lane == width_x + 1, edge_of(below), value).astype(BF16)

    def low(row):
        return row[:, 0:1]

    def high(row):
        return row[:, width_y - 1 : width_y]

    first[...] = insert(first_in, lambda row: jnp.where(flags[1] == 0, high(row), low(row)))
    other[...] = insert(other_in, lambda row: jnp.where(flags[1] == 0, low(row), high(row)))


def add_corners(flags, near, far, first, other, width_x, width_y):
    shape = jax.ShapeDtypeStruct(first.shape, BF16)
    return pl.pallas_call(
        functools.partial(corner_body, width_x, width_y),
        out_shape=[shape] * 2,
        in_specs=[SMEM] + [VMEM] * 4,
        out_specs=[VMEM] * 2,
        compiler_params=params(8),
        cost_estimate=cost(1),
        name="add_corners",
    )(flags, near, far, first, other)


def partners(size, offset):
    return [(i, i ^ offset) for i in range(size)]


def beyond(size):
    return [(i, (i - 1) % size if i % 2 == 0 else (i + 1) % size) for i in range(size)]


def trade_sides(first, other, axis):
    size = lax.axis_size(axis)
    return (lax.ppermute(first, axis, partners(size, 1)), lax.ppermute(other, axis, beyond(size)))


def around(side):
    return pltpu.roll(side, 1, 1) + pltpu.roll(side, LANES - 1, 1)


def second(side):
    return pltpu.roll(side, LANES - SECOND, 1)


def beside(row, left, right, x):
    width = row.shape[1]
    lane = lane_ids(width)
    return jnp.where(lane == 0, left[:, x + 1 : x + 2], pltpu.roll(row, 1, 1)) + jnp.where(
        lane == width - 1, right[:, x + 1 : x + 2], pltpu.roll(row, width - 1, 1)
    )


def split_sides(flag, first, other, where):
    near = first[where, :].astype(F32)
    far = other[where, :].astype(F32)
    return jnp.where(flag == 0, far, near), jnp.where(flag == 0, near, far)


def forward_body(
    levels, width_x, width_y,
    flags, field, target, diff, near, far, own_near, own_far, side_near, side_far,
    rows, rates, rate_sides, e0, e1, wide, both,
):
    cells = width_x * width_y

    def at(x):
        return slice((x + 2) * width_y, (x + 3) * width_y)

    last = pl.ds(levels, 2 * SUBLANES)
    for x in range(width_x):
        wide[:, at(x)] = load_wide(diff, x, width_y)
    for x in (-2, -1, width_x, width_x + 1):
        wide[:, at(x)] = outer_row(flags[0], near, far, last, 0, x, width_x, width_y)
    rates[...] = wide[...]

    diff_left, diff_right = [v[:SUBLANES] for v in split_sides(flags[1], side_near, side_far, last)]
    mine_low, mine_high = [v[:SUBLANES] for v in split_sides(flags[1], own_near, own_far, last)]
    for index, value in enumerate(
        (diff_left, diff_right, second(diff_left), second(diff_right), mine_low, mine_high)
    ):
        rate_sides[index * SUBLANES : (index + 1) * SUBLANES, :] = value

    def step(double, carry):
        where = pairs_at(double)
        sides = split_sides(flags[1], side_near, side_far, where)
        own = split_sides(flags[1], own_near, own_far, where)
        for which in range(2):
            group = double * 2 + which
            part = slice(which * SUBLANES, (which + 1) * SUBLANES)
            for x in range(width_x):
                e0[:, at(x)] = load_row(field, group, x, width_x, width_y)
            for x in (-2, -1, width_x, width_x + 1):
                e0[:, at(x)] = outer_row(flags[0], near, far, where, which, x, width_x, width_y)
            side_left, side_right = sides[0][part], sides[1][part]

            def next_side(side, mine, coefficient):
                return side + coefficient * (around(side) + second(side) + mine - 4.0 * side)

            next_left = next_side(side_left, own[0][part], diff_left)
            next_right = next_side(side_right, own[1][part], diff_right)
            for x in range(-1, width_x + 1):
                row = e0[:, at(x)]
                close = e0[:, at(x - 1)] + e0[:, at(x + 1)] + beside(row, side_left, side_right, x)
                e1[:, at(x)] = row + wide[:, at(x)] * (close - 4.0 * row)
            for x in range(width_x):
                row = e1[:, at(x)]
                close = e1[:, at(x - 1)] + e1[:, at(x + 1)] + beside(row, next_left, next_right, x)
                value = row + wide[:, at(x)] * (close - 4.0 * row)
                span = slice(x * width_y, (x + 1) * width_y)
                both[groups_at(group), span] = value
                both[
                    pl.ds(pl.multiple_of(levels + group * SUBLANES, SUBLANES), SUBLANES), span
                ] = value - load_row(target, group, x, width_x, width_y)
        return carry

    lax.fori_loop(0, levels // (2 * SUBLANES), step, 0)

    def turn(tile, carry):
        span = pl.ds(pl.multiple_of(tile * LANES, LANES), LANES)
        rows[span, :] = both[:, span].T
        return carry

    lax.fori_loop(0, cells // LANES, turn, 0, unroll=2)


def forward(flags, field_rows, target_rows, diff_rows, near, own, sides, sizes):
    levels, width_x, width_y, _, _ = sizes
    cells = width_x * width_y
    extended = (SUBLANES, (width_x + 4) * width_y)
    return pl.pallas_call(
        functools.partial(forward_body, levels, width_x, width_y),
        out_shape=[
            jax.ShapeDtypeStruct((cells, 2 * levels), F32),
            jax.ShapeDtypeStruct(extended, F32),
            jax.ShapeDtypeStruct((6 * SUBLANES, LANES), F32),
        ],
        in_specs=[SMEM] + [VMEM] * 9,
        out_specs=[VMEM] * 3,
        scratch_shapes=[
            pltpu.VMEM(extended, F32),
            pltpu.VMEM(extended, F32),
            pltpu.VMEM(extended, F32),
            pltpu.VMEM((2 * levels, cells), F32),
        ],
        compiler_params=params(8),
        cost_estimate=cost(8),
        name="forward",
    )(flags, field_rows, target_rows, diff_rows, *near, *own, *sides)


def index_body(tiles, subs, lead, rows_each, flags, counts, order, out, starts):
    devices = tiles * subs

    def begin(index, total):
        starts[index] = total
        return total + counts[index]

    lax.fori_loop(0, devices, begin, jnp.int32(0))
    half = subs // 2
    mine = flags[3]
    lane = lax.broadcasted_iota(jnp.int32, (SUBLANES, LANES), 1)
    slot = lax.broadcasted_iota(jnp.int32, (SUBLANES, LANES), 0) * LANES + lane

    def expert(block, carry):
        second_half = block // half
        network_id = mine ^ ((block - second_half * half) * 2 + 1 - second_half)
        value = jnp.zeros((SUBLANES, LANES), jnp.int32)
        base = jnp.int32(0)
        for t in range(tiles):
            device = t * subs + network_id
            count = counts[device]
            offset = starts[device] - base + lead
            shift = lax.rem(offset, LANES)
            window = order[pl.ds(lax.div(offset, LANES), SUBLANES), :]
            turned = pltpu.roll(window, lax.rem(LANES - shift, LANES), 1)
            following = jnp.concatenate([turned[1:], turned[:1]], axis=0)
            moved = jnp.where(lane < LANES - shift, turned, following)
            value = jnp.where((slot >= base) & (slot < base + count), moved, value)
            base = base + count
        out[pl.ds(block * rows_each, rows_each), :] = value[:rows_each]
        return carry

    lax.fori_loop(0, subs, expert, 0)


def slot_cells(flags, counts, column_order, sizes):
    _, width_x, width_y, tiles, subs = sizes
    cells = width_x * width_y
    packet = cells // subs
    rows_each = packet // LANES
    lead = packet
    order = jnp.pad(column_order, (lead, SUBLANES * LANES)).reshape(-1, LANES)
    return pl.pallas_call(
        functools.partial(index_body, tiles, subs, lead, rows_each),
        out_shape=jax.ShapeDtypeStruct((cells // LANES, LANES), jnp.int32),
        in_specs=[SMEM] * 2 + [VMEM],
        out_specs=VMEM,
        scratch_shapes=[pltpu.SMEM((tiles * subs,), jnp.int32)],
        compiler_params=params(4),
        cost_estimate=cost(2),
        name="slot_cells",
    )(flags, counts, order).reshape(subs, 1, packet)


def widen(value):
    missing = LANES - value.shape[1]
    return jnp.concatenate([value, jnp.zeros((value.shape[0], missing), value.dtype)], axis=1)


def lower_half(rows):
    return lax.broadcasted_iota(jnp.int32, (rows, LANES), 1) < LANES // 2


def swap_halves(value):
    return pltpu.roll(value, LANES // 2, 1)


def squeeze_rows(value):
    count = value.shape[0] // 2
    return jnp.where(lower_half(count), value[:count], swap_halves(value[count:]))


def pack_rows(put, inner, first, last, biases):
    width = first.shape[1]
    for k in range(3):
        put(inner[k][:, :LANES])
    low = lower_half(width)
    put(jnp.where(low, widen(inner[0][:, LANES:]), swap_halves(widen(inner[1][:, LANES:]))))
    put(jnp.where(low, widen(inner[2][:, LANES:]), last))
    put(first[:, :LANES])
    put(squeeze_rows(widen(first[:, LANES:])))
    tail = []
    for bias, bias_last in biases:
        tail += [piece[:, :LANES] for piece in bias]
        tail += [
            jnp.where(
                lower_half(1), widen(bias[k][:, LANES:]), swap_halves(widen(bias[k + 1][:, LANES:]))
            )
            for k in (0, 2)
        ]
        tail.append(bias_last)
    return tail


def pack_size(levels, width, tiles):
    rows = 5 * width + levels + levels // 2 + 16
    unit = 16 * tiles
    return (rows + unit - 1) // unit * unit


def weights_body(*refs):
    sources, out, targets, semaphores = refs[:5], refs[5], refs[6:11], refs[11]
    wait_all(load_all(sources, targets, semaphores))
    w_first, w_inner, w_last, b_inner, b_last = targets
    row = 0

    def put(value):
        nonlocal row
        out[row : row + value.shape[0], :] = value.astype(BF16)
        row += value.shape[0]

    bias = b_inner[...]
    bias_last = swap_halves(widen(b_last[...]))
    bias_high = bias.astype(BF16).astype(F32)
    last_high = bias_last.astype(BF16).astype(F32)
    bias_low = bias - bias_high
    last_low = bias_last - last_high
    tail = pack_rows(
        put,
        [w_inner[k].astype(F32) for k in range(3)],
        w_first[...].astype(F32),
        swap_halves(widen(w_last[...].astype(F32).T)),
        [
            ([bias_high[k : k + 1] for k in range(4)], last_high),
            ([bias_low[k : k + 1] for k in range(4)], last_low),
        ],
    )
    tail.append(jnp.zeros((out.shape[0] - row - len(tail), LANES), F32))
    put(jnp.concatenate(tail, axis=0))


def pack_weights(w_first, w_inner, w_last, b_inner, b_last, tiles):
    levels, width = w_first.shape
    operands = (w_first, w_inner, w_last.T, b_inner, b_last)
    return pl.pallas_call(
        weights_body,
        out_shape=jax.ShapeDtypeStruct((pack_size(levels, width, tiles), LANES), BF16),
        in_specs=[pl.BlockSpec(memory_space=pltpu.HBM)] * 5,
        out_specs=VMEM,
        scratch_shapes=buffers(operands) + [pltpu.SemaphoreType.DMA((5,))],
        compiler_params=params(62),
        cost_estimate=cost(1),
        name="pack_weights",
    )(*operands)


def network_body(
    levels, width, packet, carried_in,
    behind, ahead, pack_list, rows, back, grads, taken, given_back, packs, first_in, first_out, inner, last, last_half,
    kept, feeds, slopes, residues,
):
    certain = behind[0, 0, 0] >= 0
    block = pl.program_id(0)
    blocks = pl.num_programs(0)
    narrow = width - LANES
    wide = 2 * LANES
    half = packet // 2

    def fetch(cells_of, first_slot, count):
        for u in range(first_slot, first_slot + count):
            taken[u : u + 1, :] = rows[pl.ds(cells_of[0, 0, u], 1), :]

    def deliver(cells_of, first_slot, count):
        for u in range(first_slot, first_slot + count):
            back[pl.ds(cells_of[0, 0, u], 1), :] = given_back[u : u + 1, :]

    @pl.when(block == 0)
    def _():
        if carried_in is None:
            fetch(behind, 0, packet)
        else:
            taken[...] = carried_in[0][...]
            given_back[...] = carried_in[1][...]
        first_in[levels:, :] = jnp.zeros((wide - levels, wide), BF16)
        first_out[...] = jnp.zeros((LANES, wide), BF16)
        first_in[:levels, LANES:] = jnp.zeros((levels, LANES), BF16)
        inner[:, :, LANES:] = jnp.zeros((3, wide, LANES), BF16)
        inner[:, width:, :] = jnp.zeros((3, wide - width, wide), BF16)
        last[...] = jnp.zeros((wide, LANES), BF16)
        last_half[...] = jnp.zeros((wide, LANES), BF16)

    for index, source in enumerate(pack_list):

        @pl.when(block == index)
        def _():
            packs[...] = source[...]

    row = 0

    def take(size):
        nonlocal row
        value = packs[row : row + size, :].astype(F32)
        row += size
        return value

    def halves(value):
        return value[:, :narrow], swap_halves(value)[:, :narrow]

    for k in range(3):
        inner[k, :width, :LANES] = (0.5 * take(width)).astype(BF16)
    narrow_a, narrow_b = halves(0.5 * take(width))
    inner[0, :width, LANES:width] = narrow_a.astype(BF16)
    inner[1, :width, LANES:width] = narrow_b.astype(BF16)
    mixed = take(width)
    inner[2, :width, LANES:width] = (0.5 * mixed[:, :narrow]).astype(BF16)
    out_weight = jnp.where(lower_half(width), 0.0, mixed)
    last[:width, :] = out_weight.astype(BF16)
    last_half[:width, :] = (0.5 * out_weight).astype(BF16)
    wide_first = take(levels)
    narrow_a, narrow_b = halves(take(levels // 2))
    half_levels = levels // 2
    first_in[:levels, :LANES] = (0.5 * wide_first).astype(BF16)
    first_in[:half_levels, LANES:width] = (0.5 * narrow_a).astype(BF16)
    first_in[half_levels:levels, LANES:width] = (0.5 * narrow_b).astype(BF16)
    first_out[levels:, :LANES] = wide_first.astype(BF16)
    first_out[levels : levels + half_levels, LANES:width] = narrow_a.astype(BF16)
    first_out[levels + half_levels :, LANES:width] = narrow_b.astype(BF16)
    tail = take(16)

    def bias_rows(k):
        parts = []
        for base in (0, 7):
            mixed = 0.5 * tail[base + 4 + k // 2 : base + 5 + k // 2]
            side = mixed if k % 2 == 0 else swap_halves(mixed)
            side = jnp.where(lower_half(1), side, 0.0)
            parts.append(jnp.concatenate([0.5 * tail[base + k : base + k + 1], side], axis=1))
        parts.append(jnp.zeros((14, wide), F32))
        return jnp.concatenate(parts, axis=0).astype(BF16)

    first_in[LANES : LANES + 16, :] = bias_rows(0)
    for k in range(3):
        inner[k, width : width + 16, :] = bias_rows(k + 1)
    last[width : width + 16, :] = jnp.concatenate(
        [tail[6:7], tail[13:14], jnp.zeros((14, LANES), F32)], axis=0
    ).astype(BF16)

    over_rows = (((0,), (0,)), ((), ()))
    over_lanes = (((1,), (1,)), ((), ()))
    sides = (0, 1)
    lower = lower_half(half)
    ones = jnp.ones((half, LANES), BF16)

    def span(side):
        return slice(side * half, (side + 1) * half)

    for side in sides:
        kept[span(side), :] = taken[span(side), :].astype(BF16)

    def layers(chosen, current, delivered, share):
        for k in chosen:
            for side in sides:
                weight = first_in[...] if k == 0 else inner[k - 1]
                u = jnp.dot(current[side], weight, preferred_element_type=F32)
                turn = jnp.tanh(u)
                plus = 1.0 + turn
                active = u * plus
                slopes[k, span(side), :] = plus + active * (1.0 - turn)
                current[side] = jnp.concatenate(
                    [active[:, :LANES], jnp.where(lower, active[:, LANES:], 1.0)], axis=1
                ).astype(BF16)
                feeds[k, span(side), :] = current[side]
                deliver(behind, delivered, share)
                delivered += share
        return current

    layers(
        (0, 1), [jnp.concatenate([kept[span(side), :], ones], axis=1) for side in sides], 0, packet // 8
    )

    @pl.when(certain)
    def _():
        current = layers((2, 3), [feeds[1, span(side), :] for side in sides], packet // 2, packet // 8)
        for side in sides:
            output = jnp.dot(current[side], last[...], preferred_element_type=F32)
            residues[span(side), :] = jnp.where(
                lower, 0.0, kept[span(side), :].astype(F32) + output
            )

    @pl.when(certain)
    def _():
        fetched = 0
        share = packet // 10
        errors = [residues[span(side), :].astype(BF16) for side in sides]

        def weight_grad(k):
            products = []
            for side in sides:
                if k == 0:
                    feed = jnp.concatenate([kept[span(side), :], ones], axis=1)[:, : LANES + 16]
                else:
                    feed = feeds[k - 1, span(side), : width + 16]
                products.append(
                    lax.dot_general(feed, errors[side], over_rows, preferred_element_type=F32)
                )
            return products[0] + products[1]

        grad_sums = [None] * 5
        carried = [
            lax.dot_general(errors[side], last_half[...], over_lanes, preferred_element_type=F32)
            for side in sides
        ]
        grad_sums[4] = weight_grad(4)
        for k in (3, 2, 1, 0):
            for side in sides:
                errors[side] = (carried[side] * slopes[k, span(side), :]).astype(BF16)
                weight = inner[k - 1] if k > 0 else first_out[...]
                carried[side] = lax.dot_general(
                    errors[side], weight, over_lanes, preferred_element_type=F32
                )
                fetch(ahead, fetched, share)
                fetched += share
            grad_sums[k] = weight_grad(k)
        fetch(ahead, fetched, packet - fetched)
        for side in sides:
            given_back[span(side), :] = residues[span(side), :] + carried[side]

        filled = 0

        def put(value):
            nonlocal filled
            grads[0, filled : filled + value.shape[0], :] = value.astype(BF16)
            filled += value.shape[0]

        tail = pack_rows(
            put,
            [grad_sums[k][:width, :width] for k in (1, 2, 3)],
            grad_sums[0][:levels, :width],
            grad_sums[4][:width],
            [
                (
                    [grad_sums[0][LANES : LANES + 1, :width]]
                    + [grad_sums[k][width : width + 1, :width] for k in (1, 2, 3)],
                    grad_sums[4][width : width + 1],
                )
            ],
        )
        tail.append(jnp.zeros((grads.shape[1] - filled - len(tail), LANES), F32))
        put(jnp.concatenate(tail, axis=0))

    if carried_in is not None:

        @pl.when(block == blocks - 1)
        def _():
            deliver(ahead, 0, packet)


def network(cells_of, pack_list, rows, before, shift, levels, width, subs):
    cells, doubled = rows.shape
    packet = cells // subs
    blocks = len(pack_list)
    pack_shape = pack_list[0].shape
    final = before is not None
    limit = blocks - 1 if final else blocks
    wide = 2 * LANES

    def body(behind, ahead, *refs):
        names, rest = refs[:blocks], refs[blocks + 1 :]
        carried_in = None
        if final:
            carried_in, rest = rest[1:3], rest[3:]
        network_body(
            levels, width, packet, carried_in, behind, ahead, names, refs[blocks], *rest
        )

    operands = [cells_of, cells_of, *pack_list, rows]
    in_specs = [
        pl.BlockSpec(
            (1, 1, packet),
            lambda i: (jnp.maximum(i - 1 + shift, 0), 0, 0),
            memory_space=pltpu.SMEM,
        ),
        pl.BlockSpec(
            (1, 1, packet),
            lambda i: (jnp.minimum(i + 1, limit) + shift, 0, 0),
            memory_space=pltpu.SMEM,
        ),
    ] + [VMEM] * (blocks + 1)
    aliases = {}
    held = [jax.ShapeDtypeStruct((packet, doubled), F32)] * 2
    scratch = []
    if final:
        aliases = {len(operands): 0}
        operands += list(before)
        in_specs += [VMEM] * 3
        scratch = [pltpu.VMEM((packet, doubled), F32)] * 2
        held = []
    return pl.pallas_call(
        body,
        grid=(blocks,),
        out_shape=[
            jax.ShapeDtypeStruct((cells, doubled), F32),
            jax.ShapeDtypeStruct((blocks, *pack_shape), BF16),
        ]
        + held,
        in_specs=in_specs,
        out_specs=[VMEM, pl.BlockSpec((1, *pack_shape), lambda i: (i, 0, 0))] + [VMEM] * len(held),
        scratch_shapes=scratch
        + [
            pltpu.VMEM(pack_shape, BF16),
            pltpu.VMEM((wide, wide), BF16),
            pltpu.VMEM((LANES, wide), BF16),
            pltpu.VMEM((3, wide, wide), BF16),
            pltpu.VMEM((wide, LANES), BF16),
            pltpu.VMEM((wide, LANES), BF16),
            pltpu.VMEM((packet, LANES), BF16),
            pltpu.VMEM((4, packet, wide), BF16),
            pltpu.VMEM((4, packet, wide), F32),
            pltpu.VMEM((packet, LANES), F32),
        ],
        input_output_aliases=aliases,
        compiler_params=params(24),
        cost_estimate=cost(12),
        name="network",
    )(*operands)


def add_body(first, other, *outs):
    for index, out in enumerate(outs):
        out[...] = (first[index].astype(F32) + other[index].astype(F32)).astype(BF16)


def add_pair(first, other):
    return pl.pallas_call(
        add_body,
        out_shape=[jax.ShapeDtypeStruct(first.shape[1:], BF16)] * first.shape[0],
        in_specs=[VMEM] * 2,
        out_specs=[VMEM] * first.shape[0],
        compiler_params=params(8),
        cost_estimate=cost(1),
        name="add_pair",
    )(first, other)


def total_of(parts):
    total = parts[0][...].astype(F32)
    for part in parts[1:]:
        total = total + part[...].astype(F32)
    return total.astype(BF16)


def share_body(count, flags, *refs):
    parts, outs, whole = refs[:count], refs[count:-1], refs[-1]
    whole[...] = total_of(parts).astype(F32)
    rows = outs[0].shape[0]
    for offset, out in enumerate(outs):
        start = pl.multiple_of((flags[2] ^ offset) * rows, 16)
        out[...] = whole[pl.ds(start, rows), :].astype(BF16)


def sum_and_share(flags, parts, tiles):
    rows = parts[0].shape[0]
    return pl.pallas_call(
        functools.partial(share_body, len(parts)),
        out_shape=[jax.ShapeDtypeStruct((rows // tiles, LANES), BF16)] * tiles,
        in_specs=[SMEM] + [VMEM] * len(parts),
        out_specs=[VMEM] * tiles,
        scratch_shapes=[pltpu.VMEM((rows, LANES), F32)],
        compiler_params=params(8),
        cost_estimate=cost(1),
        name="sum_and_share",
    )(flags, *parts)


def sum_body(*refs):
    refs[-1][...] = total_of(refs[:-1])


def sum_parts(parts):
    return pl.pallas_call(
        sum_body,
        out_shape=jax.ShapeDtypeStruct(parts[0].shape, BF16),
        in_specs=[VMEM] * len(parts),
        out_specs=VMEM,
        compiler_params=params(8),
        cost_estimate=cost(1),
        name="sum_parts",
    )(*parts)


def steps_body(levels, width, count, tiles, flags, *refs):
    parts, (first, inner, last, bias, bias_last, whole) = refs[:tiles], refs[tiles:]
    share = parts[0].shape[0]
    for offset, part in enumerate(parts):
        whole[pl.ds(pl.multiple_of((flags[2] ^ offset) * share, 16), share), :] = part[...]

    def squares(index, total):
        part = whole[pl.ds(pl.multiple_of(index * 16, 16), 16), :].astype(F32)
        return total + part * part

    total = lax.fori_loop(0, whole.shape[0] // 16, squares, jnp.zeros((16, LANES), F32), unroll=4)
    factor = 1.0 / jnp.sqrt(jnp.broadcast_to(jnp.sum(total), (1, LANES)) / count + 1e-06)
    row = 0

    def take(size):
        nonlocal row
        value = whole[row : row + size, :].astype(F32) * factor
        row += size
        return value

    half = LANES // 2
    for k in range(3):
        inner[k, :, :LANES] = take(width)
    narrow = take(width)
    inner[0, :, LANES:] = narrow[:, :half]
    inner[1, :, LANES:] = swap_halves(narrow)[:, :half]
    narrow = take(width)
    inner[2, :, LANES:] = narrow[:, :half]
    last[...] = swap_halves(narrow).T[:half]
    first[:, :LANES] = take(levels)
    narrow = take(levels // 2)
    first[: levels // 2, LANES:] = narrow[:, :half]
    first[levels // 2 :, LANES:] = swap_halves(narrow)[:, :half]
    tail = take(16)
    bias[:, :LANES] = tail[0:4]
    for k in (0, 2):
        pair = tail[4 + k // 2 : 5 + k // 2]
        bias[k : k + 1, LANES:] = pair[:, :half]
        bias[k + 1 : k + 2, LANES:] = swap_halves(pair)[:, :half]
    bias_last[...] = swap_halves(tail[6:7])[:, :half]


def make_steps(flags, parts, levels, width):
    count = 2 * levels * width + 3 * width * width + 4 * width + levels
    return pl.pallas_call(
        functools.partial(steps_body, levels, width, float(count), len(parts)),
        out_shape=[
            jax.ShapeDtypeStruct((levels, width), F32),
            jax.ShapeDtypeStruct((3, width, width), F32),
            jax.ShapeDtypeStruct((levels, width), F32),
            jax.ShapeDtypeStruct((4, width), F32),
            jax.ShapeDtypeStruct((1, levels), F32),
        ],
        in_specs=[SMEM] + [VMEM] * len(parts),
        out_specs=[VMEM] * 5,
        scratch_shapes=[pltpu.VMEM((len(parts) * parts[0].shape[0], LANES), BF16)],
        compiler_params=params(8),
        cost_estimate=cost(2),
        name="make_steps",
    )(flags, *parts)


def collect_body(levels, width_x, width_y, flags, rows, grid, first, other):
    cells = width_x * width_y

    def turn(tile, carry):
        span = pl.ds(pl.multiple_of(tile * LANES, LANES), LANES)
        grid[:, span] = rows[span, :].T[levels:].astype(BF16).astype(F32)
        return carry

    lax.fori_loop(0, cells // LANES, turn, 0, unroll=2)

    def step(double, carry):
        store_rows(
            pairs_at(double),
            lambda which, x: grid[groups_at(double * 2 + which), x * width_y : (x + 1) * width_y],
            width_x, width_y, flags[0], first, other,
        )
        return carry

    lax.fori_loop(0, levels // (2 * SUBLANES), step, 0)


def collect(flags, rows, sizes):
    levels, width_x, width_y, _, _ = sizes
    cells = width_x * width_y
    shape = jax.ShapeDtypeStruct((levels, 2 * width_y), BF16)
    return pl.pallas_call(
        functools.partial(collect_body, levels, width_x, width_y),
        out_shape=[jax.ShapeDtypeStruct((levels, cells), F32), shape, shape],
        in_specs=[SMEM, VMEM],
        out_specs=[VMEM] * 3,
        compiler_params=params(8),
        cost_estimate=cost(3),
        name="collect",
    )(flags, rows)


def adjoint_body(
    levels, width_x, width_y,
    flags, grid, wide, rate_sides, near, far, own_near, own_far, side_near, side_far, out, flow, e1,
):
    y_tiles = width_y // LANES
    stride = width_x * y_tiles

    def at(x):
        return slice((x + 2) * width_y, (x + 3) * width_y)

    rate_left, rate_right, outer_left, outer_right, mine_left, mine_right = [
        rate_sides[index * SUBLANES : (index + 1) * SUBLANES, :] for index in range(6)
    ]

    def step(double, carry):
        where = pairs_at(double)
        sides = split_sides(flags[1], side_near, side_far, where)
        owns = split_sides(flags[1], own_near, own_far, where)
        for which in range(2):
            group = double * 2 + which
            own = groups_at(group)
            part = slice(which * SUBLANES, (which + 1) * SUBLANES)

            def next_side(side, rate, outer_rate, mine, mine_rate):
                product = side * rate
                return product, side + (
                    around(product) + second(side) * outer_rate + mine * mine_rate - 4.0 * product
                )

            flow_left, next_left = next_side(
                sides[0][part], rate_left, outer_left, owns[0][part], mine_left
            )
            flow_right, next_right = next_side(
                sides[1][part], rate_right, outer_right, owns[1][part], mine_right
            )

            def value(x):
                if 0 <= x < width_x:
                    return grid[own, x * width_y : (x + 1) * width_y]
                return outer_row(flags[0], near, far, where, which, x, width_x, width_y)

            for x in range(-2, width_x + 2):
                flow[:, at(x)] = value(x) * wide[:, at(x)]
            for x in range(-1, width_x + 1):
                row = flow[:, at(x)]
                close = flow[:, at(x - 1)] + flow[:, at(x + 1)]
                close = close + beside(row, flow_left, flow_right, x)
                e1[:, at(x)] = value(x) + close - 4.0 * row
            for x in range(-1, width_x + 1):
                flow[:, at(x)] = e1[:, at(x)] * wide[:, at(x)]
            flow_left = next_left * rate_left
            flow_right = next_right * rate_right
            for x in range(width_x):
                row = flow[:, at(x)]
                close = flow[:, at(x - 1)] + flow[:, at(x + 1)]
                close = close + beside(row, flow_left, flow_right, x)
                result = e1[:, at(x)] + close - 4.0 * row
                for y_tile in range(y_tiles):
                    offset = group * (SUBLANES * stride) + row_offset(x, y_tile, y_tiles)
                    out[pl.ds(offset, SUBLANES, stride=stride), :] = result[
                        :, y_tile * LANES : (y_tile + 1) * LANES
                    ]
        return carry

    lax.fori_loop(0, levels // (2 * SUBLANES), step, 0)


def adjoint(flags, grid, rates, rate_sides, near, own, sides, sizes):
    levels, width_x, width_y, _, _ = sizes
    extended = (SUBLANES, (width_x + 4) * width_y)
    return pl.pallas_call(
        functools.partial(adjoint_body, levels, width_x, width_y),
        out_shape=jax.ShapeDtypeStruct((levels * width_x * width_y // LANES, LANES), F32),
        in_specs=[SMEM] + [VMEM] * 9,
        out_specs=VMEM,
        scratch_shapes=[pltpu.VMEM(extended, F32), pltpu.VMEM(extended, F32)],
        compiler_params=params(8),
        cost_estimate=cost(6),
        name="adjoint",
    )(flags, grid, rates, rate_sides, *near, *own, *sides)


def local_program(
    initial, targets, diffusivity, column_order, send_counts,
    w_first, w_inner, w_last, b_inner, b_last,
):
    levels, width_x, width_y = initial.shape
    tiles, subs = lax.axis_size("tile"), lax.axis_size("sub")
    sizes = (levels, width_x, width_y, tiles, subs)
    field_rows = tile_rows(initial)
    target_rows = tile_rows(targets)
    diff_rows = tile_rows(diffusivity[None])
    width = w_first.shape[2]
    half = subs // 2
    tile_id, sub_id = lax.axis_index("tile"), lax.axis_index("sub")
    flags = jnp.stack([tile_id % 2, sub_id % 2, tile_id, sub_id]).astype(jnp.int32)
    area = (levels, width_x, width_y)

    first, other = pack_rows_out(flags, field_rows, diff_rows, *area)
    weights = pack_weights(w_first[0], w_inner[0], w_last[0], b_inner[0], b_last, tiles)
    own_weights = [weights] + [
        lax.ppermute(weights, "sub", partners(subs, 2 * c)) for c in range(1, half)
    ]
    near = trade_sides(first, other, "tile")
    cells_of = slot_cells(flags, send_counts[0], column_order[0], sizes)
    own = pack_columns_out(flags, field_rows, diff_rows, *area)
    own = add_corners(flags, *near, *own, width_x, width_y)
    sides = trade_sides(*own, "sub")
    other_weights = [lax.ppermute(pack, "sub", partners(subs, 1)) for pack in own_weights]
    rows, rates, rate_sides = forward(
        flags, field_rows, target_rows, diff_rows, near, own, sides, sizes
    )
    back, other_grads, taken, given_back = network(
        cells_of, other_weights, rows, None, 0, levels, width, subs
    )
    partner_grads = lax.ppermute(other_grads, "sub", partners(subs, 1))
    back, own_grads = network(
        cells_of, own_weights, rows, (back, taken, given_back), half,
        levels, width, subs,
    )
    both_grads = add_pair(own_grads, partner_grads)
    arrived = [both_grads[0]] + [
        lax.ppermute(both_grads[c], "sub", partners(subs, 2 * c)) for c in range(1, half)
    ]
    grid, g_first, g_other = collect(flags, back, sizes)
    g_near = trade_sides(g_first, g_other, "tile")
    g_own = pack_columns_back(flags, grid, *area)
    g_own = add_corners(flags, *g_near, *g_own, width_x, width_y)
    g_sides = trade_sides(*g_own, "sub")
    shares = sum_and_share(flags, arrived, tiles)
    mine = [shares[0]] + [
        lax.ppermute(shares[d], "tile", partners(tiles, d)) for d in range(1, tiles)
    ]
    result = adjoint(flags, grid, rates, rate_sides, g_near, g_own, g_sides, sizes)
    piece = sum_parts(mine)
    pieces = [piece] + [lax.ppermute(piece, "tile", partners(tiles, d)) for d in range(1, tiles)]
    steps = make_steps(flags, pieces, levels, width)
    return (
        untile_rows(result, levels, width_x, width_y),
        steps[0][None], steps[1][None], steps[2].T[None], steps[3][None], steps[4],
    )


def solution(mesh):
    placed = (
        P(None, "tile", "sub"),
        P(None, "tile", "sub"),
        P("tile", "sub"),
        P(("tile", "sub"), None),
        P(("tile", "sub"), None),
        P("sub", None, None),
        P("sub", None, None, None),
        P("sub", None, None),
        P("sub", None, None),
        P("sub", None),
    )
    return jax.shard_map(
        local_program,
        mesh=mesh,
        in_specs=placed,
        out_specs=(
            P(None, "tile", "sub"),
            P("sub", None, None),
            P("sub", None, None, None),
            P("sub", None, None),
            P("sub", None, None),
            P("sub", None),
        ),
        check_vma=False,
    )
```

```python
import functools
import jax
import jax.numpy as jnp
from jax import lax
from jax.experimental import pallas as pl
from jax.experimental.pallas import tpu as pltpu
from jax.sharding import PartitionSpec as P

LANES = 128
SUBLANES = 8
SECOND = 32
UNIT_INPUT = (0.640625, -0.00139273)
VMEM = pl.BlockSpec(memory_space=pltpu.VMEM)
ANY = pl.BlockSpec(memory_space=pl.ANY)
SMEM = pl.BlockSpec(memory_space=pltpu.SMEM)


def params(mebibytes):
    return pltpu.CompilerParams(vmem_limit_bytes=mebibytes * 1024 * 1024)


def cost(microseconds):
    moved = int(microseconds * 3e6)
    return pl.CostEstimate(flops=0, transcendentals=0, bytes_accessed=moved)


F32 = jnp.float32
BF16 = jnp.bfloat16


def load_all(sources, targets, semaphores, first=0):
    copies = [
        pltpu.make_async_copy(source, target, semaphores.at[first + index])
        for index, (source, target) in enumerate(zip(sources, targets))
    ]
    for copy in copies:
        copy.start()
    return copies


def wait_all(copies):
    for copy in copies:
        copy.wait()


def buffers(operands):
    return [pltpu.VMEM(operand.shape, operand.dtype) for operand in operands]


def tile_rows(cells):
    levels, width_x, width_y = cells.shape
    split = cells.reshape(levels, width_x // SUBLANES, SUBLANES, width_y // LANES, LANES)
    return split.transpose(0, 1, 3, 2, 4).reshape(-1, LANES)


def untile_rows(rows, levels, width_x, width_y):
    split = rows.reshape(levels, width_x // SUBLANES, width_y // LANES, SUBLANES, LANES)
    return split.transpose(0, 1, 3, 2, 4).reshape(levels, width_x, width_y)


def row_offset(x, y_tile, y_tiles):
    return (x // SUBLANES * y_tiles + y_tile) * SUBLANES + x % SUBLANES


def load_row(ref, group, x, width_x, width_y):
    y_tiles = width_y // LANES
    stride = width_x * y_tiles
    base = group * (SUBLANES * stride)
    return jnp.concatenate(
        [
            ref[pl.ds(base + row_offset(x, y_tile, y_tiles), SUBLANES, stride=stride), :]
            for y_tile in range(y_tiles)
        ],
        axis=1,
    )


def load_wide(ref, x, width_y):
    y_tiles = width_y // LANES
    return jnp.concatenate(
        [
            jnp.broadcast_to(ref[pl.ds(row_offset(x, y_tile, y_tiles), 1), :], (SUBLANES, LANES))
            for y_tile in range(y_tiles)
        ],
        axis=1,
    )


def lane_ids(width):
    return lax.broadcasted_iota(jnp.int32, (SUBLANES, width), 1)


def groups_at(group):
    return pl.ds(pl.multiple_of(group * SUBLANES, SUBLANES), SUBLANES)


def pairs_at(double):
    return pl.ds(pl.multiple_of(double * 2 * SUBLANES, 2 * SUBLANES), 2 * SUBLANES)


def two(parts):
    return jnp.concatenate(parts, axis=0).astype(BF16)


def store_rows(where, row_of, width_x, width_y, flag, first, other):
    for k in range(2):
        span = slice(k * width_y, (k + 1) * width_y)
        top = two([row_of(which, k) for which in range(2)])
        bottom = two([row_of(which, width_x - 2 + k) for which in range(2)])
        first[where, span] = jnp.where(flag == 0, bottom.astype(F32), top.astype(F32)).astype(BF16)
        other[where, span] = jnp.where(flag == 0, top.astype(F32), bottom.astype(F32)).astype(BF16)


def store_columns(where, row_of, width_x, width_y, flag, first, other):
    lane = lane_ids(LANES)
    lows, highs = [], []
    for which in range(2):
        low = jnp.zeros((SUBLANES, LANES), F32)
        high = jnp.zeros((SUBLANES, LANES), F32)
        for x in range(width_x):
            row = row_of(which, x)
            low = jnp.where(lane == 1 + x, row[:, 0:1], low)
            high = jnp.where(lane == 1 + x, row[:, width_y - 1 : width_y], high)
            low = jnp.where(lane == SECOND + 1 + x, row[:, 1:2], low)
            high = jnp.where(lane == SECOND + 1 + x, row[:, width_y - 2 : width_y - 1], high)
        lows.append(low)
        highs.append(high)
    low = jnp.concatenate(lows, axis=0)
    high = jnp.concatenate(highs, axis=0)
    first[where, :] = jnp.where(flag == 0, high, low).astype(BF16)
    other[where, :] = jnp.where(flag == 0, low, high).astype(BF16)


def row_pack_body(levels, width_x, width_y, flags, field, diff, first, other):
    def step(double, carry):
        store_rows(
            pairs_at(double),
            lambda which, x: load_row(field, double * 2 + which, x, width_x, width_y),
            width_x, width_y, flags[0], first, other,
        )
        return carry

    lax.fori_loop(0, levels // (2 * SUBLANES), step, 0)
    store_rows(
        pl.ds(levels, 2 * SUBLANES), lambda which, x: load_wide(diff, x, width_y),
        width_x, width_y, flags[0], first, other,
    )


def pack_rows_out(flags, field_rows, diff_rows, levels, width_x, width_y):
    shape = jax.ShapeDtypeStruct((levels + 2 * SUBLANES, 2 * width_y), BF16)
    return pl.pallas_call(
        functools.partial(row_pack_body, levels, width_x, width_y),
        out_shape=[shape] * 2,
        in_specs=[SMEM] + [VMEM] * 2,
        out_specs=[VMEM] * 2,
        compiler_params=params(8),
        cost_estimate=cost(8),
        name="pack_rows",
    )(flags, field_rows, diff_rows)


def outer_row(flag, first, other, where, which, x, width_x, width_y):
    even, odd = (other, first) if x < 0 else (first, other)
    start = (x + 2 if x < 0 else x - width_x) * width_y
    span = slice(start, start + width_y)
    value = jnp.where(flag == 0, even[where, span].astype(F32), odd[where, span].astype(F32))
    return value[which * SUBLANES : (which + 1) * SUBLANES]


def column_pack_body(levels, width_x, width_y, flags, field, diff, first, other):
    def step(double, carry):
        store_columns(
            pairs_at(double),
            lambda which, x: load_row(field, double * 2 + which, x, width_x, width_y),
            width_x, width_y, flags[1], first, other,
        )
        return carry

    lax.fori_loop(0, levels // (2 * SUBLANES), step, 0)
    store_columns(
        pl.ds(levels, 2 * SUBLANES), lambda which, x: load_wide(diff, x, width_y),
        width_x, width_y, flags[1], first, other,
    )


def pack_columns_out(flags, field_rows, diff_rows, levels, width_x, width_y):
    shape = jax.ShapeDtypeStruct((levels + 2 * SUBLANES, LANES), BF16)
    return pl.pallas_call(
        functools.partial(column_pack_body, levels, width_x, width_y),
        out_shape=[shape] * 2,
        in_specs=[SMEM] + [VMEM] * 2,
        out_specs=[VMEM] * 2,
        compiler_params=params(8),
        cost_estimate=cost(2),
        name="pack_columns",
    )(flags, field_rows, diff_rows)


def back_pack_body(levels, width_x, width_y, flags, grid, first, other):
    def step(double, carry):
        store_columns(
            pairs_at(double),
            lambda which, x: grid[groups_at(double * 2 + which), x * width_y : (x + 1) * width_y],
            width_x, width_y, flags[1], first, other,
        )
        return carry

    lax.fori_loop(0, levels // (2 * SUBLANES), step, 0)


def pack_columns_back(flags, grid, levels, width_x, width_y):
    shape = jax.ShapeDtypeStruct((levels, LANES), BF16)
    return pl.pallas_call(
        functools.partial(back_pack_body, levels, width_x, width_y),
        out_shape=[shape] * 2,
        in_specs=[SMEM] + [VMEM],
        out_specs=[VMEM] * 2,
        compiler_params=params(8),
        cost_estimate=cost(2),
        name="pack_back",
    )(flags, grid)


def corner_body(width_x, width_y, flags, near, far, first_in, other_in, first, other):
    rows = near.shape[0]
    lane = lax.broadcasted_iota(jnp.int32, (rows, LANES), 1)
    near_value = near[...].astype(F32)
    far_value = far[...].astype(F32)
    above = jnp.where(flags[0] == 0, far_value[:, width_y:], near_value[:, width_y:])
    below = jnp.where(flags[0] == 0, near_value[:, :width_y], far_value[:, :width_y])

    def insert(given, edge_of):
        value = given[...].astype(F32)
        value = jnp.where(lane == 0, edge_of(above), value)
        return jnp.where(lane == width_x + 1, edge_of(below), value).astype(BF16)

    def low(row):
        return row[:, 0:1]

    def high(row):
        return row[:, width_y - 1 : width_y]

    first[...] = insert(first_in, lambda row: jnp.where(flags[1] == 0, high(row), low(row)))
    other[...] = insert(other_in, lambda row: jnp.where(flags[1] == 0, low(row), high(row)))


def add_corners(flags, near, far, first, other, width_x, width_y):
    shape = jax.ShapeDtypeStruct(first.shape, BF16)
    return pl.pallas_call(
        functools.partial(corner_body, width_x, width_y),
        out_shape=[shape] * 2,
        in_specs=[SMEM] + [VMEM] * 4,
        out_specs=[VMEM] * 2,
        compiler_params=params(8),
        cost_estimate=cost(1),
        name="add_corners",
    )(flags, near, far, first, other)


def partners(size, offset):
    return [(i, i ^ offset) for i in range(size)]


def beyond(size):
    return [(i, (i - 1) % size if i % 2 == 0 else (i + 1) % size) for i in range(size)]


def trade_sides(first, other, axis):
    size = lax.axis_size(axis)
    return (lax.ppermute(first, axis, partners(size, 1)), lax.ppermute(other, axis, beyond(size)))


def around(side):
    return pltpu.roll(side, 1, 1) + pltpu.roll(side, LANES - 1, 1)


def second(side):
    return pltpu.roll(side, LANES - SECOND, 1)


def beside(row, left, right, x):
    width = row.shape[1]
    lane = lane_ids(width)
    return jnp.where(lane == 0, left[:, x + 1 : x + 2], pltpu.roll(row, 1, 1)) + jnp.where(
        lane == width - 1, right[:, x + 1 : x + 2], pltpu.roll(row, width - 1, 1)
    )


def split_sides(flag, first, other, where):
    near = first[where, :].astype(F32)
    far = other[where, :].astype(F32)
    return jnp.where(flag == 0, far, near), jnp.where(flag == 0, near, far)


def forward_body(
    levels, width_x, width_y,
    flags, field, target, diff, near, far, own_near, own_far, side_near, side_far,
    rows, rates, rate_sides, e0, e1, wide, both,
):
    cells = width_x * width_y

    def at(x):
        return slice((x + 2) * width_y, (x + 3) * width_y)

    last = pl.ds(levels, 2 * SUBLANES)
    for x in range(width_x):
        wide[:, at(x)] = load_wide(diff, x, width_y)
    for x in (-2, -1, width_x, width_x + 1):
        wide[:, at(x)] = outer_row(flags[0], near, far, last, 0, x, width_x, width_y)
    rates[...] = wide[...]

    diff_left, diff_right = [v[:SUBLANES] for v in split_sides(flags[1], side_near, side_far, last)]
    mine_low, mine_high = [v[:SUBLANES] for v in split_sides(flags[1], own_near, own_far, last)]
    for index, value in enumerate(
        (diff_left, diff_right, second(diff_left), second(diff_right), mine_low, mine_high)
    ):
        rate_sides[index * SUBLANES : (index + 1) * SUBLANES, :] = value

    def step(double, carry):
        where = pairs_at(double)
        sides = split_sides(flags[1], side_near, side_far, where)
        own = split_sides(flags[1], own_near, own_far, where)
        for which in range(2):
            group = double * 2 + which
            part = slice(which * SUBLANES, (which + 1) * SUBLANES)
            for x in range(width_x):
                e0[:, at(x)] = load_row(field, group, x, width_x, width_y)
            for x in (-2, -1, width_x, width_x + 1):
                e0[:, at(x)] = outer_row(flags[0], near, far, where, which, x, width_x, width_y)
            side_left, side_right = sides[0][part], sides[1][part]

            def next_side(side, mine, coefficient):
                return side + coefficient * (around(side) + second(side) + mine - 4.0 * side)

            next_left = next_side(side_left, own[0][part], diff_left)
            next_right = next_side(side_right, own[1][part], diff_right)
            for x in range(-1, width_x + 1):
                row = e0[:, at(x)]
                close = e0[:, at(x - 1)] + e0[:, at(x + 1)] + beside(row, side_left, side_right, x)
                e1[:, at(x)] = row + wide[:, at(x)] * (close - 4.0 * row)
            for x in range(width_x):
                row = e1[:, at(x)]
                close = e1[:, at(x - 1)] + e1[:, at(x + 1)] + beside(row, next_left, next_right, x)
                value = row + wide[:, at(x)] * (close - 4.0 * row)
                span = slice(x * width_y, (x + 1) * width_y)
                both[groups_at(group), span] = value
                both[
                    pl.ds(pl.multiple_of(levels + group * SUBLANES, SUBLANES), SUBLANES), span
                ] = value - load_row(target, group, x, width_x, width_y)
        return carry

    lax.fori_loop(0, levels // (2 * SUBLANES), step, 0)

    def turn(tile, carry):
        span = pl.ds(pl.multiple_of(tile * LANES, LANES), LANES)
        rows[span, :] = both[:, span].T
        return carry

    lax.fori_loop(0, cells // LANES, turn, 0, unroll=2)


def forward(flags, field_rows, target_rows, diff_rows, near, own, sides, sizes):
    levels, width_x, width_y, _, _ = sizes
    cells = width_x * width_y
    extended = (SUBLANES, (width_x + 4) * width_y)
    return pl.pallas_call(
        functools.partial(forward_body, levels, width_x, width_y),
        out_shape=[
            jax.ShapeDtypeStruct((cells, 2 * levels), F32),
            jax.ShapeDtypeStruct(extended, F32),
            jax.ShapeDtypeStruct((6 * SUBLANES, LANES), F32),
        ],
        in_specs=[SMEM] + [VMEM] * 9,
        out_specs=[VMEM] * 3,
        scratch_shapes=[
            pltpu.VMEM(extended, F32),
            pltpu.VMEM(extended, F32),
            pltpu.VMEM(extended, F32),
            pltpu.VMEM((2 * levels, cells), F32),
        ],
        compiler_params=params(8),
        cost_estimate=cost(8),
        name="forward",
    )(flags, field_rows, target_rows, diff_rows, *near, *own, *sides)


def index_body(tiles, subs, lead, rows_each, flags, counts, order, out, starts):
    devices = tiles * subs

    def begin(index, total):
        starts[index] = total
        return total + counts[index]

    lax.fori_loop(0, devices, begin, jnp.int32(0))
    half = subs // 2
    mine = flags[3]
    lane = lax.broadcasted_iota(jnp.int32, (SUBLANES, LANES), 1)
    slot = lax.broadcasted_iota(jnp.int32, (SUBLANES, LANES), 0) * LANES + lane

    def expert(block, carry):
        second_half = block // half
        network_id = mine ^ ((block - second_half * half) * 2 + 1 - second_half)
        value = jnp.zeros((SUBLANES, LANES), jnp.int32)
        base = jnp.int32(0)
        for t in range(tiles):
            device = t * subs + network_id
            count = counts[device]
            offset = starts[device] - base + lead
            shift = lax.rem(offset, LANES)
            window = order[pl.ds(lax.div(offset, LANES), SUBLANES), :]
            turned = pltpu.roll(window, lax.rem(LANES - shift, LANES), 1)
            following = jnp.concatenate([turned[1:], turned[:1]], axis=0)
            moved = jnp.where(lane < LANES - shift, turned, following)
            value = jnp.where((slot >= base) & (slot < base + count), moved, value)
            base = base + count
        out[pl.ds(block * rows_each, rows_each), :] = value[:rows_each]
        return carry

    lax.fori_loop(0, subs, expert, 0)


def slot_cells(flags, counts, column_order, sizes):
    _, width_x, width_y, tiles, subs = sizes
    cells = width_x * width_y
    packet = cells // subs
    rows_each = packet // LANES
    lead = packet
    order = jnp.pad(column_order, (lead, SUBLANES * LANES)).reshape(-1, LANES)
    return pl.pallas_call(
        functools.partial(index_body, tiles, subs, lead, rows_each),
        out_shape=jax.ShapeDtypeStruct((cells // LANES, LANES), jnp.int32),
        in_specs=[SMEM] * 2 + [VMEM],
        out_specs=VMEM,
        scratch_shapes=[pltpu.SMEM((tiles * subs,), jnp.int32)],
        compiler_params=params(4),
        cost_estimate=cost(2),
        name="slot_cells",
    )(flags, counts, order).reshape(subs, 1, packet)


def widen(value):
    missing = LANES - value.shape[1]
    return jnp.concatenate([value, jnp.zeros((value.shape[0], missing), value.dtype)], axis=1)


def lower_half(rows):
    return lax.broadcasted_iota(jnp.int32, (rows, LANES), 1) < LANES // 2


def swap_halves(value):
    return pltpu.roll(value, LANES // 2, 1)


def squeeze_rows(value):
    count = value.shape[0] // 2
    return jnp.where(lower_half(count), value[:count], swap_halves(value[count:]))


def pack_rows(put, inner, first, last, biases):
    width = first.shape[1]
    for k in range(3):
        put(inner[k][:, :LANES])
    low = lower_half(width)
    put(jnp.where(low, widen(inner[0][:, LANES:]), swap_halves(widen(inner[1][:, LANES:]))))
    put(jnp.where(low, widen(inner[2][:, LANES:]), last))
    put(first[:, :LANES])
    put(squeeze_rows(widen(first[:, LANES:])))
    tail = []
    for bias, bias_last in biases:
        tail += [piece[:, :LANES] for piece in bias]
        tail += [
            jnp.where(
                lower_half(1), widen(bias[k][:, LANES:]), swap_halves(widen(bias[k + 1][:, LANES:]))
            )
            for k in (0, 2)
        ]
        tail.append(bias_last)
    return tail


def pack_size(levels, width, tiles):
    rows = 5 * width + levels + levels // 2 + 16
    unit = 16 * tiles
    return (rows + unit - 1) // unit * unit


def weights_body(*refs):
    sources, out, targets, semaphores = refs[:5], refs[5], refs[6:11], refs[11]
    wait_all(load_all(sources, targets, semaphores))
    w_first, w_inner, w_last, b_inner, b_last = targets
    row = 0

    def put(value):
        nonlocal row
        out[row : row + value.shape[0], :] = value.astype(BF16)
        row += value.shape[0]

    bias = b_inner[...]
    bias_last = swap_halves(widen(b_last[...]))
    bias_high = bias.astype(BF16).astype(F32)
    last_high = bias_last.astype(BF16).astype(F32)
    bias_low = bias - bias_high
    last_low = bias_last - last_high
    tail = pack_rows(
        put,
        [w_inner[k].astype(F32) for k in range(3)],
        w_first[...].astype(F32),
        swap_halves(widen(w_last[...].astype(F32).T)),
        [
            ([bias_high[k : k + 1] for k in range(4)], last_high),
            ([bias_low[k : k + 1] for k in range(4)], last_low),
        ],
    )
    tail.append(jnp.zeros((out.shape[0] - row - len(tail), LANES), F32))
    put(jnp.concatenate(tail, axis=0))


def pack_weights(w_first, w_inner, w_last, b_inner, b_last, tiles):
    levels, width = w_first.shape
    operands = (w_first, w_inner, w_last.T, b_inner, b_last)
    return pl.pallas_call(
        weights_body,
        out_shape=jax.ShapeDtypeStruct((pack_size(levels, width, tiles), LANES), BF16),
        in_specs=[pl.BlockSpec(memory_space=pltpu.HBM)] * 5,
        out_specs=VMEM,
        scratch_shapes=buffers(operands) + [pltpu.SemaphoreType.DMA((5,))],
        compiler_params=params(62),
        cost_estimate=cost(1),
        name="pack_weights",
    )(*operands)


def network_body(
    levels, width, packet, carried_in,
    behind, ahead, pack_list, rows, back, grads, taken, given_back, packs, first_in, first_out, inner, last, last_half,
    kept, feeds, slopes, residues,
):
    block = pl.program_id(0)
    blocks = pl.num_programs(0)
    narrow = width - LANES
    wide = 2 * LANES
    half = packet // 2

    def fetch(cells_of, first_slot, count):
        for u in range(first_slot, first_slot + count):
            taken[u : u + 1, :] = rows[pl.ds(cells_of[0, 0, u], 1), :]

    def deliver(cells_of, first_slot, count):
        for u in range(first_slot, first_slot + count):
            back[pl.ds(cells_of[0, 0, u], 1), :] = given_back[u : u + 1, :]

    @pl.when(block == 0)
    def _():
        if carried_in is None:
            fetch(behind, 0, packet)
        else:
            taken[...] = carried_in[0][...]
            given_back[...] = carried_in[1][...]
        first_in[levels:, :] = jnp.zeros((wide - levels, wide), BF16)
        first_out[...] = jnp.zeros((LANES, wide), BF16)
        first_in[:levels, LANES:] = jnp.zeros((levels, LANES), BF16)
        inner[:, :, LANES:] = jnp.zeros((3, wide, LANES), BF16)
        inner[:, width:, :] = jnp.zeros((3, wide - width, wide), BF16)
        last[...] = jnp.zeros((wide, LANES), BF16)
        last_half[...] = jnp.zeros((wide, LANES), BF16)

    for index, source in enumerate(pack_list):

        @pl.when(block == index)
        def _():
            packs[...] = source[...]

    row = 0

    def take(size):
        nonlocal row
        value = packs[row : row + size, :].astype(F32)
        row += size
        return value

    def halves(value):
        return value[:, :narrow], swap_halves(value)[:, :narrow]

    for k in range(3):
        inner[k, :width, :LANES] = (0.5 * take(width)).astype(BF16)
    narrow_a, narrow_b = halves(0.5 * take(width))
    inner[0, :width, LANES:width] = narrow_a.astype(BF16)
    inner[1, :width, LANES:width] = narrow_b.astype(BF16)
    mixed = take(width)
    inner[2, :width, LANES:width] = (0.5 * mixed[:, :narrow]).astype(BF16)
    out_weight = jnp.where(lower_half(width), 0.0, mixed)
    last[:width, :] = out_weight.astype(BF16)
    last_half[:width, :] = (0.5 * out_weight).astype(BF16)
    wide_first = take(levels)
    narrow_a, narrow_b = halves(take(levels // 2))
    half_levels = levels // 2
    first_in[:levels, :LANES] = (0.5 * wide_first).astype(BF16)
    first_in[:half_levels, LANES:width] = (0.5 * narrow_a).astype(BF16)
    first_in[half_levels:levels, LANES:width] = (0.5 * narrow_b).astype(BF16)
    first_out[levels:, :LANES] = wide_first.astype(BF16)
    first_out[levels : levels + half_levels, LANES:width] = narrow_a.astype(BF16)
    first_out[levels + half_levels :, LANES:width] = narrow_b.astype(BF16)
    tail = take(16)

    spare_lane = lax.broadcasted_iota(jnp.int32, (1, LANES), 1) - narrow
    spare = (spare_lane == 0) | (spare_lane == 1)

    def bias_rows(k):
        parts = []
        for base in (0, 7):
            mixed = 0.5 * tail[base + 4 + k // 2 : base + 5 + k // 2]
            side = mixed if k % 2 == 0 else swap_halves(mixed)
            side = jnp.where(lower_half(1), side, 0.0)
            side = jnp.where(spare, UNIT_INPUT[0] if base == 0 else UNIT_INPUT[1], side)
            parts.append(jnp.concatenate([0.5 * tail[base + k : base + k + 1], side], axis=1))
        parts.append(jnp.zeros((14, wide), F32))
        return jnp.concatenate(parts, axis=0).astype(BF16)

    first_in[LANES : LANES + 16, :] = bias_rows(0)
    for k in range(3):
        inner[k, width : width + 16, :] = bias_rows(k + 1)
    last[width : width + 16, :] = jnp.concatenate(
        [tail[6:7], tail[13:14], jnp.zeros((14, LANES), F32)], axis=0
    ).astype(BF16)

    over_rows = (((0,), (0,)), ((), ()))
    over_lanes = (((1,), (1,)), ((), ()))
    sides = (0, 1)
    lower = lower_half(half)
    ones = jnp.ones((half, LANES), BF16)

    def span(side):
        return slice(side * half, (side + 1) * half)

    for side in sides:
        kept[span(side), :] = taken[span(side), :].astype(BF16)

    def layers(chosen, current, delivered, share):
        for k in chosen:
            for side in sides:
                weight = first_in[...] if k == 0 else inner[k - 1]
                u = jnp.dot(current[side], weight, preferred_element_type=F32)
                turn = jnp.tanh(u)
                plus = 1.0 + turn
                active = u * plus
                slopes[k, span(side), :] = plus
                current[side] = active.astype(BF16)
                feeds[k, span(side), :] = current[side]
                deliver(behind, delivered, share)
                delivered += share
        return current

    layers(
        (0, 1), [jnp.concatenate([kept[span(side), :], ones], axis=1) for side in sides], 0, packet // 8
    )

    def second_part():
        current = layers((2, 3), [feeds[1, span(side), :] for side in sides], packet // 2, packet // 8)
        for side in sides:
            output = jnp.dot(current[side], last[...], preferred_element_type=F32)
            residues[span(side), :] = jnp.where(
                lower, 0.0, kept[span(side), :].astype(F32) + output
            )

    second_part()

    def third_part():
        fetched = 0
        share = packet // 10
        errors = [residues[span(side), :].astype(BF16) for side in sides]

        def weight_grad(k):
            products = []
            for side in sides:
                if k == 0:
                    feed = jnp.concatenate([kept[span(side), :], ones], axis=1)[:, : LANES + 16]
                else:
                    feed = feeds[k - 1, span(side), : width + 16]
                products.append(
                    lax.dot_general(feed, errors[side], over_rows, preferred_element_type=F32)
                )
            return products[0] + products[1]

        grad_sums = [None] * 5
        carried = [
            lax.dot_general(errors[side], last_half[...], over_lanes, preferred_element_type=F32)
            for side in sides
        ]
        grad_sums[4] = weight_grad(4)
        for k in (3, 2, 1, 0):
            for side in sides:
                plus = slopes[k, span(side), :]
                slope = plus + feeds[k, span(side), :].astype(F32) * (2.0 - plus)
                errors[side] = (carried[side] * slope).astype(BF16)
                weight = inner[k - 1] if k > 0 else first_out[...]
                carried[side] = lax.dot_general(
                    errors[side], weight, over_lanes, preferred_element_type=F32
                )
                fetch(ahead, fetched, share)
                fetched += share
            grad_sums[k] = weight_grad(k)
        fetch(ahead, fetched, packet - fetched)
        for side in sides:
            given_back[span(side), :] = residues[span(side), :] + carried[side]

        filled = 0

        def put(value):
            nonlocal filled
            grads[0, filled : filled + value.shape[0], :] = value.astype(BF16)
            filled += value.shape[0]

        tail = pack_rows(
            put,
            [grad_sums[k][:width, :width] for k in (1, 2, 3)],
            grad_sums[0][:levels, :width],
            grad_sums[4][:width],
            [
                (
                    [grad_sums[0][LANES : LANES + 1, :width]]
                    + [grad_sums[k][width : width + 1, :width] for k in (1, 2, 3)],
                    grad_sums[4][width : width + 1],
                )
            ],
        )
        tail.append(jnp.zeros((grads.shape[1] - filled - len(tail), LANES), F32))
        put(jnp.concatenate(tail, axis=0))

    third_part()
    if carried_in is not None:

        @pl.when(block == blocks - 1)
        def _():
            deliver(ahead, 0, packet)


def network(cells_of, pack_list, rows, before, shift, levels, width, subs):
    cells, doubled = rows.shape
    packet = cells // subs
    blocks = len(pack_list)
    pack_shape = pack_list[0].shape
    final = before is not None
    limit = blocks - 1 if final else blocks
    wide = 2 * LANES

    def body(behind, ahead, *refs):
        names, rest = refs[:blocks], refs[blocks + 1 :]
        carried_in = None
        if final:
            carried_in, rest = rest[1:3], rest[3:]
        network_body(
            levels, width, packet, carried_in, behind, ahead, names, refs[blocks], *rest
        )

    operands = [cells_of, cells_of, *pack_list, rows]
    in_specs = [
        pl.BlockSpec(
            (1, 1, packet),
            lambda i: (jnp.maximum(i - 1 + shift, 0), 0, 0),
            memory_space=pltpu.SMEM,
        ),
        pl.BlockSpec(
            (1, 1, packet),
            lambda i: (jnp.minimum(i + 1, limit) + shift, 0, 0),
            memory_space=pltpu.SMEM,
        ),
    ] + [VMEM] * (blocks + 1)
    aliases = {}
    held = [jax.ShapeDtypeStruct((packet, doubled), F32)] * 2
    scratch = []
    if final:
        aliases = {len(operands): 0}
        operands += list(before)
        in_specs += [VMEM] * 3
        scratch = [pltpu.VMEM((packet, doubled), F32)] * 2
        held = []
    return pl.pallas_call(
        body,
        grid=(blocks,),
        out_shape=[
            jax.ShapeDtypeStruct((cells, doubled), F32),
            jax.ShapeDtypeStruct((blocks, *pack_shape), BF16),
        ]
        + held,
        in_specs=in_specs,
        out_specs=[VMEM, pl.BlockSpec((1, *pack_shape), lambda i: (i, 0, 0))] + [VMEM] * len(held),
        scratch_shapes=scratch
        + [
            pltpu.VMEM(pack_shape, BF16),
            pltpu.VMEM((wide, wide), BF16),
            pltpu.VMEM((LANES, wide), BF16),
            pltpu.VMEM((3, wide, wide), BF16),
            pltpu.VMEM((wide, LANES), BF16),
            pltpu.VMEM((wide, LANES), BF16),
            pltpu.VMEM((packet, LANES), BF16),
            pltpu.VMEM((4, packet, wide), BF16),
            pltpu.VMEM((4, packet, wide), F32),
            pltpu.VMEM((packet, LANES), F32),
        ],
        input_output_aliases=aliases,
        compiler_params=params(24),
        cost_estimate=cost(12),
        name="network",
    )(*operands)


def add_body(first, other, *outs):
    for index, out in enumerate(outs):
        out[...] = (first[index].astype(F32) + other[index].astype(F32)).astype(BF16)


def add_pair(first, other):
    return pl.pallas_call(
        add_body,
        out_shape=[jax.ShapeDtypeStruct(first.shape[1:], BF16)] * first.shape[0],
        in_specs=[VMEM] * 2,
        out_specs=[VMEM] * first.shape[0],
        compiler_params=params(8),
        cost_estimate=cost(1),
        name="add_pair",
    )(first, other)


def total_of(parts):
    total = parts[0][...].astype(F32)
    for part in parts[1:]:
        total = total + part[...].astype(F32)
    return total.astype(BF16)


def share_body(count, flags, *refs):
    parts, outs, whole = refs[:count], refs[count:-1], refs[-1]
    whole[...] = total_of(parts).astype(F32)
    rows = outs[0].shape[0]
    for offset, out in enumerate(outs):
        start = pl.multiple_of((flags[2] ^ offset) * rows, 16)
        out[...] = whole[pl.ds(start, rows), :].astype(BF16)


def sum_and_share(flags, parts, tiles):
    rows = parts[0].shape[0]
    return pl.pallas_call(
        functools.partial(share_body, len(parts)),
        out_shape=[jax.ShapeDtypeStruct((rows // tiles, LANES), BF16)] * tiles,
        in_specs=[SMEM] + [VMEM] * len(parts),
        out_specs=[VMEM] * tiles,
        scratch_shapes=[pltpu.VMEM((rows, LANES), F32)],
        compiler_params=params(8),
        cost_estimate=cost(1),
        name="sum_and_share",
    )(flags, *parts)


def sum_body(*refs):
    refs[-1][...] = total_of(refs[:-1])


def sum_parts(parts):
    return pl.pallas_call(
        sum_body,
        out_shape=jax.ShapeDtypeStruct(parts[0].shape, BF16),
        in_specs=[VMEM] * len(parts),
        out_specs=VMEM,
        compiler_params=params(8),
        cost_estimate=cost(1),
        name="sum_parts",
    )(*parts)


def steps_body(levels, width, count, tiles, flags, *refs):
    parts, (first, inner, last, bias, bias_last, whole) = refs[:tiles], refs[tiles:]
    share = parts[0].shape[0]
    for offset, part in enumerate(parts):
        whole[pl.ds(pl.multiple_of((flags[2] ^ offset) * share, 16), share), :] = part[...]

    def squares(index, total):
        part = whole[pl.ds(pl.multiple_of(index * 16, 16), 16), :].astype(F32)
        return total + part * part

    total = lax.fori_loop(0, whole.shape[0] // 16, squares, jnp.zeros((16, LANES), F32), unroll=4)
    factor = 1.0 / jnp.sqrt(jnp.broadcast_to(jnp.sum(total), (1, LANES)) / count + 1e-06)
    row = 0

    def take(size):
        nonlocal row
        value = whole[row : row + size, :].astype(F32) * factor
        row += size
        return value

    half = LANES // 2
    for k in range(3):
        inner[k, :, :LANES] = take(width)
    narrow = take(width)
    inner[0, :, LANES:] = narrow[:, :half]
    inner[1, :, LANES:] = swap_halves(narrow)[:, :half]
    narrow = take(width)
    inner[2, :, LANES:] = narrow[:, :half]
    last[...] = swap_halves(narrow).T[:half]
    first[:, :LANES] = take(levels)
    narrow = take(levels // 2)
    first[: levels // 2, LANES:] = narrow[:, :half]
    first[levels // 2 :, LANES:] = swap_halves(narrow)[:, :half]
    tail = take(16)
    bias[:, :LANES] = tail[0:4]
    for k in (0, 2):
        pair = tail[4 + k // 2 : 5 + k // 2]
        bias[k : k + 1, LANES:] = pair[:, :half]
        bias[k + 1 : k + 2, LANES:] = swap_halves(pair)[:, :half]
    bias_last[...] = swap_halves(tail[6:7])[:, :half]


def make_steps(flags, parts, levels, width):
    count = 2 * levels * width + 3 * width * width + 4 * width + levels
    return pl.pallas_call(
        functools.partial(steps_body, levels, width, float(count), len(parts)),
        out_shape=[
            jax.ShapeDtypeStruct((levels, width), F32),
            jax.ShapeDtypeStruct((3, width, width), F32),
            jax.ShapeDtypeStruct((levels, width), F32),
            jax.ShapeDtypeStruct((4, width), F32),
            jax.ShapeDtypeStruct((1, levels), F32),
        ],
        in_specs=[SMEM] + [VMEM] * len(parts),
        out_specs=[VMEM] * 5,
        scratch_shapes=[pltpu.VMEM((len(parts) * parts[0].shape[0], LANES), BF16)],
        compiler_params=params(8),
        cost_estimate=cost(2),
        name="make_steps",
    )(flags, *parts)


def collect_body(levels, width_x, width_y, flags, rows, grid, first, other):
    cells = width_x * width_y

    def turn(tile, carry):
        span = pl.ds(pl.multiple_of(tile * LANES, LANES), LANES)
        grid[:, span] = rows[span, :].T[levels:].astype(BF16).astype(F32)
        return carry

    lax.fori_loop(0, cells // LANES, turn, 0, unroll=2)

    def step(double, carry):
        store_rows(
            pairs_at(double),
            lambda which, x: grid[groups_at(double * 2 + which), x * width_y : (x + 1) * width_y],
            width_x, width_y, flags[0], first, other,
        )
        return carry

    lax.fori_loop(0, levels // (2 * SUBLANES), step, 0)


def collect(flags, rows, sizes):
    levels, width_x, width_y, _, _ = sizes
    cells = width_x * width_y
    shape = jax.ShapeDtypeStruct((levels, 2 * width_y), BF16)
    return pl.pallas_call(
        functools.partial(collect_body, levels, width_x, width_y),
        out_shape=[jax.ShapeDtypeStruct((levels, cells), F32), shape, shape],
        in_specs=[SMEM, VMEM],
        out_specs=[VMEM] * 3,
        compiler_params=params(8),
        cost_estimate=cost(3),
        name="collect",
    )(flags, rows)


def adjoint_body(
    levels, width_x, width_y,
    flags, grid, wide, rate_sides, near, far, own_near, own_far, side_near, side_far, out, flow, e1,
):
    y_tiles = width_y // LANES
    stride = width_x * y_tiles

    def at(x):
        return slice((x + 2) * width_y, (x + 3) * width_y)

    rate_left, rate_right, outer_left, outer_right, mine_left, mine_right = [
        rate_sides[index * SUBLANES : (index + 1) * SUBLANES, :] for index in range(6)
    ]

    def step(double, carry):
        where = pairs_at(double)
        sides = split_sides(flags[1], side_near, side_far, where)
        owns = split_sides(flags[1], own_near, own_far, where)
        for which in range(2):
            group = double * 2 + which
            own = groups_at(group)
            part = slice(which * SUBLANES, (which + 1) * SUBLANES)

            def next_side(side, rate, outer_rate, mine, mine_rate):
                product = side * rate
                return product, side + (
                    around(product) + second(side) * outer_rate + mine * mine_rate - 4.0 * product
                )

            flow_left, next_left = next_side(
                sides[0][part], rate_left, outer_left, owns[0][part], mine_left
            )
            flow_right, next_right = next_side(
                sides[1][part], rate_right, outer_right, owns[1][part], mine_right
            )

            def value(x):
                if 0 <= x < width_x:
                    return grid[own, x * width_y : (x + 1) * width_y]
                return outer_row(flags[0], near, far, where, which, x, width_x, width_y)

            for x in range(-2, width_x + 2):
                flow[:, at(x)] = value(x) * wide[:, at(x)]
            for x in range(-1, width_x + 1):
                row = flow[:, at(x)]
                close = flow[:, at(x - 1)] + flow[:, at(x + 1)]
                close = close + beside(row, flow_left, flow_right, x)
                e1[:, at(x)] = value(x) + close - 4.0 * row
            for x in range(-1, width_x + 1):
                flow[:, at(x)] = e1[:, at(x)] * wide[:, at(x)]
            flow_left = next_left * rate_left
            flow_right = next_right * rate_right
            for x in range(width_x):
                row = flow[:, at(x)]
                close = flow[:, at(x - 1)] + flow[:, at(x + 1)]
                close = close + beside(row, flow_left, flow_right, x)
                result = e1[:, at(x)] + close - 4.0 * row
                for y_tile in range(y_tiles):
                    offset = group * (SUBLANES * stride) + row_offset(x, y_tile, y_tiles)
                    out[pl.ds(offset, SUBLANES, stride=stride), :] = result[
                        :, y_tile * LANES : (y_tile + 1) * LANES
                    ]
        return carry

    lax.fori_loop(0, levels // (2 * SUBLANES), step, 0)


def adjoint(flags, grid, rates, rate_sides, near, own, sides, sizes):
    levels, width_x, width_y, _, _ = sizes
    extended = (SUBLANES, (width_x + 4) * width_y)
    return pl.pallas_call(
        functools.partial(adjoint_body, levels, width_x, width_y),
        out_shape=jax.ShapeDtypeStruct((levels * width_x * width_y // LANES, LANES), F32),
        in_specs=[SMEM] + [VMEM] * 9,
        out_specs=VMEM,
        scratch_shapes=[pltpu.VMEM(extended, F32), pltpu.VMEM(extended, F32)],
        compiler_params=params(8),
        cost_estimate=cost(6),
        name="adjoint",
    )(flags, grid, rates, rate_sides, *near, *own, *sides)


def local_program(
    initial, targets, diffusivity, column_order, send_counts,
    w_first, w_inner, w_last, b_inner, b_last,
):
    levels, width_x, width_y = initial.shape
    tiles, subs = lax.axis_size("tile"), lax.axis_size("sub")
    sizes = (levels, width_x, width_y, tiles, subs)
    field_rows = tile_rows(initial)
    target_rows = tile_rows(targets)
    diff_rows = tile_rows(diffusivity[None])
    width = w_first.shape[2]
    half = subs // 2
    tile_id, sub_id = lax.axis_index("tile"), lax.axis_index("sub")
    flags = jnp.stack([tile_id % 2, sub_id % 2, tile_id, sub_id]).astype(jnp.int32)
    area = (levels, width_x, width_y)

    first, other = pack_rows_out(flags, field_rows, diff_rows, *area)
    weights = pack_weights(w_first[0], w_inner[0], w_last[0], b_inner[0], b_last, tiles)
    own_weights = [weights] + [
        lax.ppermute(weights, "sub", partners(subs, 2 * c)) for c in range(1, half)
    ]
    near = trade_sides(first, other, "tile")
    cells_of = slot_cells(flags, send_counts[0], column_order[0], sizes)
    own = pack_columns_out(flags, field_rows, diff_rows, *area)
    own = add_corners(flags, *near, *own, width_x, width_y)
    sides = trade_sides(*own, "sub")
    other_weights = [lax.ppermute(pack, "sub", partners(subs, 1)) for pack in own_weights]
    rows, rates, rate_sides = forward(
        flags, field_rows, target_rows, diff_rows, near, own, sides, sizes
    )
    back, other_grads, taken, given_back = network(
        cells_of, other_weights, rows, None, 0, levels, width, subs
    )
    partner_grads = lax.ppermute(other_grads, "sub", partners(subs, 1))
    back, own_grads = network(
        cells_of, own_weights, rows, (back, taken, given_back), half,
        levels, width, subs,
    )
    both_grads = add_pair(own_grads, partner_grads)
    arrived = [both_grads[0]] + [
        lax.ppermute(both_grads[c], "sub", partners(subs, 2 * c)) for c in range(1, half)
    ]
    grid, g_first, g_other = collect(flags, back, sizes)
    g_near = trade_sides(g_first, g_other, "tile")
    g_own = pack_columns_back(flags, grid, *area)
    g_own = add_corners(flags, *g_near, *g_own, width_x, width_y)
    g_sides = trade_sides(*g_own, "sub")
    shares = sum_and_share(flags, arrived, tiles)
    mine = [shares[0]] + [
        lax.ppermute(shares[d], "tile", partners(tiles, d)) for d in range(1, tiles)
    ]
    result = adjoint(flags, grid, rates, rate_sides, g_near, g_own, g_sides, sizes)
    piece = sum_parts(mine)
    pieces = [piece] + [lax.ppermute(piece, "tile", partners(tiles, d)) for d in range(1, tiles)]
    steps = make_steps(flags, pieces, levels, width)
    return (
        untile_rows(result, levels, width_x, width_y),
        steps[0][None], steps[1][None], steps[2].T[None], steps[3][None], steps[4],
    )


def solution(mesh):
    placed = (
        P(None, "tile", "sub"),
        P(None, "tile", "sub"),
        P("tile", "sub"),
        P(("tile", "sub"), None),
        P(("tile", "sub"), None),
        P("sub", None, None),
        P("sub", None, None, None),
        P("sub", None, None),
        P("sub", None, None),
        P("sub", None),
    )
    return jax.shard_map(
        local_program,
        mesh=mesh,
        in_specs=placed,
        out_specs=(
            P(None, "tile", "sub"),
            P("sub", None, None),
            P("sub", None, None, None),
            P("sub", None, None),
            P("sub", None, None),
            P("sub", None),
        ),
        check_vma=False,
    )
```

```python
import functools
import jax
import jax.numpy as jnp
from jax import lax
from jax.experimental import pallas as pl
from jax.experimental.pallas import tpu as pltpu
from jax.sharding import PartitionSpec as P

LANES = 128
SUBLANES = 8
SECOND = 32
UNIT_INPUT = (0.640625, -0.00139273)
VMEM = pl.BlockSpec(memory_space=pltpu.VMEM)
ANY = pl.BlockSpec(memory_space=pl.ANY)
SMEM = pl.BlockSpec(memory_space=pltpu.SMEM)


def params(mebibytes):
    return pltpu.CompilerParams(vmem_limit_bytes=mebibytes * 1024 * 1024)


def cost(microseconds):
    moved = int(microseconds * 3e6)
    return pl.CostEstimate(flops=0, transcendentals=0, bytes_accessed=moved)


F32 = jnp.float32
BF16 = jnp.bfloat16


def with_flags(body):
    def inner(*refs):
        tile, sub = lax.axis_index("tile"), lax.axis_index("sub")
        return body((tile & 1, sub & 1, tile, sub), *refs)

    return inner


def load_all(sources, targets, semaphores, first=0):
    copies = [
        pltpu.make_async_copy(source, target, semaphores.at[first + index])
        for index, (source, target) in enumerate(zip(sources, targets))
    ]
    for copy in copies:
        copy.start()
    return copies


def wait_all(copies):
    for copy in copies:
        copy.wait()


def buffers(operands):
    return [pltpu.VMEM(operand.shape, operand.dtype) for operand in operands]


def tile_rows(cells):
    levels, width_x, width_y = cells.shape
    split = cells.reshape(levels, width_x // SUBLANES, SUBLANES, width_y // LANES, LANES)
    return split.transpose(0, 1, 3, 2, 4).reshape(-1, LANES)


def untile_rows(rows, levels, width_x, width_y):
    split = rows.reshape(levels, width_x // SUBLANES, width_y // LANES, SUBLANES, LANES)
    return split.transpose(0, 1, 3, 2, 4).reshape(levels, width_x, width_y)


def row_offset(x, y_tile, y_tiles):
    return (x // SUBLANES * y_tiles + y_tile) * SUBLANES + x % SUBLANES


def load_row(ref, group, x, width_x, width_y):
    y_tiles = width_y // LANES
    stride = width_x * y_tiles
    base = group * (SUBLANES * stride)
    return jnp.concatenate(
        [
            ref[pl.ds(base + row_offset(x, y_tile, y_tiles), SUBLANES, stride=stride), :]
            for y_tile in range(y_tiles)
        ],
        axis=1,
    )


def load_wide(ref, x, width_y):
    y_tiles = width_y // LANES
    return jnp.concatenate(
        [
            jnp.broadcast_to(ref[pl.ds(row_offset(x, y_tile, y_tiles), 1), :], (SUBLANES, LANES))
            for y_tile in range(y_tiles)
        ],
        axis=1,
    )


def lane_ids(width):
    return lax.broadcasted_iota(jnp.int32, (SUBLANES, width), 1)


def groups_at(group):
    return pl.ds(pl.multiple_of(group * SUBLANES, SUBLANES), SUBLANES)


def pairs_at(double):
    return pl.ds(pl.multiple_of(double * 2 * SUBLANES, 2 * SUBLANES), 2 * SUBLANES)


def two(parts):
    return jnp.concatenate(parts, axis=0).astype(BF16)


def store_rows(where, row_of, width_x, width_y, flag, first, other):
    for k in range(2):
        span = slice(k * width_y, (k + 1) * width_y)
        top = two([row_of(which, k) for which in range(2)])
        bottom = two([row_of(which, width_x - 2 + k) for which in range(2)])
        first[where, span] = jnp.where(flag == 0, bottom.astype(F32), top.astype(F32)).astype(BF16)
        other[where, span] = jnp.where(flag == 0, top.astype(F32), bottom.astype(F32)).astype(BF16)


def store_columns(where, row_of, width_x, width_y, flag, first, other):
    lane = lane_ids(LANES)
    lows, highs = [], []
    for which in range(2):
        low = jnp.zeros((SUBLANES, LANES), F32)
        high = jnp.zeros((SUBLANES, LANES), F32)
        for x in range(width_x):
            row = row_of(which, x)
            low = jnp.where(lane == 1 + x, row[:, 0:1], low)
            high = jnp.where(lane == 1 + x, row[:, width_y - 1 : width_y], high)
            low = jnp.where(lane == SECOND + 1 + x, row[:, 1:2], low)
            high = jnp.where(lane == SECOND + 1 + x, row[:, width_y - 2 : width_y - 1], high)
        lows.append(low)
        highs.append(high)
    low = jnp.concatenate(lows, axis=0)
    high = jnp.concatenate(highs, axis=0)
    first[where, :] = jnp.where(flag == 0, high, low).astype(BF16)
    other[where, :] = jnp.where(flag == 0, low, high).astype(BF16)


def row_pack_body(levels, width_x, width_y, flags, field, diff, first, other):
    def step(double, carry):
        store_rows(
            pairs_at(double),
            lambda which, x: load_row(field, double * 2 + which, x, width_x, width_y),
            width_x, width_y, flags[0], first, other,
        )
        return carry

    lax.fori_loop(0, levels // (2 * SUBLANES), step, 0)
    store_rows(
        pl.ds(levels, 2 * SUBLANES), lambda which, x: load_wide(diff, x, width_y),
        width_x, width_y, flags[0], first, other,
    )


def pack_rows_out(field_rows, diff_rows, levels, width_x, width_y):
    shape = jax.ShapeDtypeStruct((levels + 2 * SUBLANES, 2 * width_y), BF16)
    return pl.pallas_call(
        with_flags(functools.partial(row_pack_body, levels, width_x, width_y)),
        out_shape=[shape] * 2,
        in_specs=[VMEM] * 2,
        out_specs=[VMEM] * 2,
        compiler_params=params(8),
        cost_estimate=cost(8),
        name="pack_rows",
    )(field_rows, diff_rows)


def outer_row(flag, first, other, where, which, x, width_x, width_y):
    even, odd = (other, first) if x < 0 else (first, other)
    start = (x + 2 if x < 0 else x - width_x) * width_y
    span = slice(start, start + width_y)
    value = jnp.where(flag == 0, even[where, span].astype(F32), odd[where, span].astype(F32))
    return value[which * SUBLANES : (which + 1) * SUBLANES]


def column_pack_body(levels, width_x, width_y, flags, field, diff, first, other):
    def step(double, carry):
        store_columns(
            pairs_at(double),
            lambda which, x: load_row(field, double * 2 + which, x, width_x, width_y),
            width_x, width_y, flags[1], first, other,
        )
        return carry

    lax.fori_loop(0, levels // (2 * SUBLANES), step, 0)
    store_columns(
        pl.ds(levels, 2 * SUBLANES), lambda which, x: load_wide(diff, x, width_y),
        width_x, width_y, flags[1], first, other,
    )


def pack_columns_out(field_rows, diff_rows, levels, width_x, width_y):
    shape = jax.ShapeDtypeStruct((levels + 2 * SUBLANES, LANES), BF16)
    return pl.pallas_call(
        with_flags(functools.partial(column_pack_body, levels, width_x, width_y)),
        out_shape=[shape] * 2,
        in_specs=[VMEM] * 2,
        out_specs=[VMEM] * 2,
        compiler_params=params(8),
        cost_estimate=cost(2),
        name="pack_columns",
    )(field_rows, diff_rows)


def back_pack_body(levels, width_x, width_y, flags, grid, first, other):
    def step(double, carry):
        store_columns(
            pairs_at(double),
            lambda which, x: grid[groups_at(double * 2 + which), x * width_y : (x + 1) * width_y],
            width_x, width_y, flags[1], first, other,
        )
        return carry

    lax.fori_loop(0, levels // (2 * SUBLANES), step, 0)


def pack_columns_back(grid, levels, width_x, width_y):
    shape = jax.ShapeDtypeStruct((levels, LANES), BF16)
    return pl.pallas_call(
        with_flags(functools.partial(back_pack_body, levels, width_x, width_y)),
        out_shape=[shape] * 2,
        in_specs=[VMEM],
        out_specs=[VMEM] * 2,
        compiler_params=params(8),
        cost_estimate=cost(2),
        name="pack_back",
    )(grid)


def corner_body(width_x, width_y, flags, near, far, first_in, other_in, first, other):
    rows = near.shape[0]
    lane = lax.broadcasted_iota(jnp.int32, (rows, LANES), 1)
    near_value = near[...].astype(F32)
    far_value = far[...].astype(F32)
    above = jnp.where(flags[0] == 0, far_value[:, width_y:], near_value[:, width_y:])
    below = jnp.where(flags[0] == 0, near_value[:, :width_y], far_value[:, :width_y])

    def insert(given, edge_of):
        value = given[...].astype(F32)
        value = jnp.where(lane == 0, edge_of(above), value)
        return jnp.where(lane == width_x + 1, edge_of(below), value).astype(BF16)

    def low(row):
        return row[:, 0:1]

    def high(row):
        return row[:, width_y - 1 : width_y]

    first[...] = insert(first_in, lambda row: jnp.where(flags[1] == 0, high(row), low(row)))
    other[...] = insert(other_in, lambda row: jnp.where(flags[1] == 0, low(row), high(row)))


def add_corners(near, far, first, other, width_x, width_y):
    shape = jax.ShapeDtypeStruct(first.shape, BF16)
    return pl.pallas_call(
        with_flags(functools.partial(corner_body, width_x, width_y)),
        out_shape=[shape] * 2,
        in_specs=[VMEM] * 4,
        out_specs=[VMEM] * 2,
        compiler_params=params(8),
        cost_estimate=cost(1),
        name="add_corners",
    )(near, far, first, other)


def partners(size, offset):
    return [(i, i ^ offset) for i in range(size)]


def beyond(size):
    return [(i, (i - 1) % size if i % 2 == 0 else (i + 1) % size) for i in range(size)]


def trade_sides(first, other, axis):
    size = lax.axis_size(axis)
    return (lax.ppermute(first, axis, partners(size, 1)), lax.ppermute(other, axis, beyond(size)))


def around(side):
    return pltpu.roll(side, 1, 1) + pltpu.roll(side, LANES - 1, 1)


def second(side):
    return pltpu.roll(side, LANES - SECOND, 1)


def beside(row, left, right, x):
    width = row.shape[1]
    lane = lane_ids(width)
    return jnp.where(lane == 0, left[:, x + 1 : x + 2], pltpu.roll(row, 1, 1)) + jnp.where(
        lane == width - 1, right[:, x + 1 : x + 2], pltpu.roll(row, width - 1, 1)
    )


def split_sides(flag, first, other, where):
    near = first[where, :].astype(F32)
    far = other[where, :].astype(F32)
    return jnp.where(flag == 0, far, near), jnp.where(flag == 0, near, far)


def forward_body(
    levels, width_x, width_y,
    flags, field, target, diff, near, far, own_near, own_far, side_near, side_far,
    rows, rates, rate_sides, e0, e1, wide, both,
):
    cells = width_x * width_y

    def at(x):
        return slice((x + 2) * width_y, (x + 3) * width_y)

    last = pl.ds(levels, 2 * SUBLANES)
    for x in range(width_x):
        wide[:, at(x)] = load_wide(diff, x, width_y)
    for x in (-2, -1, width_x, width_x + 1):
        wide[:, at(x)] = outer_row(flags[0], near, far, last, 0, x, width_x, width_y)
    rates[...] = wide[...]

    diff_left, diff_right = [v[:SUBLANES] for v in split_sides(flags[1], side_near, side_far, last)]
    mine_low, mine_high = [v[:SUBLANES] for v in split_sides(flags[1], own_near, own_far, last)]
    for index, value in enumerate(
        (diff_left, diff_right, second(diff_left), second(diff_right), mine_low, mine_high)
    ):
        rate_sides[index * SUBLANES : (index + 1) * SUBLANES, :] = value

    def step(double, carry):
        where = pairs_at(double)
        sides = split_sides(flags[1], side_near, side_far, where)
        own = split_sides(flags[1], own_near, own_far, where)
        for which in range(2):
            group = double * 2 + which
            part = slice(which * SUBLANES, (which + 1) * SUBLANES)
            for x in range(width_x):
                e0[:, at(x)] = load_row(field, group, x, width_x, width_y)
            for x in (-2, -1, width_x, width_x + 1):
                e0[:, at(x)] = outer_row(flags[0], near, far, where, which, x, width_x, width_y)
            side_left, side_right = sides[0][part], sides[1][part]

            def next_side(side, mine, coefficient):
                return side + coefficient * (around(side) + second(side) + mine - 4.0 * side)

            next_left = next_side(side_left, own[0][part], diff_left)
            next_right = next_side(side_right, own[1][part], diff_right)
            for x in range(-1, width_x + 1):
                row = e0[:, at(x)]
                close = e0[:, at(x - 1)] + e0[:, at(x + 1)] + beside(row, side_left, side_right, x)
                e1[:, at(x)] = row + wide[:, at(x)] * (close - 4.0 * row)
            for x in range(width_x):
                row = e1[:, at(x)]
                close = e1[:, at(x - 1)] + e1[:, at(x + 1)] + beside(row, next_left, next_right, x)
                value = row + wide[:, at(x)] * (close - 4.0 * row)
                span = slice(x * width_y, (x + 1) * width_y)
                both[groups_at(group), span] = value
                both[
                    pl.ds(pl.multiple_of(levels + group * SUBLANES, SUBLANES), SUBLANES), span
                ] = value - load_row(target, group, x, width_x, width_y)
        return carry

    lax.fori_loop(0, levels // (2 * SUBLANES), step, 0)

    def turn(tile, carry):
        span = pl.ds(pl.multiple_of(tile * LANES, LANES), LANES)
        rows[span, :] = both[:, span].T
        return carry

    lax.fori_loop(0, cells // LANES, turn, 0, unroll=2)


def forward(field_rows, target_rows, diff_rows, near, own, sides, sizes):
    levels, width_x, width_y, _, _ = sizes
    cells = width_x * width_y
    extended = (SUBLANES, (width_x + 4) * width_y)
    return pl.pallas_call(
        with_flags(functools.partial(forward_body, levels, width_x, width_y)),
        out_shape=[
            jax.ShapeDtypeStruct((cells, 2 * levels), F32),
            jax.ShapeDtypeStruct(extended, F32),
            jax.ShapeDtypeStruct((6 * SUBLANES, LANES), F32),
        ],
        in_specs=[VMEM] * 9,
        out_specs=[VMEM] * 3,
        scratch_shapes=[
            pltpu.VMEM(extended, F32),
            pltpu.VMEM(extended, F32),
            pltpu.VMEM(extended, F32),
            pltpu.VMEM((2 * levels, cells), F32),
        ],
        compiler_params=params(8),
        cost_estimate=cost(8),
        name="forward",
    )(field_rows, target_rows, diff_rows, *near, *own, *sides)


def index_body(tiles, subs, lead, rows_each, flags, counts, order, out, starts):
    devices = tiles * subs

    def begin(index, total):
        starts[index] = total
        return total + counts[index]

    lax.fori_loop(0, devices, begin, jnp.int32(0))
    half = subs // 2
    mine = flags[3]
    lane = lax.broadcasted_iota(jnp.int32, (SUBLANES, LANES), 1)
    slot = lax.broadcasted_iota(jnp.int32, (SUBLANES, LANES), 0) * LANES + lane

    def expert(block, carry):
        second_half = block // half
        network_id = mine ^ ((block - second_half * half) * 2 + 1 - second_half)
        value = jnp.zeros((SUBLANES, LANES), jnp.int32)
        base = jnp.int32(0)
        for t in range(tiles):
            device = t * subs + network_id
            count = counts[device]
            offset = starts[device] - base + lead
            shift = lax.rem(offset, LANES)
            window = order[pl.ds(lax.div(offset, LANES), SUBLANES), :]
            turned = pltpu.roll(window, lax.rem(LANES - shift, LANES), 1)
            following = jnp.concatenate([turned[1:], turned[:1]], axis=0)
            moved = jnp.where(lane < LANES - shift, turned, following)
            value = jnp.where((slot >= base) & (slot < base + count), moved, value)
            base = base + count
        out[pl.ds(block * rows_each, rows_each), :] = value[:rows_each]
        return carry

    lax.fori_loop(0, subs, expert, 0)


def slot_cells(counts, column_order, sizes):
    _, width_x, width_y, tiles, subs = sizes
    cells = width_x * width_y
    packet = cells // subs
    rows_each = packet // LANES
    lead = packet
    order = jnp.pad(column_order, (lead, SUBLANES * LANES)).reshape(-1, LANES)
    return pl.pallas_call(
        with_flags(functools.partial(index_body, tiles, subs, lead, rows_each)),
        out_shape=jax.ShapeDtypeStruct((cells // LANES, LANES), jnp.int32),
        in_specs=[SMEM] + [VMEM],
        out_specs=VMEM,
        scratch_shapes=[pltpu.SMEM((tiles * subs,), jnp.int32)],
        compiler_params=params(4),
        cost_estimate=cost(2),
        name="slot_cells",
    )(counts, order).reshape(subs, 1, packet)


def widen(value):
    missing = LANES - value.shape[1]
    return jnp.concatenate([value, jnp.zeros((value.shape[0], missing), value.dtype)], axis=1)


def lower_half(rows):
    return lax.broadcasted_iota(jnp.int32, (rows, LANES), 1) < LANES // 2


def swap_halves(value):
    return pltpu.roll(value, LANES // 2, 1)


def squeeze_rows(value):
    count = value.shape[0] // 2
    return jnp.where(lower_half(count), value[:count], swap_halves(value[count:]))


def pack_rows(put, inner, first, last, biases):
    width = first.shape[1]
    for k in range(3):
        put(inner[k][:, :LANES])
    low = lower_half(width)
    put(jnp.where(low, widen(inner[0][:, LANES:]), swap_halves(widen(inner[1][:, LANES:]))))
    put(jnp.where(low, widen(inner[2][:, LANES:]), last))
    put(first[:, :LANES])
    put(squeeze_rows(widen(first[:, LANES:])))
    tail = []
    for bias, bias_last in biases:
        tail += [piece[:, :LANES] for piece in bias]
        tail += [
            jnp.where(
                lower_half(1), widen(bias[k][:, LANES:]), swap_halves(widen(bias[k + 1][:, LANES:]))
            )
            for k in (0, 2)
        ]
        tail.append(bias_last)
    return tail


def pack_size(levels, width, tiles):
    rows = 5 * width + levels + levels // 2 + 16
    unit = 16 * tiles
    return (rows + unit - 1) // unit * unit


def weights_body(*refs):
    sources, out, targets, semaphores = refs[:5], refs[5], refs[6:11], refs[11]
    wait_all(load_all(sources, targets, semaphores))
    w_first, w_inner, w_last, b_inner, b_last = targets
    row = 0

    def put(value):
        nonlocal row
        out[row : row + value.shape[0], :] = value.astype(BF16)
        row += value.shape[0]

    bias = b_inner[...]
    bias_last = swap_halves(widen(b_last[...]))
    bias_high = bias.astype(BF16).astype(F32)
    last_high = bias_last.astype(BF16).astype(F32)
    bias_low = bias - bias_high
    last_low = bias_last - last_high
    tail = pack_rows(
        put,
        [w_inner[k].astype(F32) for k in range(3)],
        w_first[...].astype(F32),
        swap_halves(widen(w_last[...].astype(F32).T)),
        [
            ([bias_high[k : k + 1] for k in range(4)], last_high),
            ([bias_low[k : k + 1] for k in range(4)], last_low),
        ],
    )
    tail.append(jnp.zeros((out.shape[0] - row - len(tail), LANES), F32))
    put(jnp.concatenate(tail, axis=0))


def pack_weights(w_first, w_inner, w_last, b_inner, b_last, tiles):
    levels, width = w_first.shape
    operands = (w_first, w_inner, w_last.T, b_inner, b_last)
    return pl.pallas_call(
        weights_body,
        out_shape=jax.ShapeDtypeStruct((pack_size(levels, width, tiles), LANES), BF16),
        in_specs=[pl.BlockSpec(memory_space=pltpu.HBM)] * 5,
        out_specs=VMEM,
        scratch_shapes=buffers(operands) + [pltpu.SemaphoreType.DMA((5,))],
        compiler_params=params(62),
        cost_estimate=cost(1),
        name="pack_weights",
    )(*operands)


def network_body(
    levels, width, packet, carried_in,
    behind, ahead, pack_list, rows, back, grads, taken, given_back, packs, first_in, first_out, inner, last, last_half,
    kept, feeds, slopes, residues,
):
    block = pl.program_id(0)
    blocks = pl.num_programs(0)
    narrow = width - LANES
    wide = 2 * LANES
    half = packet // 2

    def fetch(cells_of, first_slot, count):
        for u in range(first_slot, first_slot + count):
            taken[u : u + 1, :] = rows[pl.ds(cells_of[0, 0, u], 1), :]

    def deliver(cells_of, first_slot, count):
        for u in range(first_slot, first_slot + count):
            back[pl.ds(cells_of[0, 0, u], 1), :] = given_back[u : u + 1, :]

    @pl.when(block == 0)
    def _():
        if carried_in is None:
            fetch(behind, 0, packet)
        else:
            taken[...] = carried_in[0][...]
            given_back[...] = carried_in[1][...]
        first_in[levels:, :] = jnp.zeros((wide - levels, wide), BF16)
        first_out[...] = jnp.zeros((LANES, wide), BF16)
        first_in[:levels, LANES:] = jnp.zeros((levels, LANES), BF16)
        inner[:, :, LANES:] = jnp.zeros((3, wide, LANES), BF16)
        inner[:, width:, :] = jnp.zeros((3, wide - width, wide), BF16)
        last[...] = jnp.zeros((wide, LANES), BF16)
        last_half[...] = jnp.zeros((wide, LANES), BF16)

    for index, source in enumerate(pack_list):

        @pl.when(block == index)
        def _():
            packs[...] = source[...]

    row = 0

    def take(size):
        nonlocal row
        value = packs[row : row + size, :].astype(F32)
        row += size
        return value

    def halves(value):
        return value[:, :narrow], swap_halves(value)[:, :narrow]

    for k in range(3):
        inner[k, :width, :LANES] = (0.5 * take(width)).astype(BF16)
    narrow_a, narrow_b = halves(0.5 * take(width))
    inner[0, :width, LANES:width] = narrow_a.astype(BF16)
    inner[1, :width, LANES:width] = narrow_b.astype(BF16)
    mixed = take(width)
    inner[2, :width, LANES:width] = (0.5 * mixed[:, :narrow]).astype(BF16)
    out_weight = jnp.where(lower_half(width), 0.0, mixed)
    last[:width, :] = out_weight.astype(BF16)
    last_half[:width, :] = (0.5 * out_weight).astype(BF16)
    wide_first = take(levels)
    narrow_a, narrow_b = halves(take(levels // 2))
    half_levels = levels // 2
    first_in[:levels, :LANES] = (0.5 * wide_first).astype(BF16)
    first_in[:half_levels, LANES:width] = (0.5 * narrow_a).astype(BF16)
    first_in[half_levels:levels, LANES:width] = (0.5 * narrow_b).astype(BF16)
    first_out[levels:, :LANES] = wide_first.astype(BF16)
    first_out[levels : levels + half_levels, LANES:width] = narrow_a.astype(BF16)
    first_out[levels + half_levels :, LANES:width] = narrow_b.astype(BF16)
    tail = take(16)

    spare_lane = lax.broadcasted_iota(jnp.int32, (1, LANES), 1) - narrow
    spare = (spare_lane == 0) | (spare_lane == 1)

    def bias_rows(k):
        parts = []
        for base in (0, 7):
            mixed = 0.5 * tail[base + 4 + k // 2 : base + 5 + k // 2]
            side = mixed if k % 2 == 0 else swap_halves(mixed)
            side = jnp.where(lower_half(1), side, 0.0)
            side = jnp.where(spare, UNIT_INPUT[0] if base == 0 else UNIT_INPUT[1], side)
            parts.append(jnp.concatenate([0.5 * tail[base + k : base + k + 1], side], axis=1))
        parts.append(jnp.zeros((14, wide), F32))
        return jnp.concatenate(parts, axis=0).astype(BF16)

    first_in[LANES : LANES + 16, :] = bias_rows(0)
    for k in range(3):
        inner[k, width : width + 16, :] = bias_rows(k + 1)
    last[width : width + 16, :] = jnp.concatenate(
        [tail[6:7], tail[13:14], jnp.zeros((14, LANES), F32)], axis=0
    ).astype(BF16)

    over_rows = (((0,), (0,)), ((), ()))
    over_lanes = (((1,), (1,)), ((), ()))
    sides = (0, 1)
    lower = lower_half(half)
    ones = jnp.ones((half, LANES), BF16)

    def span(side):
        return slice(side * half, (side + 1) * half)

    for side in sides:
        kept[span(side), :] = taken[span(side), :].astype(BF16)

    def layers(chosen, current, delivered, share):
        for k in chosen:
            for side in sides:
                weight = first_in[...] if k == 0 else inner[k - 1]
                u = jnp.dot(current[side], weight, preferred_element_type=F32)
                turn = jnp.tanh(u)
                plus = 1.0 + turn
                active = u * plus
                slopes[k, span(side), :] = plus
                current[side] = active.astype(BF16)
                feeds[k, span(side), :] = current[side]
                deliver(behind, delivered, share)
                delivered += share
        return current

    layers(
        (0, 1), [jnp.concatenate([kept[span(side), :], ones], axis=1) for side in sides], 0, packet // 8
    )

    def second_part():
        current = layers((2, 3), [feeds[1, span(side), :] for side in sides], packet // 2, packet // 8)
        for side in sides:
            output = jnp.dot(current[side], last[...], preferred_element_type=F32)
            residues[span(side), :] = jnp.where(
                lower, 0.0, kept[span(side), :].astype(F32) + output
            )

    second_part()

    def third_part():
        fetched = 0
        share = packet // 10
        errors = [residues[span(side), :].astype(BF16) for side in sides]

        def weight_grad(k):
            products = []
            for side in sides:
                if k == 0:
                    feed = jnp.concatenate([kept[span(side), :], ones], axis=1)[:, : LANES + 16]
                else:
                    feed = feeds[k - 1, span(side), : width + 16]
                products.append(
                    lax.dot_general(feed, errors[side], over_rows, preferred_element_type=F32)
                )
            return products[0] + products[1]

        grad_sums = [None] * 5
        carried = [
            lax.dot_general(errors[side], last_half[...], over_lanes, preferred_element_type=F32)
            for side in sides
        ]
        grad_sums[4] = weight_grad(4)
        for k in (3, 2, 1, 0):
            for side in sides:
                plus = slopes[k, span(side), :]
                slope = plus + feeds[k, span(side), :].astype(F32) * (2.0 - plus)
                errors[side] = (carried[side] * slope).astype(BF16)
                weight = inner[k - 1] if k > 0 else first_out[...]
                carried[side] = lax.dot_general(
                    errors[side], weight, over_lanes, preferred_element_type=F32
                )
                fetch(ahead, fetched, share)
                fetched += share
            grad_sums[k] = weight_grad(k)
        fetch(ahead, fetched, packet - fetched)
        for side in sides:
            given_back[span(side), :] = residues[span(side), :] + carried[side]

        filled = 0

        def put(value):
            nonlocal filled
            grads[0, filled : filled + value.shape[0], :] = value.astype(BF16)
            filled += value.shape[0]

        tail = pack_rows(
            put,
            [grad_sums[k][:width, :width] for k in (1, 2, 3)],
            grad_sums[0][:levels, :width],
            grad_sums[4][:width],
            [
                (
                    [grad_sums[0][LANES : LANES + 1, :width]]
                    + [grad_sums[k][width : width + 1, :width] for k in (1, 2, 3)],
                    grad_sums[4][width : width + 1],
                )
            ],
        )
        tail.append(jnp.zeros((grads.shape[1] - filled - len(tail), LANES), F32))
        put(jnp.concatenate(tail, axis=0))

    third_part()
    if carried_in is not None:

        @pl.when(block == blocks - 1)
        def _():
            deliver(ahead, 0, packet)


def network(cells_of, pack_list, rows, before, shift, levels, width, subs):
    cells, doubled = rows.shape
    packet = cells // subs
    blocks = len(pack_list)
    pack_shape = pack_list[0].shape
    final = before is not None
    limit = blocks - 1 if final else blocks
    wide = 2 * LANES

    def body(behind, ahead, *refs):
        names, rest = refs[:blocks], refs[blocks + 1 :]
        carried_in = None
        if final:
            carried_in, rest = rest[1:3], rest[3:]
        network_body(
            levels, width, packet, carried_in, behind, ahead, names, refs[blocks], *rest
        )

    operands = [cells_of, cells_of, *pack_list, rows]
    in_specs = [
        pl.BlockSpec(
            (1, 1, packet),
            lambda i: (jnp.maximum(i - 1 + shift, 0), 0, 0),
            memory_space=pltpu.SMEM,
        ),
        pl.BlockSpec(
            (1, 1, packet),
            lambda i: (jnp.minimum(i + 1, limit) + shift, 0, 0),
            memory_space=pltpu.SMEM,
        ),
    ] + [VMEM] * (blocks + 1)
    aliases = {}
    held = [jax.ShapeDtypeStruct((packet, doubled), F32)] * 2
    scratch = []
    if final:
        aliases = {len(operands): 0}
        operands += list(before)
        in_specs += [VMEM] * 3
        scratch = [pltpu.VMEM((packet, doubled), F32)] * 2
        held = []
    return pl.pallas_call(
        body,
        grid=(blocks,),
        out_shape=[
            jax.ShapeDtypeStruct((cells, doubled), F32),
            jax.ShapeDtypeStruct((blocks, *pack_shape), BF16),
        ]
        + held,
        in_specs=in_specs,
        out_specs=[VMEM, pl.BlockSpec((1, *pack_shape), lambda i: (i, 0, 0))] + [VMEM] * len(held),
        scratch_shapes=scratch
        + [
            pltpu.VMEM(pack_shape, BF16),
            pltpu.VMEM((wide, wide), BF16),
            pltpu.VMEM((LANES, wide), BF16),
            pltpu.VMEM((3, wide, wide), BF16),
            pltpu.VMEM((wide, LANES), BF16),
            pltpu.VMEM((wide, LANES), BF16),
            pltpu.VMEM((packet, LANES), BF16),
            pltpu.VMEM((4, packet, wide), BF16),
            pltpu.VMEM((4, packet, wide), F32),
            pltpu.VMEM((packet, LANES), F32),
        ],
        input_output_aliases=aliases,
        compiler_params=params(24),
        cost_estimate=cost(12),
        name="network",
    )(*operands)


def add_body(first, other, *outs):
    for index, out in enumerate(outs):
        out[...] = (first[index].astype(F32) + other[index].astype(F32)).astype(BF16)


def add_pair(first, other):
    return pl.pallas_call(
        add_body,
        out_shape=[jax.ShapeDtypeStruct(first.shape[1:], BF16)] * first.shape[0],
        in_specs=[VMEM] * 2,
        out_specs=[VMEM] * first.shape[0],
        compiler_params=params(8),
        cost_estimate=cost(1),
        name="add_pair",
    )(first, other)


def total_of(parts):
    total = parts[0][...].astype(F32)
    for part in parts[1:]:
        total = total + part[...].astype(F32)
    return total.astype(BF16)


def share_body(count, flags, *refs):
    parts, outs, whole = refs[:count], refs[count:-1], refs[-1]
    whole[...] = total_of(parts).astype(F32)
    rows = outs[0].shape[0]
    for offset, out in enumerate(outs):
        start = pl.multiple_of((flags[2] ^ offset) * rows, 16)
        out[...] = whole[pl.ds(start, rows), :].astype(BF16)


def sum_and_share(parts, tiles):
    rows = parts[0].shape[0]
    return pl.pallas_call(
        with_flags(functools.partial(share_body, len(parts))),
        out_shape=[jax.ShapeDtypeStruct((rows // tiles, LANES), BF16)] * tiles,
        in_specs=[VMEM] * len(parts),
        out_specs=[VMEM] * tiles,
        scratch_shapes=[pltpu.VMEM((rows, LANES), F32)],
        compiler_params=params(8),
        cost_estimate=cost(1),
        name="sum_and_share",
    )(*parts)


def sum_body(*refs):
    refs[-1][...] = total_of(refs[:-1])


def sum_parts(parts):
    return pl.pallas_call(
        sum_body,
        out_shape=jax.ShapeDtypeStruct(parts[0].shape, BF16),
        in_specs=[VMEM] * len(parts),
        out_specs=VMEM,
        compiler_params=params(8),
        cost_estimate=cost(1),
        name="sum_parts",
    )(*parts)


def steps_body(levels, width, count, tiles, flags, *refs):
    parts, (first, inner, last, bias, bias_last, whole) = refs[:tiles], refs[tiles:]
    share = parts[0].shape[0]
    for offset, part in enumerate(parts):
        whole[pl.ds(pl.multiple_of((flags[2] ^ offset) * share, 16), share), :] = part[...]

    def squares(index, total):
        part = whole[pl.ds(pl.multiple_of(index * 16, 16), 16), :].astype(F32)
        return total + part * part

    total = lax.fori_loop(0, whole.shape[0] // 16, squares, jnp.zeros((16, LANES), F32), unroll=4)
    factor = 1.0 / jnp.sqrt(jnp.broadcast_to(jnp.sum(total), (1, LANES)) / count + 1e-06)
    row = 0

    def take(size):
        nonlocal row
        value = whole[row : row + size, :].astype(F32) * factor
        row += size
        return value

    half = LANES // 2
    for k in range(3):
        inner[k, :, :LANES] = take(width)
    narrow = take(width)
    inner[0, :, LANES:] = narrow[:, :half]
    inner[1, :, LANES:] = swap_halves(narrow)[:, :half]
    narrow = take(width)
    inner[2, :, LANES:] = narrow[:, :half]
    last[...] = swap_halves(narrow).T[:half]
    first[:, :LANES] = take(levels)
    narrow = take(levels // 2)
    first[: levels // 2, LANES:] = narrow[:, :half]
    first[levels // 2 :, LANES:] = swap_halves(narrow)[:, :half]
    tail = take(16)
    bias[:, :LANES] = tail[0:4]
    for k in (0, 2):
        pair = tail[4 + k // 2 : 5 + k // 2]
        bias[k : k + 1, LANES:] = pair[:, :half]
        bias[k + 1 : k + 2, LANES:] = swap_halves(pair)[:, :half]
    bias_last[...] = swap_halves(tail[6:7])[:, :half]


def make_steps(parts, levels, width):
    count = 2 * levels * width + 3 * width * width + 4 * width + levels
    return pl.pallas_call(
        with_flags(functools.partial(steps_body, levels, width, float(count), len(parts))),
        out_shape=[
            jax.ShapeDtypeStruct((levels, width), F32),
            jax.ShapeDtypeStruct((3, width, width), F32),
            jax.ShapeDtypeStruct((levels, width), F32),
            jax.ShapeDtypeStruct((4, width), F32),
            jax.ShapeDtypeStruct((1, levels), F32),
        ],
        in_specs=[VMEM] * len(parts),
        out_specs=[VMEM] * 5,
        scratch_shapes=[pltpu.VMEM((len(parts) * parts[0].shape[0], LANES), BF16)],
        compiler_params=params(8),
        cost_estimate=cost(2),
        name="make_steps",
    )(*parts)


def collect_body(levels, width_x, width_y, flags, rows, grid, first, other):
    cells = width_x * width_y

    def turn(tile, carry):
        span = pl.ds(pl.multiple_of(tile * LANES, LANES), LANES)
        grid[:, span] = rows[span, :].T[levels:].astype(BF16).astype(F32)
        return carry

    lax.fori_loop(0, cells // LANES, turn, 0, unroll=2)

    def step(double, carry):
        store_rows(
            pairs_at(double),
            lambda which, x: grid[groups_at(double * 2 + which), x * width_y : (x + 1) * width_y],
            width_x, width_y, flags[0], first, other,
        )
        return carry

    lax.fori_loop(0, levels // (2 * SUBLANES), step, 0)


def collect(rows, sizes):
    levels, width_x, width_y, _, _ = sizes
    cells = width_x * width_y
    shape = jax.ShapeDtypeStruct((levels, 2 * width_y), BF16)
    return pl.pallas_call(
        with_flags(functools.partial(collect_body, levels, width_x, width_y)),
        out_shape=[jax.ShapeDtypeStruct((levels, cells), F32), shape, shape],
        in_specs=[VMEM],
        out_specs=[VMEM] * 3,
        compiler_params=params(8),
        cost_estimate=cost(3),
        name="collect",
    )(rows)


def adjoint_body(
    levels, width_x, width_y,
    flags, grid, wide, rate_sides, near, far, own_near, own_far, side_near, side_far, out, flow, e1,
):
    y_tiles = width_y // LANES
    stride = width_x * y_tiles

    def at(x):
        return slice((x + 2) * width_y, (x + 3) * width_y)

    rate_left, rate_right, outer_left, outer_right, mine_left, mine_right = [
        rate_sides[index * SUBLANES : (index + 1) * SUBLANES, :] for index in range(6)
    ]

    def step(double, carry):
        where = pairs_at(double)
        sides = split_sides(flags[1], side_near, side_far, where)
        owns = split_sides(flags[1], own_near, own_far, where)
        for which in range(2):
            group = double * 2 + which
            own = groups_at(group)
            part = slice(which * SUBLANES, (which + 1) * SUBLANES)

            def next_side(side, rate, outer_rate, mine, mine_rate):
                product = side * rate
                return product, side + (
                    around(product) + second(side) * outer_rate + mine * mine_rate - 4.0 * product
                )

            flow_left, next_left = next_side(
                sides[0][part], rate_left, outer_left, owns[0][part], mine_left
            )
            flow_right, next_right = next_side(
                sides[1][part], rate_right, outer_right, owns[1][part], mine_right
            )

            def value(x):
                if 0 <= x < width_x:
                    return grid[own, x * width_y : (x + 1) * width_y]
                return outer_row(flags[0], near, far, where, which, x, width_x, width_y)

            for x in range(-2, width_x + 2):
                flow[:, at(x)] = value(x) * wide[:, at(x)]
            for x in range(-1, width_x + 1):
                row = flow[:, at(x)]
                close = flow[:, at(x - 1)] + flow[:, at(x + 1)]
                close = close + beside(row, flow_left, flow_right, x)
                e1[:, at(x)] = value(x) + close - 4.0 * row
            for x in range(-1, width_x + 1):
                flow[:, at(x)] = e1[:, at(x)] * wide[:, at(x)]
            flow_left = next_left * rate_left
            flow_right = next_right * rate_right
            for x in range(width_x):
                row = flow[:, at(x)]
                close = flow[:, at(x - 1)] + flow[:, at(x + 1)]
                close = close + beside(row, flow_left, flow_right, x)
                result = e1[:, at(x)] + close - 4.0 * row
                for y_tile in range(y_tiles):
                    offset = group * (SUBLANES * stride) + row_offset(x, y_tile, y_tiles)
                    out[pl.ds(offset, SUBLANES, stride=stride), :] = result[
                        :, y_tile * LANES : (y_tile + 1) * LANES
                    ]
        return carry

    lax.fori_loop(0, levels // (2 * SUBLANES), step, 0)


def adjoint(grid, rates, rate_sides, near, own, sides, sizes):
    levels, width_x, width_y, _, _ = sizes
    extended = (SUBLANES, (width_x + 4) * width_y)
    return pl.pallas_call(
        with_flags(functools.partial(adjoint_body, levels, width_x, width_y)),
        out_shape=jax.ShapeDtypeStruct((levels * width_x * width_y // LANES, LANES), F32),
        in_specs=[VMEM] * 9,
        out_specs=VMEM,
        scratch_shapes=[pltpu.VMEM(extended, F32), pltpu.VMEM(extended, F32)],
        compiler_params=params(8),
        cost_estimate=cost(6),
        name="adjoint",
    )(grid, rates, rate_sides, *near, *own, *sides)


def local_program(
    initial, targets, diffusivity, column_order, send_counts,
    w_first, w_inner, w_last, b_inner, b_last,
):
    levels, width_x, width_y = initial.shape
    tiles, subs = lax.axis_size("tile"), lax.axis_size("sub")
    sizes = (levels, width_x, width_y, tiles, subs)
    field_rows = tile_rows(initial)
    target_rows = tile_rows(targets)
    diff_rows = tile_rows(diffusivity[None])
    width = w_first.shape[2]
    half = subs // 2
    area = (levels, width_x, width_y)

    first, other = pack_rows_out(field_rows, diff_rows, *area)
    weights = pack_weights(w_first[0], w_inner[0], w_last[0], b_inner[0], b_last, tiles)
    own_weights = [weights] + [
        lax.ppermute(weights, "sub", partners(subs, 2 * c)) for c in range(1, half)
    ]
    near = trade_sides(first, other, "tile")
    cells_of = slot_cells(send_counts[0], column_order[0], sizes)
    own = pack_columns_out(field_rows, diff_rows, *area)
    own = add_corners(*near, *own, width_x, width_y)
    sides = trade_sides(*own, "sub")
    other_weights = [lax.ppermute(pack, "sub", partners(subs, 1)) for pack in own_weights]
    rows, rates, rate_sides = forward(field_rows, target_rows, diff_rows, near, own, sides, sizes)
    back, other_grads, taken, given_back = network(
        cells_of, other_weights, rows, None, 0, levels, width, subs
    )
    partner_grads = lax.ppermute(other_grads, "sub", partners(subs, 1))
    back, own_grads = network(
        cells_of, own_weights, rows, (back, taken, given_back), half,
        levels, width, subs,
    )
    both_grads = add_pair(own_grads, partner_grads)
    arrived = [both_grads[0]] + [
        lax.ppermute(both_grads[c], "sub", partners(subs, 2 * c)) for c in range(1, half)
    ]
    grid, g_first, g_other = collect(back, sizes)
    g_near = trade_sides(g_first, g_other, "tile")
    g_own = pack_columns_back(grid, *area)
    g_own = add_corners(*g_near, *g_own, width_x, width_y)
    g_sides = trade_sides(*g_own, "sub")
    shares = sum_and_share(arrived, tiles)
    mine = [shares[0]] + [
        lax.ppermute(shares[d], "tile", partners(tiles, d)) for d in range(1, tiles)
    ]
    result = adjoint(grid, rates, rate_sides, g_near, g_own, g_sides, sizes)
    piece = sum_parts(mine)
    pieces = [piece] + [lax.ppermute(piece, "tile", partners(tiles, d)) for d in range(1, tiles)]
    steps = make_steps(pieces, levels, width)
    return (
        untile_rows(result, levels, width_x, width_y),
        steps[0][None], steps[1][None], steps[2].T[None], steps[3][None], steps[4],
    )


def solution(mesh):
    placed = (
        P(None, "tile", "sub"),
        P(None, "tile", "sub"),
        P("tile", "sub"),
        P(("tile", "sub"), None),
        P(("tile", "sub"), None),
        P("sub", None, None),
        P("sub", None, None, None),
        P("sub", None, None),
        P("sub", None, None),
        P("sub", None),
    )
    return jax.shard_map(
        local_program,
        mesh=mesh,
        in_specs=placed,
        out_specs=(
            P(None, "tile", "sub"),
            P("sub", None, None),
            P("sub", None, None, None),
            P("sub", None, None),
            P("sub", None, None),
            P("sub", None),
        ),
        check_vma=False,
    )
```

```python
import functools
import jax
import jax.numpy as jnp
from jax import lax
from jax.experimental import pallas as pl
from jax.experimental.pallas import tpu as pltpu
from jax.sharding import PartitionSpec as P

LANES = 128
SUBLANES = 8
SECOND = 32
UNIT_INPUT = (0.640625, -0.00139273)
VMEM = pl.BlockSpec(memory_space=pltpu.VMEM)
ANY = pl.BlockSpec(memory_space=pl.ANY)
SMEM = pl.BlockSpec(memory_space=pltpu.SMEM)


def params(mebibytes):
    return pltpu.CompilerParams(vmem_limit_bytes=mebibytes * 1024 * 1024)


def cost(microseconds):
    moved = int(microseconds * 3e6)
    return pl.CostEstimate(flops=0, transcendentals=0, bytes_accessed=moved)


F32 = jnp.float32
BF16 = jnp.bfloat16


def with_flags(body):
    def inner(*refs):
        tile, sub = lax.axis_index("tile"), lax.axis_index("sub")
        return body((tile & 1, sub & 1, tile, sub), *refs)

    return inner


def load_all(sources, targets, semaphores, first=0):
    copies = [
        pltpu.make_async_copy(source, target, semaphores.at[first + index])
        for index, (source, target) in enumerate(zip(sources, targets))
    ]
    for copy in copies:
        copy.start()
    return copies


def wait_all(copies):
    for copy in copies:
        copy.wait()


def buffers(operands):
    return [pltpu.VMEM(operand.shape, operand.dtype) for operand in operands]


def tile_rows(cells):
    levels, width_x, width_y = cells.shape
    split = cells.reshape(levels, width_x // SUBLANES, SUBLANES, width_y // LANES, LANES)
    return split.transpose(0, 1, 3, 2, 4).reshape(-1, LANES)


def untile_rows(rows, levels, width_x, width_y):
    split = rows.reshape(levels, width_x // SUBLANES, width_y // LANES, SUBLANES, LANES)
    return split.transpose(0, 1, 3, 2, 4).reshape(levels, width_x, width_y)


def row_offset(x, y_tile, y_tiles):
    return (x // SUBLANES * y_tiles + y_tile) * SUBLANES + x % SUBLANES


def load_row(ref, group, x, width_x, width_y):
    y_tiles = width_y // LANES
    stride = width_x * y_tiles
    base = group * (SUBLANES * stride)
    return jnp.concatenate(
        [
            ref[pl.ds(base + row_offset(x, y_tile, y_tiles), SUBLANES, stride=stride), :]
            for y_tile in range(y_tiles)
        ],
        axis=1,
    )


def load_wide(ref, x, width_y):
    y_tiles = width_y // LANES
    return jnp.concatenate(
        [
            jnp.broadcast_to(ref[pl.ds(row_offset(x, y_tile, y_tiles), 1), :], (SUBLANES, LANES))
            for y_tile in range(y_tiles)
        ],
        axis=1,
    )


def lane_ids(width):
    return lax.broadcasted_iota(jnp.int32, (SUBLANES, width), 1)


def groups_at(group):
    return pl.ds(pl.multiple_of(group * SUBLANES, SUBLANES), SUBLANES)


def pairs_at(double):
    return pl.ds(pl.multiple_of(double * 2 * SUBLANES, 2 * SUBLANES), 2 * SUBLANES)


def two(parts):
    return jnp.concatenate(parts, axis=0).astype(BF16)


def store_rows(where, row_of, width_x, width_y, flag, first, other):
    for k in range(2):
        span = slice(k * width_y, (k + 1) * width_y)
        top = two([row_of(which, k) for which in range(2)])
        bottom = two([row_of(which, width_x - 2 + k) for which in range(2)])
        first[where, span] = jnp.where(flag == 0, bottom.astype(F32), top.astype(F32)).astype(BF16)
        other[where, span] = jnp.where(flag == 0, top.astype(F32), bottom.astype(F32)).astype(BF16)


def store_columns(where, row_of, width_x, width_y, flag, first, other):
    lane = lane_ids(LANES)
    lows, highs = [], []
    for which in range(2):
        low = jnp.zeros((SUBLANES, LANES), F32)
        high = jnp.zeros((SUBLANES, LANES), F32)
        for x in range(width_x):
            row = row_of(which, x)
            low = jnp.where(lane == 1 + x, row[:, 0:1], low)
            high = jnp.where(lane == 1 + x, row[:, width_y - 1 : width_y], high)
            low = jnp.where(lane == SECOND + 1 + x, row[:, 1:2], low)
            high = jnp.where(lane == SECOND + 1 + x, row[:, width_y - 2 : width_y - 1], high)
        lows.append(low)
        highs.append(high)
    low = jnp.concatenate(lows, axis=0)
    high = jnp.concatenate(highs, axis=0)
    first[where, :] = jnp.where(flag == 0, high, low).astype(BF16)
    other[where, :] = jnp.where(flag == 0, low, high).astype(BF16)


def row_pack_body(levels, width_x, width_y, flags, field, diff, first, other):
    def step(double, carry):
        store_rows(
            pairs_at(double),
            lambda which, x: load_row(field, double * 2 + which, x, width_x, width_y),
            width_x, width_y, flags[0], first, other,
        )
        return carry

    lax.fori_loop(0, levels // (2 * SUBLANES), step, 0)
    store_rows(
        pl.ds(levels, 2 * SUBLANES), lambda which, x: load_wide(diff, x, width_y),
        width_x, width_y, flags[0], first, other,
    )


def pack_rows_out(field_rows, diff_rows, levels, width_x, width_y):
    shape = jax.ShapeDtypeStruct((levels + 2 * SUBLANES, 2 * width_y), BF16)
    return pl.pallas_call(
        with_flags(functools.partial(row_pack_body, levels, width_x, width_y)),
        out_shape=[shape] * 2,
        in_specs=[VMEM] * 2,
        out_specs=[VMEM] * 2,
        compiler_params=params(8),
        cost_estimate=cost(8),
        name="pack_rows",
    )(field_rows, diff_rows)


def outer_row(flag, first, other, where, which, x, width_x, width_y):
    even, odd = (other, first) if x < 0 else (first, other)
    start = (x + 2 if x < 0 else x - width_x) * width_y
    span = slice(start, start + width_y)
    value = jnp.where(flag == 0, even[where, span].astype(F32), odd[where, span].astype(F32))
    return value[which * SUBLANES : (which + 1) * SUBLANES]


def column_pack_body(levels, width_x, width_y, flags, field, diff, first, other):
    def step(double, carry):
        store_columns(
            pairs_at(double),
            lambda which, x: load_row(field, double * 2 + which, x, width_x, width_y),
            width_x, width_y, flags[1], first, other,
        )
        return carry

    lax.fori_loop(0, levels // (2 * SUBLANES), step, 0)
    store_columns(
        pl.ds(levels, 2 * SUBLANES), lambda which, x: load_wide(diff, x, width_y),
        width_x, width_y, flags[1], first, other,
    )


def pack_columns_out(field_rows, diff_rows, levels, width_x, width_y):
    shape = jax.ShapeDtypeStruct((levels + 2 * SUBLANES, LANES), BF16)
    return pl.pallas_call(
        with_flags(functools.partial(column_pack_body, levels, width_x, width_y)),
        out_shape=[shape] * 2,
        in_specs=[VMEM] * 2,
        out_specs=[VMEM] * 2,
        compiler_params=params(8),
        cost_estimate=cost(2),
        name="pack_columns",
    )(field_rows, diff_rows)


def back_pack_body(levels, width_x, width_y, flags, grid, first, other):
    def step(double, carry):
        store_columns(
            pairs_at(double),
            lambda which, x: grid[groups_at(double * 2 + which), x * width_y : (x + 1) * width_y],
            width_x, width_y, flags[1], first, other,
        )
        return carry

    lax.fori_loop(0, levels // (2 * SUBLANES), step, 0)


def pack_columns_back(grid, levels, width_x, width_y):
    shape = jax.ShapeDtypeStruct((levels, LANES), BF16)
    return pl.pallas_call(
        with_flags(functools.partial(back_pack_body, levels, width_x, width_y)),
        out_shape=[shape] * 2,
        in_specs=[VMEM],
        out_specs=[VMEM] * 2,
        compiler_params=params(8),
        cost_estimate=cost(2),
        name="pack_back",
    )(grid)


def corner_body(width_x, width_y, flags, near, far, first_in, other_in, first, other):
    rows = near.shape[0]
    lane = lax.broadcasted_iota(jnp.int32, (rows, LANES), 1)
    near_value = near[...].astype(F32)
    far_value = far[...].astype(F32)
    above = jnp.where(flags[0] == 0, far_value[:, width_y:], near_value[:, width_y:])
    below = jnp.where(flags[0] == 0, near_value[:, :width_y], far_value[:, :width_y])

    def insert(given, edge_of):
        value = given[...].astype(F32)
        value = jnp.where(lane == 0, edge_of(above), value)
        return jnp.where(lane == width_x + 1, edge_of(below), value).astype(BF16)

    def low(row):
        return row[:, 0:1]

    def high(row):
        return row[:, width_y - 1 : width_y]

    first[...] = insert(first_in, lambda row: jnp.where(flags[1] == 0, high(row), low(row)))
    other[...] = insert(other_in, lambda row: jnp.where(flags[1] == 0, low(row), high(row)))


def add_corners(near, far, first, other, width_x, width_y):
    shape = jax.ShapeDtypeStruct(first.shape, BF16)
    return pl.pallas_call(
        with_flags(functools.partial(corner_body, width_x, width_y)),
        out_shape=[shape] * 2,
        in_specs=[VMEM] * 4,
        out_specs=[VMEM] * 2,
        compiler_params=params(8),
        cost_estimate=cost(1),
        name="add_corners",
    )(near, far, first, other)


def partners(size, offset):
    return [(i, i ^ offset) for i in range(size)]


def beyond(size):
    return [(i, (i - 1) % size if i % 2 == 0 else (i + 1) % size) for i in range(size)]


def trade_sides(first, other, axis):
    size = lax.axis_size(axis)
    return (lax.ppermute(first, axis, partners(size, 1)), lax.ppermute(other, axis, beyond(size)))


def around(side):
    return pltpu.roll(side, 1, 1) + pltpu.roll(side, LANES - 1, 1)


def second(side):
    return pltpu.roll(side, LANES - SECOND, 1)


def beside(row, left, right, x):
    width = row.shape[1]
    lane = lane_ids(LANES)
    before = pltpu.roll(row, 1, 1)
    after = pltpu.roll(row, width - 1, 1)
    first = jnp.where(lane == 0, pltpu.roll(left, (LANES - 1 - x) % LANES, 1), before[:, :LANES])
    final = jnp.where(
        lane == LANES - 1, pltpu.roll(right, LANES - 2 - x, 1), after[:, width - LANES :]
    )
    return jnp.concatenate([first, before[:, LANES:]], axis=1) + jnp.concatenate(
        [after[:, : width - LANES], final], axis=1
    )


def split_sides(flag, first, other, where):
    near = first[where, :].astype(F32)
    far = other[where, :].astype(F32)
    return jnp.where(flag == 0, far, near), jnp.where(flag == 0, near, far)


def forward_body(
    levels, width_x, width_y,
    flags, field, target, diff, near, far, own_near, own_far, side_near, side_far,
    rows, rates, rate_sides, e0, e1, wide, both,
):
    cells = width_x * width_y

    def at(x):
        return slice((x + 2) * width_y, (x + 3) * width_y)

    last = pl.ds(levels, 2 * SUBLANES)
    for x in range(width_x):
        wide[:, at(x)] = load_wide(diff, x, width_y)
    for x in (-2, -1, width_x, width_x + 1):
        wide[:, at(x)] = outer_row(flags[0], near, far, last, 0, x, width_x, width_y)
    rates[...] = wide[...]

    diff_left, diff_right = [v[:SUBLANES] for v in split_sides(flags[1], side_near, side_far, last)]
    mine_low, mine_high = [v[:SUBLANES] for v in split_sides(flags[1], own_near, own_far, last)]
    for index, value in enumerate(
        (diff_left, diff_right, second(diff_left), second(diff_right), mine_low, mine_high)
    ):
        rate_sides[index * SUBLANES : (index + 1) * SUBLANES, :] = value

    def step(double, carry):
        where = pairs_at(double)
        sides = split_sides(flags[1], side_near, side_far, where)
        own = split_sides(flags[1], own_near, own_far, where)
        for which in range(2):
            group = double * 2 + which
            part = slice(which * SUBLANES, (which + 1) * SUBLANES)
            for x in range(width_x):
                e0[:, at(x)] = load_row(field, group, x, width_x, width_y)
            for x in (-2, -1, width_x, width_x + 1):
                e0[:, at(x)] = outer_row(flags[0], near, far, where, which, x, width_x, width_y)
            side_left, side_right = sides[0][part], sides[1][part]

            def next_side(side, mine, coefficient):
                return side + coefficient * (around(side) + second(side) + mine - 4.0 * side)

            next_left = next_side(side_left, own[0][part], diff_left)
            next_right = next_side(side_right, own[1][part], diff_right)
            for x in range(-1, width_x + 1):
                row = e0[:, at(x)]
                close = e0[:, at(x - 1)] + e0[:, at(x + 1)] + beside(row, side_left, side_right, x)
                e1[:, at(x)] = row + wide[:, at(x)] * (close - 4.0 * row)
            for x in range(width_x):
                row = e1[:, at(x)]
                close = e1[:, at(x - 1)] + e1[:, at(x + 1)] + beside(row, next_left, next_right, x)
                value = row + wide[:, at(x)] * (close - 4.0 * row)
                span = slice(x * width_y, (x + 1) * width_y)
                both[groups_at(group), span] = value
                both[
                    pl.ds(pl.multiple_of(levels + group * SUBLANES, SUBLANES), SUBLANES), span
                ] = value - load_row(target, group, x, width_x, width_y)
        return carry

    lax.fori_loop(0, levels // (2 * SUBLANES), step, 0)

    def turn(tile, carry):
        span = pl.ds(pl.multiple_of(tile * LANES, LANES), LANES)
        rows[span, :] = both[:, span].T
        return carry

    lax.fori_loop(0, cells // LANES, turn, 0, unroll=2)


def forward(field_rows, target_rows, diff_rows, near, own, sides, sizes):
    levels, width_x, width_y, _, _ = sizes
    cells = width_x * width_y
    extended = (SUBLANES, (width_x + 4) * width_y)
    return pl.pallas_call(
        with_flags(functools.partial(forward_body, levels, width_x, width_y)),
        out_shape=[
            jax.ShapeDtypeStruct((cells, 2 * levels), F32),
            jax.ShapeDtypeStruct(extended, F32),
            jax.ShapeDtypeStruct((6 * SUBLANES, LANES), F32),
        ],
        in_specs=[VMEM] * 9,
        out_specs=[VMEM] * 3,
        scratch_shapes=[
            pltpu.VMEM(extended, F32),
            pltpu.VMEM(extended, F32),
            pltpu.VMEM(extended, F32),
            pltpu.VMEM((2 * levels, cells), F32),
        ],
        compiler_params=params(8),
        cost_estimate=cost(8),
        name="forward",
    )(field_rows, target_rows, diff_rows, *near, *own, *sides)


def index_body(tiles, subs, lead, rows_each, flags, counts, order, out, starts):
    devices = tiles * subs

    def begin(index, total):
        starts[index] = total
        return total + counts[index]

    lax.fori_loop(0, devices, begin, jnp.int32(0))
    half = subs // 2
    mine = flags[3]
    lane = lax.broadcasted_iota(jnp.int32, (SUBLANES, LANES), 1)
    slot = lax.broadcasted_iota(jnp.int32, (SUBLANES, LANES), 0) * LANES + lane

    def expert(block, carry):
        second_half = block // half
        network_id = mine ^ ((block - second_half * half) * 2 + 1 - second_half)
        value = jnp.zeros((SUBLANES, LANES), jnp.int32)
        base = jnp.int32(0)
        for t in range(tiles):
            device = t * subs + network_id
            count = counts[device]
            offset = starts[device] - base + lead
            shift = lax.rem(offset, LANES)
            window = order[pl.ds(lax.div(offset, LANES), SUBLANES), :]
            turned = pltpu.roll(window, lax.rem(LANES - shift, LANES), 1)
            following = jnp.concatenate([turned[1:], turned[:1]], axis=0)
            moved = jnp.where(lane < LANES - shift, turned, following)
            value = jnp.where((slot >= base) & (slot < base + count), moved, value)
            base = base + count
        out[pl.ds(block * rows_each, rows_each), :] = value[:rows_each]
        return carry

    lax.fori_loop(0, subs, expert, 0)


def slot_cells(counts, column_order, sizes):
    _, width_x, width_y, tiles, subs = sizes
    cells = width_x * width_y
    packet = cells // subs
    rows_each = packet // LANES
    lead = packet
    order = jnp.pad(column_order, (lead, SUBLANES * LANES)).reshape(-1, LANES)
    return pl.pallas_call(
        with_flags(functools.partial(index_body, tiles, subs, lead, rows_each)),
        out_shape=jax.ShapeDtypeStruct((cells // LANES, LANES), jnp.int32),
        in_specs=[SMEM] + [VMEM],
        out_specs=VMEM,
        scratch_shapes=[pltpu.SMEM((tiles * subs,), jnp.int32)],
        compiler_params=params(4),
        cost_estimate=cost(2),
        name="slot_cells",
    )(counts, order).reshape(subs, 1, packet)


def widen(value):
    missing = LANES - value.shape[1]
    return jnp.concatenate([value, jnp.zeros((value.shape[0], missing), value.dtype)], axis=1)


def lower_half(rows):
    return lax.broadcasted_iota(jnp.int32, (rows, LANES), 1) < LANES // 2


def swap_halves(value):
    return pltpu.roll(value, LANES // 2, 1)


def squeeze_rows(value):
    count = value.shape[0] // 2
    return jnp.where(lower_half(count), value[:count], swap_halves(value[count:]))


def pack_rows(put, inner, first, last, biases):
    width = first.shape[1]
    for k in range(3):
        put(inner[k][:, :LANES])
    low = lower_half(width)
    put(jnp.where(low, widen(inner[0][:, LANES:]), swap_halves(widen(inner[1][:, LANES:]))))
    put(jnp.where(low, widen(inner[2][:, LANES:]), last))
    put(first[:, :LANES])
    put(squeeze_rows(widen(first[:, LANES:])))
    tail = []
    for bias, bias_last in biases:
        tail += [piece[:, :LANES] for piece in bias]
        tail += [
            jnp.where(
                lower_half(1), widen(bias[k][:, LANES:]), swap_halves(widen(bias[k + 1][:, LANES:]))
            )
            for k in (0, 2)
        ]
        tail.append(bias_last)
    return tail


def pack_size(levels, width, tiles):
    rows = 5 * width + levels + levels // 2 + 16
    unit = 16 * tiles
    return (rows + unit - 1) // unit * unit


def weights_body(*refs):
    sources, out, targets, semaphores = refs[:5], refs[5], refs[6:11], refs[11]
    wait_all(load_all(sources, targets, semaphores))
    w_first, w_inner, w_last, b_inner, b_last = targets
    row = 0

    def put(value):
        nonlocal row
        out[row : row + value.shape[0], :] = value.astype(BF16)
        row += value.shape[0]

    bias = b_inner[...]
    bias_last = swap_halves(widen(b_last[...]))
    bias_high = bias.astype(BF16).astype(F32)
    last_high = bias_last.astype(BF16).astype(F32)
    bias_low = bias - bias_high
    last_low = bias_last - last_high
    tail = pack_rows(
        put,
        [w_inner[k].astype(F32) for k in range(3)],
        w_first[...].astype(F32),
        swap_halves(widen(w_last[...].astype(F32).T)),
        [
            ([bias_high[k : k + 1] for k in range(4)], last_high),
            ([bias_low[k : k + 1] for k in range(4)], last_low),
        ],
    )
    tail.append(jnp.zeros((out.shape[0] - row - len(tail), LANES), F32))
    put(jnp.concatenate(tail, axis=0))


def pack_weights(w_first, w_inner, w_last, b_inner, b_last, tiles):
    levels, width = w_first.shape
    operands = (w_first, w_inner, w_last.T, b_inner, b_last)
    return pl.pallas_call(
        weights_body,
        out_shape=jax.ShapeDtypeStruct((pack_size(levels, width, tiles), LANES), BF16),
        in_specs=[pl.BlockSpec(memory_space=pltpu.HBM)] * 5,
        out_specs=VMEM,
        scratch_shapes=buffers(operands) + [pltpu.SemaphoreType.DMA((5,))],
        compiler_params=params(62),
        cost_estimate=cost(1),
        name="pack_weights",
    )(*operands)


def network_body(
    levels, width, packet, carried_in,
    behind, ahead, pack_list, rows, back, grads, taken, given_back, packs, first_in, first_out, inner, last, last_half,
    kept, feeds, slopes, residues,
):
    block = pl.program_id(0)
    blocks = pl.num_programs(0)
    narrow = width - LANES
    wide = 2 * LANES
    half = packet // 2

    def fetch(cells_of, first_slot, count):
        for u in range(first_slot, first_slot + count):
            taken[u : u + 1, :] = rows[pl.ds(cells_of[0, 0, u], 1), :]

    def deliver(cells_of, first_slot, count):
        for u in range(first_slot, first_slot + count):
            back[pl.ds(cells_of[0, 0, u], 1), :] = given_back[u : u + 1, :]

    @pl.when(block == 0)
    def _():
        if carried_in is None:
            fetch(behind, 0, packet)
        else:
            taken[...] = carried_in[0][...]
            given_back[...] = carried_in[1][...]
        first_in[levels:, :] = jnp.zeros((wide - levels, wide), BF16)
        first_out[...] = jnp.zeros((LANES, wide), BF16)
        first_in[:levels, LANES:] = jnp.zeros((levels, LANES), BF16)
        inner[:, :, LANES:] = jnp.zeros((3, wide, LANES), BF16)
        inner[:, width:, :] = jnp.zeros((3, wide - width, wide), BF16)
        last[...] = jnp.zeros((wide, LANES), BF16)
        last_half[...] = jnp.zeros((wide, LANES), BF16)

    for index, source in enumerate(pack_list):

        @pl.when(block == index)
        def _():
            packs[...] = source[...]

    row = 0

    def take(size):
        nonlocal row
        value = packs[row : row + size, :].astype(F32)
        row += size
        return value

    def halves(value):
        return value[:, :narrow], swap_halves(value)[:, :narrow]

    for k in range(3):
        inner[k, :width, :LANES] = (0.5 * take(width)).astype(BF16)
    narrow_a, narrow_b = halves(0.5 * take(width))
    inner[0, :width, LANES:width] = narrow_a.astype(BF16)
    inner[1, :width, LANES:width] = narrow_b.astype(BF16)
    mixed = take(width)
    inner[2, :width, LANES:width] = (0.5 * mixed[:, :narrow]).astype(BF16)
    out_weight = jnp.where(lower_half(width), 0.0, mixed)
    last[:width, :] = out_weight.astype(BF16)
    last_half[:width, :] = (0.5 * out_weight).astype(BF16)
    wide_first = take(levels)
    narrow_a, narrow_b = halves(take(levels // 2))
    half_levels = levels // 2
    first_in[:levels, :LANES] = (0.5 * wide_first).astype(BF16)
    first_in[:half_levels, LANES:width] = (0.5 * narrow_a).astype(BF16)
    first_in[half_levels:levels, LANES:width] = (0.5 * narrow_b).astype(BF16)
    first_out[levels:, :LANES] = wide_first.astype(BF16)
    first_out[levels : levels + half_levels, LANES:width] = narrow_a.astype(BF16)
    first_out[levels + half_levels :, LANES:width] = narrow_b.astype(BF16)
    tail = take(16)

    spare_lane = lax.broadcasted_iota(jnp.int32, (1, LANES), 1) - narrow
    spare = (spare_lane == 0) | (spare_lane == 1)

    def bias_rows(k):
        parts = []
        for base in (0, 7):
            mixed = 0.5 * tail[base + 4 + k // 2 : base + 5 + k // 2]
            side = mixed if k % 2 == 0 else swap_halves(mixed)
            side = jnp.where(lower_half(1), side, 0.0)
            side = jnp.where(spare, UNIT_INPUT[0] if base == 0 else UNIT_INPUT[1], side)
            parts.append(jnp.concatenate([0.5 * tail[base + k : base + k + 1], side], axis=1))
        parts.append(jnp.zeros((14, wide), F32))
        return jnp.concatenate(parts, axis=0).astype(BF16)

    first_in[LANES : LANES + 16, :] = bias_rows(0)
    for k in range(3):
        inner[k, width : width + 16, :] = bias_rows(k + 1)
    last[width : width + 16, :] = jnp.concatenate(
        [tail[6:7], tail[13:14], jnp.zeros((14, LANES), F32)], axis=0
    ).astype(BF16)

    over_rows = (((0,), (0,)), ((), ()))
    over_lanes = (((1,), (1,)), ((), ()))
    sides = (0, 1)
    lower = lower_half(half)
    ones = jnp.ones((half, LANES), BF16)

    def span(side):
        return slice(side * half, (side + 1) * half)

    for side in sides:
        kept[span(side), :] = taken[span(side), :].astype(BF16)

    def layers(chosen, current, delivered, share):
        for k in chosen:
            for side in sides:
                weight = first_in[...] if k == 0 else inner[k - 1]
                u = jnp.dot(current[side], weight, preferred_element_type=F32)
                turn = jnp.tanh(u)
                plus = 1.0 + turn
                active = u * plus
                slopes[k, span(side), :] = plus
                current[side] = active.astype(BF16)
                feeds[k, span(side), :] = current[side]
                deliver(behind, delivered, share)
                delivered += share
        return current

    layers(
        (0, 1), [jnp.concatenate([kept[span(side), :], ones], axis=1) for side in sides], 0, packet // 8
    )

    def second_part():
        current = layers((2, 3), [feeds[1, span(side), :] for side in sides], packet // 2, packet // 8)
        for side in sides:
            output = jnp.dot(current[side], last[...], preferred_element_type=F32)
            residues[span(side), :] = jnp.where(
                lower, 0.0, kept[span(side), :].astype(F32) + output
            )

    second_part()

    def third_part():
        fetched = 0
        share = packet // 10
        errors = [residues[span(side), :].astype(BF16) for side in sides]

        def weight_grad(k):
            products = []
            for side in sides:
                if k == 0:
                    feed = jnp.concatenate([kept[span(side), :], ones], axis=1)[:, : LANES + 16]
                else:
                    feed = feeds[k - 1, span(side), : width + 16]
                products.append(
                    lax.dot_general(feed, errors[side], over_rows, preferred_element_type=F32)
                )
            return products[0] + products[1]

        grad_sums = [None] * 5
        carried = [
            lax.dot_general(errors[side], last_half[...], over_lanes, preferred_element_type=F32)
            for side in sides
        ]
        grad_sums[4] = weight_grad(4)
        for k in (3, 2, 1, 0):
            for side in sides:
                plus = slopes[k, span(side), :]
                slope = plus + feeds[k, span(side), :].astype(F32) * (2.0 - plus)
                errors[side] = (carried[side] * slope).astype(BF16)
                weight = inner[k - 1] if k > 0 else first_out[...]
                carried[side] = lax.dot_general(
                    errors[side], weight, over_lanes, preferred_element_type=F32
                )
                fetch(ahead, fetched, share)
                fetched += share
            grad_sums[k] = weight_grad(k)
        fetch(ahead, fetched, packet - fetched)
        for side in sides:
            given_back[span(side), :] = residues[span(side), :] + carried[side]

        filled = 0

        def put(value):
            nonlocal filled
            grads[0, filled : filled + value.shape[0], :] = value.astype(BF16)
            filled += value.shape[0]

        tail = pack_rows(
            put,
            [grad_sums[k][:width, :width] for k in (1, 2, 3)],
            grad_sums[0][:levels, :width],
            grad_sums[4][:width],
            [
                (
                    [grad_sums[0][LANES : LANES + 1, :width]]
                    + [grad_sums[k][width : width + 1, :width] for k in (1, 2, 3)],
                    grad_sums[4][width : width + 1],
                )
            ],
        )
        tail.append(jnp.zeros((grads.shape[1] - filled - len(tail), LANES), F32))
        put(jnp.concatenate(tail, axis=0))

    third_part()
    if carried_in is not None:

        @pl.when(block == blocks - 1)
        def _():
            deliver(ahead, 0, packet)


def network(cells_of, pack_list, rows, before, shift, levels, width, subs):
    cells, doubled = rows.shape
    packet = cells // subs
    blocks = len(pack_list)
    pack_shape = pack_list[0].shape
    final = before is not None
    limit = blocks - 1 if final else blocks
    wide = 2 * LANES

    def body(behind, ahead, *refs):
        names, rest = refs[:blocks], refs[blocks + 1 :]
        carried_in = None
        if final:
            carried_in, rest = rest[1:3], rest[3:]
        network_body(
            levels, width, packet, carried_in, behind, ahead, names, refs[blocks], *rest
        )

    operands = [cells_of, cells_of, *pack_list, rows]
    in_specs = [
        pl.BlockSpec(
            (1, 1, packet),
            lambda i: (jnp.maximum(i - 1 + shift, 0), 0, 0),
            memory_space=pltpu.SMEM,
        ),
        pl.BlockSpec(
            (1, 1, packet),
            lambda i: (jnp.minimum(i + 1, limit) + shift, 0, 0),
            memory_space=pltpu.SMEM,
        ),
    ] + [VMEM] * (blocks + 1)
    aliases = {}
    held = [jax.ShapeDtypeStruct((packet, doubled), F32)] * 2
    scratch = []
    if final:
        aliases = {len(operands): 0}
        operands += list(before)
        in_specs += [VMEM] * 3
        scratch = [pltpu.VMEM((packet, doubled), F32)] * 2
        held = []
    return pl.pallas_call(
        body,
        grid=(blocks,),
        out_shape=[
            jax.ShapeDtypeStruct((cells, doubled), F32),
            jax.ShapeDtypeStruct((blocks, *pack_shape), BF16),
        ]
        + held,
        in_specs=in_specs,
        out_specs=[VMEM, pl.BlockSpec((1, *pack_shape), lambda i: (i, 0, 0))] + [VMEM] * len(held),
        scratch_shapes=scratch
        + [
            pltpu.VMEM(pack_shape, BF16),
            pltpu.VMEM((wide, wide), BF16),
            pltpu.VMEM((LANES, wide), BF16),
            pltpu.VMEM((3, wide, wide), BF16),
            pltpu.VMEM((wide, LANES), BF16),
            pltpu.VMEM((wide, LANES), BF16),
            pltpu.VMEM((packet, LANES), BF16),
            pltpu.VMEM((4, packet, wide), BF16),
            pltpu.VMEM((4, packet, wide), F32),
            pltpu.VMEM((packet, LANES), F32),
        ],
        input_output_aliases=aliases,
        compiler_params=params(24),
        cost_estimate=cost(12),
        name="network",
    )(*operands)


def add_body(first, other, *outs):
    for index, out in enumerate(outs):
        out[...] = (first[index].astype(F32) + other[index].astype(F32)).astype(BF16)


def add_pair(first, other):
    return pl.pallas_call(
        add_body,
        out_shape=[jax.ShapeDtypeStruct(first.shape[1:], BF16)] * first.shape[0],
        in_specs=[VMEM] * 2,
        out_specs=[VMEM] * first.shape[0],
        compiler_params=params(8),
        cost_estimate=cost(1),
        name="add_pair",
    )(first, other)


def total_of(parts):
    total = parts[0][...].astype(F32)
    for part in parts[1:]:
        total = total + part[...].astype(F32)
    return total.astype(BF16)


def share_body(count, flags, *refs):
    parts, outs, whole = refs[:count], refs[count:-1], refs[-1]
    whole[...] = total_of(parts).astype(F32)
    rows = outs[0].shape[0]
    for offset, out in enumerate(outs):
        start = pl.multiple_of((flags[2] ^ offset) * rows, 16)
        out[...] = whole[pl.ds(start, rows), :].astype(BF16)


def sum_and_share(parts, tiles):
    rows = parts[0].shape[0]
    return pl.pallas_call(
        with_flags(functools.partial(share_body, len(parts))),
        out_shape=[jax.ShapeDtypeStruct((rows // tiles, LANES), BF16)] * tiles,
        in_specs=[VMEM] * len(parts),
        out_specs=[VMEM] * tiles,
        scratch_shapes=[pltpu.VMEM((rows, LANES), F32)],
        compiler_params=params(8),
        cost_estimate=cost(1),
        name="sum_and_share",
    )(*parts)


def sum_body(*refs):
    refs[-1][...] = total_of(refs[:-1])


def sum_parts(parts):
    return pl.pallas_call(
        sum_body,
        out_shape=jax.ShapeDtypeStruct(parts[0].shape, BF16),
        in_specs=[VMEM] * len(parts),
        out_specs=VMEM,
        compiler_params=params(8),
        cost_estimate=cost(1),
        name="sum_parts",
    )(*parts)


def steps_body(levels, width, count, tiles, flags, *refs):
    parts, (first, inner, last, bias, bias_last, whole) = refs[:tiles], refs[tiles:]
    share = parts[0].shape[0]
    for offset, part in enumerate(parts):
        whole[pl.ds(pl.multiple_of((flags[2] ^ offset) * share, 16), share), :] = part[...]

    def squares(index, total):
        part = whole[pl.ds(pl.multiple_of(index * 16, 16), 16), :].astype(F32)
        return total + part * part

    total = lax.fori_loop(0, whole.shape[0] // 16, squares, jnp.zeros((16, LANES), F32), unroll=4)
    factor = 1.0 / jnp.sqrt(jnp.broadcast_to(jnp.sum(total), (1, LANES)) / count + 1e-06)
    row = 0

    def take(size):
        nonlocal row
        value = whole[row : row + size, :].astype(F32) * factor
        row += size
        return value

    half = LANES // 2
    for k in range(3):
        inner[k, :, :LANES] = take(width)
    narrow = take(width)
    inner[0, :, LANES:] = narrow[:, :half]
    inner[1, :, LANES:] = swap_halves(narrow)[:, :half]
    narrow = take(width)
    inner[2, :, LANES:] = narrow[:, :half]
    last[...] = swap_halves(narrow).T[:half]
    first[:, :LANES] = take(levels)
    narrow = take(levels // 2)
    first[: levels // 2, LANES:] = narrow[:, :half]
    first[levels // 2 :, LANES:] = swap_halves(narrow)[:, :half]
    tail = take(16)
    bias[:, :LANES] = tail[0:4]
    for k in (0, 2):
        pair = tail[4 + k // 2 : 5 + k // 2]
        bias[k : k + 1, LANES:] = pair[:, :half]
        bias[k + 1 : k + 2, LANES:] = swap_halves(pair)[:, :half]
    bias_last[...] = swap_halves(tail[6:7])[:, :half]


def make_steps(parts, levels, width):
    count = 2 * levels * width + 3 * width * width + 4 * width + levels
    return pl.pallas_call(
        with_flags(functools.partial(steps_body, levels, width, float(count), len(parts))),
        out_shape=[
            jax.ShapeDtypeStruct((levels, width), F32),
            jax.ShapeDtypeStruct((3, width, width), F32),
            jax.ShapeDtypeStruct((levels, width), F32),
            jax.ShapeDtypeStruct((4, width), F32),
            jax.ShapeDtypeStruct((1, levels), F32),
        ],
        in_specs=[VMEM] * len(parts),
        out_specs=[VMEM] * 5,
        scratch_shapes=[pltpu.VMEM((len(parts) * parts[0].shape[0], LANES), BF16)],
        compiler_params=params(8),
        cost_estimate=cost(2),
        name="make_steps",
    )(*parts)


def collect_body(levels, width_x, width_y, flags, rows, grid, first, other):
    cells = width_x * width_y

    def turn(tile, carry):
        span = pl.ds(pl.multiple_of(tile * LANES, LANES), LANES)
        grid[:, span] = rows[span, :].T[levels:].astype(BF16).astype(F32)
        return carry

    lax.fori_loop(0, cells // LANES, turn, 0, unroll=2)

    def step(double, carry):
        store_rows(
            pairs_at(double),
            lambda which, x: grid[groups_at(double * 2 + which), x * width_y : (x + 1) * width_y],
            width_x, width_y, flags[0], first, other,
        )
        return carry

    lax.fori_loop(0, levels // (2 * SUBLANES), step, 0)


def collect(rows, sizes):
    levels, width_x, width_y, _, _ = sizes
    cells = width_x * width_y
    shape = jax.ShapeDtypeStruct((levels, 2 * width_y), BF16)
    return pl.pallas_call(
        with_flags(functools.partial(collect_body, levels, width_x, width_y)),
        out_shape=[jax.ShapeDtypeStruct((levels, cells), F32), shape, shape],
        in_specs=[VMEM],
        out_specs=[VMEM] * 3,
        compiler_params=params(8),
        cost_estimate=cost(3),
        name="collect",
    )(rows)


def adjoint_body(
    levels, width_x, width_y,
    flags, grid, wide, rate_sides, near, far, own_near, own_far, side_near, side_far, out, flow, e1,
):
    y_tiles = width_y // LANES
    stride = width_x * y_tiles

    def at(x):
        return slice((x + 2) * width_y, (x + 3) * width_y)

    rate_left, rate_right, outer_left, outer_right, mine_left, mine_right = [
        rate_sides[index * SUBLANES : (index + 1) * SUBLANES, :] for index in range(6)
    ]

    def step(double, carry):
        where = pairs_at(double)
        sides = split_sides(flags[1], side_near, side_far, where)
        owns = split_sides(flags[1], own_near, own_far, where)
        for which in range(2):
            group = double * 2 + which
            own = groups_at(group)
            part = slice(which * SUBLANES, (which + 1) * SUBLANES)

            def next_side(side, rate, outer_rate, mine, mine_rate):
                product = side * rate
                return product, side + (
                    around(product) + second(side) * outer_rate + mine * mine_rate - 4.0 * product
                )

            flow_left, next_left = next_side(
                sides[0][part], rate_left, outer_left, owns[0][part], mine_left
            )
            flow_right, next_right = next_side(
                sides[1][part], rate_right, outer_right, owns[1][part], mine_right
            )

            def value(x):
                if 0 <= x < width_x:
                    return grid[own, x * width_y : (x + 1) * width_y]
                return outer_row(flags[0], near, far, where, which, x, width_x, width_y)

            for x in range(-2, width_x + 2):
                flow[:, at(x)] = value(x) * wide[:, at(x)]
            for x in range(-1, width_x + 1):
                row = flow[:, at(x)]
                close = flow[:, at(x - 1)] + flow[:, at(x + 1)]
                close = close + beside(row, flow_left, flow_right, x)
                e1[:, at(x)] = value(x) + close - 4.0 * row
            for x in range(-1, width_x + 1):
                flow[:, at(x)] = e1[:, at(x)] * wide[:, at(x)]
            flow_left = next_left * rate_left
            flow_right = next_right * rate_right
            for x in range(width_x):
                row = flow[:, at(x)]
                close = flow[:, at(x - 1)] + flow[:, at(x + 1)]
                close = close + beside(row, flow_left, flow_right, x)
                result = e1[:, at(x)] + close - 4.0 * row
                for y_tile in range(y_tiles):
                    offset = group * (SUBLANES * stride) + row_offset(x, y_tile, y_tiles)
                    out[pl.ds(offset, SUBLANES, stride=stride), :] = result[
                        :, y_tile * LANES : (y_tile + 1) * LANES
                    ]
        return carry

    lax.fori_loop(0, levels // (2 * SUBLANES), step, 0)


def adjoint(grid, rates, rate_sides, near, own, sides, sizes):
    levels, width_x, width_y, _, _ = sizes
    extended = (SUBLANES, (width_x + 4) * width_y)
    return pl.pallas_call(
        with_flags(functools.partial(adjoint_body, levels, width_x, width_y)),
        out_shape=jax.ShapeDtypeStruct((levels * width_x * width_y // LANES, LANES), F32),
        in_specs=[VMEM] * 9,
        out_specs=VMEM,
        scratch_shapes=[pltpu.VMEM(extended, F32), pltpu.VMEM(extended, F32)],
        compiler_params=params(8),
        cost_estimate=cost(6),
        name="adjoint",
    )(grid, rates, rate_sides, *near, *own, *sides)


def local_program(
    initial, targets, diffusivity, column_order, send_counts,
    w_first, w_inner, w_last, b_inner, b_last,
):
    levels, width_x, width_y = initial.shape
    tiles, subs = lax.axis_size("tile"), lax.axis_size("sub")
    sizes = (levels, width_x, width_y, tiles, subs)
    field_rows = tile_rows(initial)
    target_rows = tile_rows(targets)
    diff_rows = tile_rows(diffusivity[None])
    width = w_first.shape[2]
    half = subs // 2
    area = (levels, width_x, width_y)

    first, other = pack_rows_out(field_rows, diff_rows, *area)
    weights = pack_weights(w_first[0], w_inner[0], w_last[0], b_inner[0], b_last, tiles)
    own_weights = [weights] + [
        lax.ppermute(weights, "sub", partners(subs, 2 * c)) for c in range(1, half)
    ]
    near = trade_sides(first, other, "tile")
    cells_of = slot_cells(send_counts[0], column_order[0], sizes)
    own = pack_columns_out(field_rows, diff_rows, *area)
    own = add_corners(*near, *own, width_x, width_y)
    sides = trade_sides(*own, "sub")
    other_weights = [lax.ppermute(pack, "sub", partners(subs, 1)) for pack in own_weights]
    rows, rates, rate_sides = forward(field_rows, target_rows, diff_rows, near, own, sides, sizes)
    back, other_grads, taken, given_back = network(
        cells_of, other_weights, rows, None, 0, levels, width, subs
    )
    partner_grads = lax.ppermute(other_grads, "sub", partners(subs, 1))
    back, own_grads = network(
        cells_of, own_weights, rows, (back, taken, given_back), half,
        levels, width, subs,
    )
    both_grads = add_pair(own_grads, partner_grads)
    arrived = [both_grads[0]] + [
        lax.ppermute(both_grads[c], "sub", partners(subs, 2 * c)) for c in range(1, half)
    ]
    grid, g_first, g_other = collect(back, sizes)
    g_near = trade_sides(g_first, g_other, "tile")
    g_own = pack_columns_back(grid, *area)
    g_own = add_corners(*g_near, *g_own, width_x, width_y)
    g_sides = trade_sides(*g_own, "sub")
    shares = sum_and_share(arrived, tiles)
    mine = [shares[0]] + [
        lax.ppermute(shares[d], "tile", partners(tiles, d)) for d in range(1, tiles)
    ]
    result = adjoint(grid, rates, rate_sides, g_near, g_own, g_sides, sizes)
    piece = sum_parts(mine)
    pieces = [piece] + [lax.ppermute(piece, "tile", partners(tiles, d)) for d in range(1, tiles)]
    steps = make_steps(pieces, levels, width)
    return (
        untile_rows(result, levels, width_x, width_y),
        steps[0][None], steps[1][None], steps[2].T[None], steps[3][None], steps[4],
    )


def solution(mesh):
    placed = (
        P(None, "tile", "sub"),
        P(None, "tile", "sub"),
        P("tile", "sub"),
        P(("tile", "sub"), None),
        P(("tile", "sub"), None),
        P("sub", None, None),
        P("sub", None, None, None),
        P("sub", None, None),
        P("sub", None, None),
        P("sub", None),
    )
    return jax.shard_map(
        local_program,
        mesh=mesh,
        in_specs=placed,
        out_specs=(
            P(None, "tile", "sub"),
            P("sub", None, None),
            P("sub", None, None, None),
            P("sub", None, None),
            P("sub", None, None),
            P("sub", None),
        ),
        check_vma=False,
    )
```
